32 devices in a mesh: groups: 2 (over y), frame: 8 (over z, x), row: 2 (over core).
Axes of the slice: x: 2, y: 2, z: 4, core: 2. Of those that a mesh axis runs over, the one named last changes fastest.
Arguments:
- frames_in: bfloat16 [16, 4, 48, 640], P(('groups', 'frame'), 'row'), parts along dimension 0, may hold values from -6 to 6
- norm_gains: float32 [3, 640], replicated, may hold values from 0.25 to 1.75
- conv_weight: bfloat16 [5760, 640], P('frame'), may hold values from -0.078125 to 0.078125
- time_weight: bfloat16 [1920, 640], P('frame'), may hold values from -0.125 to 0.125
- attention_weight: bfloat16 [640, 2560], P('frame'), may hold values from -0.3125 to 0.3125
- reference_keys: bfloat16 [4, 16, 640], P('groups', ('frame', 'row')), parts along dimension 0, may hold values from -600 to 600
- reference_values: bfloat16 [4, 16, 640], P('groups', ('frame', 'row')), parts along dimension 0, may hold values from -12 to 12
- reference_pick: int32 [16], P(('groups', 'frame')), parts along dimension 0, may hold values from 0 to 1
Outputs:
- frames_out: bfloat16 [16, 4, 48, 640], P(('groups', 'frame'), 'row'), parts along dimension 0
The draws below stay inside these ranges and needn't reach their ends.
There are 2 independent parts, one for each index of `groups`. The reference program is written for one: setup_inputs(seed, part) draws one part's arguments, and reference() takes and returns one part's arrays. A program takes and returns all parts, laid end to end along the dimension named above; an argument that names none is the same for every part. Nothing has to cross between parts.
All inputs are finite; a program needn't handle non-finite values.
Results may differ from the reference program's by a relative error of at most 0.035.
Values may be sent and summed in bfloat16 or wider, within the bound.
A program may use at most 64 MiB of HBM per device.

```python
import jax
import jax.numpy as jnp
from jax import lax

CH = 640
HEADS = 10
HEAD_DIM = 64
W = 48
REFS = 2
FRAMES = 8
H = 4
REF_TOK = 16


def draw_reference_keys(key, part):
    base = jnp.clip(2.0 * jax.random.normal(key, (REFS, REF_TOK, CH), jnp.float32), -12.0, 12.0)
    return base.astype(jnp.bfloat16)


def touch_ends(drawn, key, low, top_value):
    place = [jax.random.randint(jax.random.fold_in(key, axis), (), 0, length) for axis, length in enumerate(drawn.shape)]
    longest = drawn.shape.index(max(drawn.shape))
    beside = place[:longest] + [(place[longest] + 1) % drawn.shape[longest]] + place[longest + 1:]
    return drawn.at[tuple(place)].set(low).at[tuple(beside)].set(top_value)


def block_scale(own_key, extent, pieces, smallest, high):
    def one(dim, blocks):
        draws = jax.random.uniform(jax.random.fold_in(jax.random.fold_in(own_key, 6), dim), (blocks,), jnp.float32, smallest / len(pieces), high / len(pieces))
        return jnp.repeat(jnp.exp(draws), extent[dim] // blocks).reshape((-1,) + (1,) * (len(extent) - dim - 1))

    factor_of = one(*pieces[0])
    for cut in pieces[1:]:
        factor_of = factor_of * one(*cut)
    return factor_of


def normal_values(key, shape, scale, limit, pieces=(), kind=jnp.bfloat16):
    loudness = block_scale(key, shape, pieces, -0.22, 0.18) if pieces else 1.0
    array = jax.random.normal(key, shape, jnp.float32) * scale * loudness
    return jnp.minimum(jnp.maximum(array, -limit), limit).astype(kind)


def setup_inputs(seed: int = 0, part: int = 0) -> dict:
    key_of = jax.random.split(jax.random.key(seed), 9)
    part_splits = jax.random.split(jax.random.fold_in(key_of[8], part), 9)
    frames_in = normal_values(part_splits[0], (FRAMES, H, W, CH), 1.0, 6.0, ((0, 8), (1, 2)))
    norm_gains = jnp.clip(1.0 + 0.15 * jax.random.normal(key_of[1], (3, CH), jnp.float32), 0.25, 1.75)
    conv_weight = normal_values(key_of[2], (9 * CH, CH), (9 * CH) ** -0.5, 0.078125, ((0, 8),))
    time_weight = normal_values(key_of[3], (3 * CH, CH), (3 * CH) ** -0.5, 0.125, ((0, 8),))
    attention_weight = normal_values(key_of[4], (CH, 4 * CH), (CH // 2) ** -0.5, 0.3125, ((0, 8),))
    reference_keys = draw_reference_keys(jax.random.fold_in(jax.random.fold_in(key_of[8], part), 71), part)
    reference_values = normal_values(part_splits[6], (REFS, REF_TOK, CH), 2.0, 12.0, ((1, 16),))
    reference_pick = touch_ends(jax.random.randint(part_splits[7], (FRAMES,), 0, REFS), jax.random.fold_in(part_splits[7], 1), 0, REFS - 1).astype(jnp.int32)
    return {"frames_in": frames_in, "norm_gains": norm_gains, "conv_weight": conv_weight, "time_weight": time_weight, "attention_weight": attention_weight, "reference_keys": reference_keys, "reference_values": reference_values, "reference_pick": reference_pick}


def normalize(values, gain):
    scale = lax.rsqrt(lax.optimization_barrier(jnp.mean(values * values, axis=-1, keepdims=True)) + 1e-05)
    return values * scale * gain

def attend_frame(operands):
    queries, own_keys, own_values, picked_keys, picked_values = operands
    keys_all = jnp.concatenate([own_keys, picked_keys], axis=0)
    values_all = jnp.concatenate([own_values, picked_values], axis=0)
    query_heads = queries.reshape(queries.shape[0], HEADS, HEAD_DIM).astype(jnp.float32)
    key_heads = keys_all.reshape(keys_all.shape[0], HEADS, HEAD_DIM).astype(jnp.float32)
    value_heads = values_all.reshape(values_all.shape[0], HEADS, HEAD_DIM).astype(jnp.float32)
    scores = jnp.einsum('qhd,khd->hqk', query_heads, key_heads) * HEAD_DIM ** (-0.5)
    ceiling = lax.optimization_barrier(jnp.max(scores, axis=-1, keepdims=True))
    weights = jnp.exp(scores - ceiling)
    probs = (weights / lax.optimization_barrier(jnp.sum(weights, axis=-1, keepdims=True))).astype(jnp.bfloat16)
    attended = jnp.einsum('hqk,khd->qhd', probs.astype(jnp.float32), value_heads)
    return attended.astype(jnp.bfloat16).reshape(queries.shape[0], CH)

def reference(frames_in, norm_gains, conv_weight, time_weight, attention_weight, reference_keys, reference_values, reference_pick):
    inputs = frames_in.astype(jnp.float32)
    tokens = FRAMES * H * W
    activated = jax.nn.silu(normalize(inputs, norm_gains[0])).astype(jnp.bfloat16)
    padded = jnp.pad(activated, ((0, 0), (1, 1), (1, 1), (0, 0)))
    spatial = jnp.zeros((tokens, CH), jnp.float32)
    for offset_row in range(3):
        for offset_col in range(3):
            window = padded[:, offset_row:offset_row + H, offset_col:offset_col + W, :].reshape(tokens, CH)
            row_start = (3 * offset_row + offset_col) * CH
            spatial = spatial + jnp.dot(window, conv_weight[row_start:row_start + CH], preferred_element_type=jnp.float32)
    hidden = (inputs + spatial.reshape(inputs.shape)).astype(jnp.bfloat16)
    hidden_wide = hidden.astype(jnp.float32)
    mixed = jax.nn.silu(normalize(hidden_wide, norm_gains[1])).astype(jnp.bfloat16)
    nearby = jnp.pad(mixed, ((1, 1), (0, 0), (0, 0), (0, 0)))
    temporal = jnp.zeros((tokens, CH), jnp.float32)
    for offset_frame in range(3):
        window = nearby[offset_frame:offset_frame + FRAMES].reshape(tokens, CH)
        temporal = temporal + jnp.dot(window, time_weight[offset_frame * CH:(offset_frame + 1) * CH], preferred_element_type=jnp.float32)
    blended = (hidden_wide + temporal.reshape(inputs.shape)).astype(jnp.bfloat16)
    blended_wide = blended.astype(jnp.float32)
    normed = normalize(blended_wide, norm_gains[2]).astype(jnp.bfloat16).reshape(tokens, CH)
    projected = jnp.dot(normed, attention_weight[:, :3 * CH], preferred_element_type=jnp.float32).astype(jnp.bfloat16)
    projected = projected.reshape(FRAMES, H * W, 3 * CH)
    queries = projected[:, :, :CH]
    own_keys = projected[:, :, CH:2 * CH]
    own_values = projected[:, :, 2 * CH:]
    picked_keys = reference_keys[reference_pick]
    picked_values = reference_values[reference_pick]
    attended = lax.map(attend_frame, (queries, own_keys, own_values, picked_keys, picked_values))
    output = jnp.dot(attended.reshape(tokens, CH), attention_weight[:, 3 * CH:], preferred_element_type=jnp.float32)
    return (blended_wide + output.reshape(inputs.shape)).astype(jnp.bfloat16)
```

```python
import functools

import jax
import jax.numpy as jnp
from jax import lax
from jax.experimental import pallas as pl
from jax.experimental.pallas import tpu as pltpu
from jax.sharding import PartitionSpec as P

HEADS = 10
LANES = 2
QUAD = 4
MESH = pl.DeviceIdType.MESH


def padded_2(x, sides, width):
    for axis, dim in sides:
        devices, length = (lax.axis_size(axis), x.shape[dim])
        up = [(i, (i + 1) % devices) for i in range(devices - 1)]
        down = [(j, i) for i, j in up]
        last = lax.slice_in_dim(x, length - width, length, axis=dim)
        initial = lax.slice_in_dim(x, 0, width, axis=dim)
        before = lax.ppermute(last, axis, up)
        after = lax.ppermute(initial, axis, down)
        x = jnp.concatenate([before, x, after], axis=dim)
    return x


def normalize(values, gain):
    scale = lax.rsqrt(jnp.mean(values * values, axis=-1, keepdims=True) + 1e-05)
    return values * scale * gain


def heads_first(block, head_dim):
    split = block.reshape(block.shape[0], block.shape[1], HEADS, head_dim)
    return jnp.transpose(split, (2, 0, 1, 3))


def by_collectives(
    frames_in,
    norm_gains,
    conv_weight,
    time_weight,
    attention_weight,
    reference_keys,
    reference_values,
    reference_pick,
):
    local_frames, local_rows, columns, channels = frames_in.shape
    head_dim = channels // HEADS
    tokens = local_frames * local_rows * columns
    row_count = lax.axis_size("row")
    row_place = lax.axis_index("row")

    def halve(matrix):
        share = matrix.shape[1] // row_count
        return lax.dynamic_slice_in_dim(matrix, row_place * share, share, 1)

    conv_half, time_half, attention_half = (
        lax.all_gather(halve(conv_weight), "frame", axis=0, tiled=True),
        lax.all_gather(halve(time_weight), "frame", axis=0, tiled=True),
        lax.all_gather(halve(attention_weight), "frame", axis=0, tiled=True),
    )
    conv_full, time_full, attention_full = (
        lax.all_gather(conv_half, "row", axis=1, tiled=True),
        lax.all_gather(time_half, "row", axis=1, tiled=True),
        lax.all_gather(attention_half, "row", axis=1, tiled=True),
    )
    inputs = frames_in.astype(jnp.float32)
    activated = jax.nn.silu(normalize(inputs, norm_gains[0])).astype(jnp.bfloat16)
    padded = padded_2(activated, (("row", 1),), 1)
    padded = jnp.pad(padded, ((0, 0), (0, 0), (1, 1), (0, 0)))
    spatial = jnp.zeros((tokens, channels), jnp.float32)
    for offset_row in range(3):
        for offset_col in range(3):
            window = padded[
                :, offset_row : offset_row + local_rows, offset_col : offset_col + columns, :
            ].reshape(tokens, channels)
            row_start = (3 * offset_row + offset_col) * channels
            spatial = spatial + jnp.dot(
                window,
                conv_full[row_start : row_start + channels],
                preferred_element_type=jnp.float32,
            )
    hidden = (inputs + spatial.reshape(inputs.shape)).astype(jnp.bfloat16)
    hidden_wide = hidden.astype(jnp.float32)
    mixed = jax.nn.silu(normalize(hidden_wide, norm_gains[1])).astype(jnp.bfloat16)
    nearby = padded_2(mixed, (("frame", 0),), 1)
    temporal = jnp.zeros((tokens, channels), jnp.float32)
    for offset_frame in range(3):
        window = nearby[offset_frame : offset_frame + local_frames].reshape(tokens, channels)
        temporal = temporal + jnp.dot(
            window,
            time_full[offset_frame * channels : (offset_frame + 1) * channels],
            preferred_element_type=jnp.float32,
        )
    blended = (hidden_wide + temporal.reshape(inputs.shape)).astype(jnp.bfloat16)
    blended_wide = blended.astype(jnp.float32)
    normed = normalize(blended_wide, norm_gains[2]).astype(jnp.bfloat16).reshape(tokens, channels)
    projected = jnp.dot(
        normed, attention_full[:, : 3 * channels], preferred_element_type=jnp.float32
    ).astype(jnp.bfloat16)
    projected = projected.reshape(local_frames, local_rows * columns, 3 * channels)
    queries = projected[:, :, :channels]
    own_keys = projected[:, :, channels : 2 * channels]
    own_values = projected[:, :, 2 * channels :]
    frame_keys, frame_values = (
        lax.all_gather(own_keys, "row", axis=1, tiled=True),
        lax.all_gather(own_values, "row", axis=1, tiled=True),
    )
    cache_keys, cache_values = (
        lax.all_gather(reference_keys, ("frame", "row"), axis=1, tiled=True),
        lax.all_gather(reference_values, ("frame", "row"), axis=1, tiled=True),
    )
    picked_keys = jnp.take(cache_keys, reference_pick, axis=0)
    picked_values = jnp.take(cache_values, reference_pick, axis=0)
    keys_all = jnp.concatenate([frame_keys, picked_keys], axis=1)
    values_all = jnp.concatenate([frame_values, picked_values], axis=1)

    def one_head(operands):
        query_head, key_head, value_head = operands
        scores = jnp.einsum(
            "fqd,fkd->fqk", query_head, key_head, preferred_element_type=jnp.float32
        ) * head_dim ** (-0.5)
        ceiling = jnp.max(scores, axis=-1, keepdims=True)
        weights = jnp.exp(scores - ceiling)
        probs = (weights / jnp.sum(weights, axis=-1, keepdims=True)).astype(jnp.bfloat16)
        return jnp.einsum(
            "fqk,fkd->fqd", probs, value_head, preferred_element_type=jnp.float32
        ).astype(jnp.bfloat16)

    per_head = lax.map(
        one_head,
        (
            heads_first(queries, head_dim),
            heads_first(keys_all, head_dim),
            heads_first(values_all, head_dim),
        ),
    )
    attended = jnp.transpose(per_head, (1, 2, 0, 3)).reshape(tokens, channels)
    output = jnp.dot(
        attended, attention_full[:, 3 * channels :], preferred_element_type=jnp.float32
    )
    return (blended_wide + output.reshape(inputs.shape)).astype(jnp.bfloat16)


def round_up(value, unit):
    return -(-value // unit) * unit


def flip(frame, k):
    z, x = frame // LANES, frame % LANES
    kz, kx = k // LANES, k % LANES
    high = (z // 2 + kz // 2) % 2
    low = (z % 2 + kz % 2) % 2
    return (2 * high + low) * LANES + (x + kx) % 2


def kernel(
    heads, images,
    x_ref, gains_ref, refs_ref, pick_ref, conv_ref, time_ref, attn_ref,
    out_ref,
    x_own, conv_w, time_w, attn_w, shifted, part, partial_out, partial_in, mix, kv, cache, attended,
    local_sem, act_send, act_recv, edge_send, edge_recv, conv_send, conv_recv,
    lane_recv, cross_recv, other_recv, mate_recv, weight_send,
    sum_send, sum_recv, misc_send, misc_recv, cache_send, cache_recv,
):
    y, frame, r = lax.axis_index("groups"), lax.axis_index("frame"), lax.axis_index("row")
    frames = 2 * QUAD
    _, rows, columns, ch = x_ref.shape
    tokens = rows * columns
    head_dim = ch // heads
    share = ch // 8
    conv_rows, time_rows, attn_rows = conv_ref.shape[0], time_ref.shape[0], attn_ref.shape[0]
    conv_quarter = round_up(conv_rows, 64) // 4
    time_quarter = round_up(time_rows, 64) // 4
    time_span = 4 * time_quarter
    f32, bf16 = jnp.float32, jnp.bfloat16
    own = frame % QUAD
    mine, theirs = 2 * y + r, 2 * (1 - y) + r
    mate = {"row": 1 - r}
    opposite = {"groups": 1 - y}

    def rows_at(start, size):
        return pl.ds(pl.multiple_of(start, 16), size)

    def at_frame(k):
        return {"frame": flip(frame, k)}

    def remote(src, dst, send_sem, recv_sem, to):
        return pltpu.make_async_remote_copy(
            src_ref=src, dst_ref=dst, send_sem=send_sem, recv_sem=recv_sem,
            device_id=to, device_id_type=MESH,
        )

    def await_bytes(ref, sem):
        pltpu.make_async_copy(ref, ref, sem).wait()

    def clear(slot, shard):
        for i in range(8):
            start = i * share + jnp.where(i < shard, 0, conv_rows)
            conv_w[slot, rows_at(start, share), :] = jnp.zeros((share, ch), bf16)

    opposite_shard = flip(frame, 4)
    clear(1, opposite_shard)
    partners = [at_frame(k) for k in range(1, frames)] + [mate, opposite]
    barrier = pltpu.get_barrier_semaphore()
    for to in partners:
        pl.semaphore_signal(barrier, inc=1, device_id=to, device_id_type=MESH)

    clear(0, frame)
    fills = [
        pltpu.make_async_copy(x_ref.at[0], x_own, local_sem.at[0]),
        pltpu.make_async_copy(conv_ref, conv_w.at[0, rows_at(frame * share, conv_rows)], local_sem.at[1]),
        pltpu.make_async_copy(time_ref, time_w.at[rows_at(frame * time_span, time_rows)], local_sem.at[2]),
        pltpu.make_async_copy(attn_ref, attn_w.at[rows_at(frame * attn_rows, attn_rows)], local_sem.at[3]),
        pltpu.make_async_copy(refs_ref, cache.at[r, frame], local_sem.at[4]),
    ]
    for f in fills:
        f.start()
    if time_span > time_rows:
        gap = time_span - time_rows
        time_w[rows_at(frame * time_span + time_rows, gap), :] = jnp.zeros((gap, ch), bf16)
    shifted[1, :, rows_at(r * (rows + 1) * columns, columns), :] = jnp.zeros((QUAD, columns, ch), bf16)

    def act(v, g):
        n = normalize(v, gains_ref[g:g + 1, :])
        return n / (1.0 + jnp.exp(-n))

    fills[0].wait()
    own_x = x_own[...].reshape(tokens, ch).astype(f32)
    shifted[1, own, columns:columns + tokens, :] = act(own_x, 0).astype(bf16)
    pl.semaphore_wait(barrier, len(partners))

    own_act = shifted.at[1, own, columns:columns + tokens]
    act_copies = {k: remote(own_act, own_act, act_send.at[k], act_recv.at[k], at_frame(k)) for k in range(1, QUAD)}

    def edge(k):
        slot = flip(own, k)
        return remote(
            shifted.at[1, slot, rows_at(rows * columns - r * (rows - 1) * columns, columns)],
            shifted.at[1, slot, rows_at(r * (rows + 1) * columns, columns)],
            edge_send.at[k], edge_recv.at[k], mate,
        )

    def edge_wait(k):
        slot = flip(own, k)
        await_bytes(shifted.at[1, slot, rows_at((1 - r) * (rows + 1) * columns, columns)], edge_recv.at[k])

    def conv_part(slot, shard, q):
        return conv_w.at[slot, rows_at(shard * share + q * conv_quarter, conv_quarter)]

    def time_part(d, q, count=1):
        return time_w.at[rows_at(d * time_span + q * time_quarter, count * time_quarter)]

    def attn_part(d, q, count=1):
        return attn_w.at[rows_at(d * attn_rows, attn_rows), pl.ds(pl.multiple_of(q * ch, 128), count * ch)]

    def pieces(w):
        return time_part if w == 0 else attn_part

    def send_weight(w, ref, recv_sem, to):
        remote(ref, ref, weight_send.at[w], recv_sem, to).start()

    def weights_across(w):
        send_weight(w, pieces(w)(frame, 2 * r, 2), cross_recv.at[w, 0], at_frame(1))

    def weights_along(w, k):
        send_weight(w, pieces(w)(frame, mine), lane_recv.at[w, k], at_frame(2 * k))

    def from_lane(w, k):
        ref = pieces(w)(flip(frame, 2 * k), mine)
        await_bytes(ref, lane_recv.at[w, k])
        send_weight(w, ref, cross_recv.at[w, k], at_frame(1))
        send_weight(w, ref, other_recv.at[w, 2 * k], opposite)
        send_weight(w, ref, mate_recv.at[w], mate)

    def from_cross(w, k):
        ref = pieces(w)(flip(frame, 1), 2 * r, 2) if k == 0 else pieces(w)(flip(frame, 2 * k + 1), mine)
        await_bytes(ref, cross_recv.at[w, k])
        if k > 0:
            send_weight(w, ref, other_recv.at[w, 2 * k + 1], opposite)
        send_weight(w, ref, mate_recv.at[w], mate)

    def from_other(w, k):
        ref = pieces(w)(flip(frame, k), theirs)
        await_bytes(ref, other_recv.at[w, k])
        send_weight(w, ref, mate_recv.at[w], mate)

    def weight_bytes(w, quarters):
        if w == 0:
            return time_w.at[0:quarters * time_quarter]
        return attn_w.at[0:quarters * attn_rows // 2, 0:2 * ch]

    def from_mate(w):
        await_bytes(weight_bytes(w, 14), mate_recv.at[w])

    def weights_sent(w):
        if w == 0:
            await_bytes(time_w.at[0:28 * time_quarter], weight_send.at[w])
        else:
            await_bytes(attn_w.at[0:7 * attn_rows], weight_send.at[w])

    def exchange(src, dst, k, to):
        return remote(src, dst, misc_send.at[k], misc_recv.at[k], to)

    def share_refs(k):
        return remote(cache.at[r, frame], cache.at[r, frame], cache_send.at[0], cache_recv.at[0], at_frame(k))

    for k in range(1, QUAD):
        act_copies[k].start()
    edge(0).start()
    fills[1].wait()
    conv_lane = remote(conv_part(0, frame, mine), conv_part(1, frame, mine), conv_send.at[0], conv_recv.at[0], at_frame(4))
    conv_lane.start()
    fills[2].wait()
    weights_across(0)
    fills[3].wait()
    weights_across(1)
    fills[4].wait()
    for k in range(1, frames):
        share_refs(k).start()
    for k in range(1, QUAD):
        slot = flip(own, k)
        await_bytes(shifted.at[1, slot, columns:columns + tokens], act_recv.at[k])
        edge(k).start()
    for k in range(1, QUAD):
        weights_along(0, k)

    blank = jnp.zeros((1, ch), f32)

    def shift(k):
        slot = flip(own, k)
        edge_wait(k)
        for i in range(rows + 2):
            span = slice(i * columns, (i + 1) * columns)
            row = shifted[1, slot, span, :].astype(f32)
            shifted[0, slot, span, :] = jnp.concatenate([blank, row[:columns - 1]], axis=0).astype(bf16)
            shifted[2, slot, span, :] = jnp.concatenate([row[1:], blank], axis=0).astype(bf16)

    for k in range(QUAD):
        shift(k)

    def windows(shard, j, slot=None):
        tap = shard + j
        dy, dx = tap // 3, tap % 3
        if slot is None:
            return shifted[dx, :, rows_at(dy * columns, tokens), :].reshape(QUAD * tokens, ch)
        return shifted[dx, slot, rows_at(dy * columns, tokens), :]

    def partial_sum(slot, shard, j, place=None):
        return jnp.dot(windows(shard, j, place), conv_w[slot, j * ch:(j + 1) * ch, :], preferred_element_type=f32)

    part[...] = (partial_sum(0, frame, 0) + partial_sum(0, frame, 1)).reshape(QUAD, tokens, ch)

    from_cross(0, 0)
    from_cross(1, 0)

    await_bytes(conv_part(1, opposite_shard, mine), conv_recv.at[0])
    conv_across = remote(conv_part(1, opposite_shard, mine), conv_part(1, opposite_shard, mine), conv_send.at[1], conv_recv.at[1], opposite)
    conv_mate = remote(conv_part(1, opposite_shard, mine), conv_part(1, opposite_shard, mine), conv_send.at[2], conv_recv.at[2], mate)
    conv_again = remote(conv_part(1, opposite_shard, theirs), conv_part(1, opposite_shard, theirs), conv_send.at[3], conv_recv.at[3], mate)
    conv_across.start()
    conv_mate.start()
    from_lane(0, 1)
    from_cross(0, 1)
    await_bytes(conv_part(1, opposite_shard, theirs), conv_recv.at[1])
    conv_again.start()
    for k in range(1, QUAD):
        weights_along(1, k)
    await_bytes(conv_part(1, opposite_shard, 2 * y + 1 - r), conv_recv.at[2])
    await_bytes(conv_part(1, opposite_shard, 2 * (1 - y) + 1 - r), conv_recv.at[3])

    sums = {}
    total = part[...] + (
        partial_sum(1, opposite_shard, 0) + partial_sum(1, opposite_shard, 1)
    ).reshape(QUAD, tokens, ch)
    part[...] = total
    partial_out[...] = total.astype(bf16)
    for k in range(1, QUAD):
        sums[k] = remote(partial_out.at[flip(own, k)], partial_in.at[own], sum_send.at[k], sum_recv.at[k], at_frame(k))
        sums[k].start()

    from_lane(0, 2)
    from_cross(0, 2)
    from_lane(0, 3)
    from_cross(0, 3)
    for k in range(2, frames):
        from_other(0, k)

    total = own_x + part[own]
    for k in range(1, QUAD):
        slot = flip(own, k)
        await_bytes(partial_in.at[slot], sum_recv.at[k])
        total = total + partial_in[slot].astype(f32)
    hidden = total.astype(bf16).astype(f32)
    mix[1] = act(hidden, 1).astype(bf16)

    @pl.when(frame == 0)
    def _():
        mix[0] = jnp.zeros((tokens, ch), bf16)

    @pl.when(frame == frames - 1)
    def _():
        mix[2] = jnp.zeros((tokens, ch), bf16)

    later = exchange(mix.at[1], mix.at[0], 1, {"frame": jnp.minimum(frame + 1, frames - 1)})
    earlier = exchange(mix.at[1], mix.at[2], 2, {"frame": jnp.maximum(frame - 1, 0)})

    @pl.when(frame < frames - 1)
    def _():
        later.start()

    @pl.when(frame > 0)
    def _():
        earlier.start()

    for k in range(1, QUAD):
        from_lane(1, k)
        from_cross(1, k)
    await_bytes(cache.at[r, 0:frames - 1], cache_recv.at[0])
    cache_mate = remote(cache.at[r], cache.at[r], cache_send.at[1], cache_recv.at[1], mate)
    cache_mate.start()
    from_mate(0)

    def time_tap(t):
        found = []
        at, left = t * ch, ch
        while left:
            shard, inside = at // time_rows, at % time_rows
            count = min(time_rows - inside, left)
            found.append(time_w[shard * time_span + inside:shard * time_span + inside + count, :])
            at, left = at + count, left - count
        return jnp.concatenate(found, axis=0)

    total = hidden + jnp.dot(mix[1], time_tap(1), preferred_element_type=f32)

    @pl.when(frame > 0)
    def _():
        later.wait_recv()

    @pl.when(frame < frames - 1)
    def _():
        earlier.wait_recv()

    total = total + jnp.dot(mix[0], time_tap(0), preferred_element_type=f32)
    total = total + jnp.dot(mix[2], time_tap(2), preferred_element_type=f32)
    blended = total.astype(bf16).astype(f32)
    normed = normalize(blended, gains_ref[2:3, :]).astype(bf16)
    for k in range(2, frames):
        from_other(1, k)
    from_mate(1)
    kv[r] = jnp.dot(normed, attn_w[:, ch:3 * ch], preferred_element_type=f32).astype(bf16)
    swap = exchange(kv.at[r], kv.at[r], 3, mate)
    swap.start()
    queries = jnp.dot(normed, attn_w[:, :ch], preferred_element_type=f32).astype(bf16)
    cache_mate.wait_send()
    await_bytes(cache.at[1 - r], cache_recv.at[1])
    pick = pick_ref[0]
    cached = cache[...].astype(f32).reshape((2 * frames,) + cache.shape[2:])
    picked_keys = jnp.zeros((2 * frames, ch), f32)
    picked_values = jnp.zeros((2 * frames, ch), f32)
    for i in range(images):
        picked_keys = jnp.where(pick == i, cached[:, i, :], picked_keys)
        picked_values = jnp.where(pick == i, cached[:, images + i, :], picked_values)
    picked_keys, picked_values = picked_keys.astype(bf16), picked_values.astype(bf16)
    for k in range(1, QUAD):
        act_copies[k].wait_send()
        sums[k].wait_send()
    for k in range(QUAD):
        edge(k).wait_send()
    for c in (conv_lane, conv_across, conv_mate, conv_again):
        c.wait_send()
    await_bytes(cache.at[r, 0:frames - 1], cache_send.at[0])
    weights_sent(0)
    weights_sent(1)
    swap.wait_send()
    await_bytes(kv.at[1 - r], misc_recv.at[3])
    keys = jnp.concatenate([kv[0, :, :ch], kv[1, :, :ch], picked_keys], axis=0)
    values = jnp.concatenate([kv[0, :, ch:], kv[1, :, ch:], picked_values], axis=0)
    for h in range(heads):
        at = slice(h * head_dim, (h + 1) * head_dim)
        scores = lax.dot_general(
            queries[:, at], keys[:, at], (((1,), (1,)), ((), ())), preferred_element_type=f32
        ) * head_dim ** (-0.5)
        weights = jnp.exp(scores - jnp.max(scores, axis=-1, keepdims=True))
        probs = (weights / jnp.sum(weights, axis=-1, keepdims=True)).astype(bf16)
        attended[:, at] = jnp.dot(probs, values[:, at], preferred_element_type=f32).astype(bf16)
    result = blended + jnp.dot(attended[...], attn_w[:, 3 * ch:], preferred_element_type=f32)
    out_ref[0] = result.astype(bf16).reshape(rows, columns, ch)

    @pl.when(frame < frames - 1)
    def _():
        later.wait_send()

    @pl.when(frame > 0)
    def _():
        earlier.wait_send()


def by_kernel(
    frame_count, frames_in, norm_gains, conv_weight, time_weight, attention_weight,
    reference_keys, reference_values, reference_pick,
):
    _, rows, columns, ch = frames_in.shape
    tokens = rows * columns
    images = reference_keys.shape[0]
    blank = jnp.zeros((-2 * images % 8, ch), reference_keys.dtype)
    refs = jnp.concatenate([reference_keys[:, 0], reference_values[:, 0], blank], axis=0)
    vmem = pl.BlockSpec(memory_space=pltpu.VMEM)
    hbm = pl.BlockSpec(memory_space=pl.ANY)
    dma = pltpu.SemaphoreType.DMA
    bf16 = jnp.bfloat16
    time_span = round_up(time_weight.shape[0], 64)
    conv_span = max(17 * ch // 8, 7 * ch // 8 + round_up(conv_weight.shape[0], 64))
    return pl.pallas_call(
        functools.partial(kernel, HEADS, images),
        out_shape=jax.ShapeDtypeStruct(frames_in.shape, bf16),
        in_specs=[hbm, vmem, hbm, pl.BlockSpec(memory_space=pltpu.SMEM), hbm, hbm, hbm],
        out_specs=vmem,
        scratch_shapes=[
            pltpu.VMEM((rows, columns, ch), bf16),
            pltpu.VMEM((2, conv_span, ch), bf16),
            pltpu.VMEM((frame_count * time_span, ch), bf16),
            pltpu.VMEM((frame_count * attention_weight.shape[0], 4 * ch), bf16),
            pltpu.VMEM((3, QUAD, tokens + 2 * columns, ch), bf16),
            pltpu.VMEM((QUAD, tokens, ch), jnp.float32),
            pltpu.VMEM((QUAD, tokens, ch), bf16),
            pltpu.VMEM((QUAD, tokens, ch), bf16),
            pltpu.VMEM((3, tokens, ch), bf16),
            pltpu.VMEM((2, tokens, 2 * ch), bf16),
            pltpu.VMEM((2, frame_count) + refs.shape, bf16),
            pltpu.VMEM((tokens, ch), bf16),
            dma((5,)),
            dma((QUAD,)),
            dma((QUAD,)),
            dma((QUAD,)),
            dma((QUAD,)),
            dma((4,)),
            dma((4,)),
            dma((2, QUAD)),
            dma((2, QUAD)),
            dma((2, frame_count)),
            dma((2,)),
            dma((2,)),
            dma((QUAD,)),
            dma((QUAD,)),
            dma((4,)),
            dma((4,)),
            dma((2,)),
            dma((2,)),
        ],
        compiler_params=pltpu.CompilerParams(
            collective_id=0, has_side_effects=True, vmem_limit_bytes=40 * 2**20
        ),
    )(frames_in, norm_gains, refs, reference_pick, conv_weight, time_weight, attention_weight)


def on_device(sizes, *operands):
    frames_in, _, conv_weight, time_weight, attention_weight, keys, _, _ = operands
    count = sizes["frame"]
    rows, columns, channels = frames_in.shape[1:]
    share = channels // 8
    fits = (
        sizes["groups"] == 2 and sizes["row"] == 2 and count == 2 * QUAD
        and frames_in.shape[0] == 1 and rows == 2 and columns % 16 == 0 and keys.shape[1] == 1
        and channels % 128 == 0 and conv_weight.shape[0] == 9 * share
        and time_weight.shape[0] == 3 * share and attention_weight.shape[0] == share
    )
    if fits:
        return by_kernel(count, *operands)
    return by_collectives(*operands)


def solution(mesh):
    return jax.shard_map(
        functools.partial(on_device, dict(mesh.shape)),
        mesh=mesh,
        in_specs=(
            P(("groups", "frame"), "row", None, None),
            P(),
            P("frame", None),
            P("frame", None),
            P("frame", None),
            P("groups", ("frame", "row"), None),
            P("groups", ("frame", "row"), None),
            P(("groups", "frame")),
        ),
        out_specs=P(("groups", "frame"), "row", None, None),
        check_vma=False,
    )
```

```python
import functools

import jax
import jax.numpy as jnp
from jax import lax
from jax.experimental import pallas as pl
from jax.experimental.pallas import tpu as pltpu
from jax.sharding import PartitionSpec as P

HEADS = 10
LANES = 2
QUAD = 4
CHUNKS = 3
MESH = pl.DeviceIdType.MESH


def padded_2(x, sides, width):
    for axis, dim in sides:
        devices, length = (lax.axis_size(axis), x.shape[dim])
        up = [(i, (i + 1) % devices) for i in range(devices - 1)]
        down = [(j, i) for i, j in up]
        last = lax.slice_in_dim(x, length - width, length, axis=dim)
        initial = lax.slice_in_dim(x, 0, width, axis=dim)
        before = lax.ppermute(last, axis, up)
        after = lax.ppermute(initial, axis, down)
        x = jnp.concatenate([before, x, after], axis=dim)
    return x


def normalize(values, gain):
    scale = lax.rsqrt(jnp.mean(values * values, axis=-1, keepdims=True) + 1e-05)
    return values * scale * gain


def heads_first(block, head_dim):
    split = block.reshape(block.shape[0], block.shape[1], HEADS, head_dim)
    return jnp.transpose(split, (2, 0, 1, 3))


def by_collectives(
    frames_in,
    norm_gains,
    conv_weight,
    time_weight,
    attention_weight,
    reference_keys,
    reference_values,
    reference_pick,
):
    local_frames, local_rows, columns, channels = frames_in.shape
    head_dim = channels // HEADS
    tokens = local_frames * local_rows * columns
    row_count = lax.axis_size("row")
    row_place = lax.axis_index("row")

    def halve(matrix):
        share = matrix.shape[1] // row_count
        return lax.dynamic_slice_in_dim(matrix, row_place * share, share, 1)

    conv_half, time_half, attention_half = (
        lax.all_gather(halve(conv_weight), "frame", axis=0, tiled=True),
        lax.all_gather(halve(time_weight), "frame", axis=0, tiled=True),
        lax.all_gather(halve(attention_weight), "frame", axis=0, tiled=True),
    )
    conv_full, time_full, attention_full = (
        lax.all_gather(conv_half, "row", axis=1, tiled=True),
        lax.all_gather(time_half, "row", axis=1, tiled=True),
        lax.all_gather(attention_half, "row", axis=1, tiled=True),
    )
    inputs = frames_in.astype(jnp.float32)
    activated = jax.nn.silu(normalize(inputs, norm_gains[0])).astype(jnp.bfloat16)
    padded = padded_2(activated, (("row", 1),), 1)
    padded = jnp.pad(padded, ((0, 0), (0, 0), (1, 1), (0, 0)))
    spatial = jnp.zeros((tokens, channels), jnp.float32)
    for offset_row in range(3):
        for offset_col in range(3):
            window = padded[
                :, offset_row : offset_row + local_rows, offset_col : offset_col + columns, :
            ].reshape(tokens, channels)
            row_start = (3 * offset_row + offset_col) * channels
            spatial = spatial + jnp.dot(
                window,
                conv_full[row_start : row_start + channels],
                preferred_element_type=jnp.float32,
            )
    hidden = (inputs + spatial.reshape(inputs.shape)).astype(jnp.bfloat16)
    hidden_wide = hidden.astype(jnp.float32)
    mixed = jax.nn.silu(normalize(hidden_wide, norm_gains[1])).astype(jnp.bfloat16)
    nearby = padded_2(mixed, (("frame", 0),), 1)
    temporal = jnp.zeros((tokens, channels), jnp.float32)
    for offset_frame in range(3):
        window = nearby[offset_frame : offset_frame + local_frames].reshape(tokens, channels)
        temporal = temporal + jnp.dot(
            window,
            time_full[offset_frame * channels : (offset_frame + 1) * channels],
            preferred_element_type=jnp.float32,
        )
    blended = (hidden_wide + temporal.reshape(inputs.shape)).astype(jnp.bfloat16)
    blended_wide = blended.astype(jnp.float32)
    normed = normalize(blended_wide, norm_gains[2]).astype(jnp.bfloat16).reshape(tokens, channels)
    projected = jnp.dot(
        normed, attention_full[:, : 3 * channels], preferred_element_type=jnp.float32
    ).astype(jnp.bfloat16)
    projected = projected.reshape(local_frames, local_rows * columns, 3 * channels)
    queries = projected[:, :, :channels]
    own_keys = projected[:, :, channels : 2 * channels]
    own_values = projected[:, :, 2 * channels :]
    frame_keys, frame_values = (
        lax.all_gather(own_keys, "row", axis=1, tiled=True),
        lax.all_gather(own_values, "row", axis=1, tiled=True),
    )
    cache_keys, cache_values = (
        lax.all_gather(reference_keys, ("frame", "row"), axis=1, tiled=True),
        lax.all_gather(reference_values, ("frame", "row"), axis=1, tiled=True),
    )
    picked_keys = jnp.take(cache_keys, reference_pick, axis=0)
    picked_values = jnp.take(cache_values, reference_pick, axis=0)
    keys_all = jnp.concatenate([frame_keys, picked_keys], axis=1)
    values_all = jnp.concatenate([frame_values, picked_values], axis=1)

    def one_head(operands):
        query_head, key_head, value_head = operands
        scores = jnp.einsum(
            "fqd,fkd->fqk", query_head, key_head, preferred_element_type=jnp.float32
        ) * head_dim ** (-0.5)
        ceiling = jnp.max(scores, axis=-1, keepdims=True)
        weights = jnp.exp(scores - ceiling)
        probs = (weights / jnp.sum(weights, axis=-1, keepdims=True)).astype(jnp.bfloat16)
        return jnp.einsum(
            "fqk,fkd->fqd", probs, value_head, preferred_element_type=jnp.float32
        ).astype(jnp.bfloat16)

    per_head = lax.map(
        one_head,
        (
            heads_first(queries, head_dim),
            heads_first(keys_all, head_dim),
            heads_first(values_all, head_dim),
        ),
    )
    attended = jnp.transpose(per_head, (1, 2, 0, 3)).reshape(tokens, channels)
    output = jnp.dot(
        attended, attention_full[:, 3 * channels :], preferred_element_type=jnp.float32
    )
    return (blended_wide + output.reshape(inputs.shape)).astype(jnp.bfloat16)


def round_up(value, unit):
    return -(-value // unit) * unit


def flip(frame, k):
    z, x = frame // LANES, frame % LANES
    kz, kx = k // LANES, k % LANES
    high = (z // 2 + kz // 2) % 2
    low = (z % 2 + kz % 2) % 2
    return (2 * high + low) * LANES + (x + kx) % 2


def kernel(
    heads, images,
    x_ref, gains_ref, refs_ref, pick_ref, conv_ref, time_ref, attn_ref,
    out_ref,
    x_own, conv_w, time_w, attn_w, shifted, part, partial_out, partial_in, mix, kv, cache, attended,
    local_sem, act_send, act_recv, edge_send, edge_recv, conv_send, conv_recv,
    lane_recv, cross_recv, other_recv, mate_recv, weight_send,
    sum_send, sum_recv, misc_send, misc_recv, cache_send, cache_recv,
):
    y, frame, r = lax.axis_index("groups"), lax.axis_index("frame"), lax.axis_index("row")
    frames = 2 * QUAD
    _, rows, columns, ch = x_ref.shape
    tokens = rows * columns
    head_dim = ch // heads
    share = ch // 8
    conv_rows, time_rows, attn_rows = conv_ref.shape[0], time_ref.shape[0], attn_ref.shape[0]
    conv_quarter = round_up(conv_rows, 64 * CHUNKS) // 4
    conv_chunk = conv_quarter // CHUNKS
    time_quarter = round_up(time_rows, 64) // 4
    time_span = 4 * time_quarter
    f32, bf16 = jnp.float32, jnp.bfloat16
    own = frame % QUAD
    mine, theirs = 2 * y + r, 2 * (1 - y) + r
    mate = {"row": 1 - r}
    opposite = {"groups": 1 - y}

    def rows_at(start, size):
        return pl.ds(pl.multiple_of(start, 16), size)

    def at_frame(k):
        return {"frame": flip(frame, k)}

    def remote(src, dst, send_sem, recv_sem, to):
        return pltpu.make_async_remote_copy(
            src_ref=src, dst_ref=dst, send_sem=send_sem, recv_sem=recv_sem,
            device_id=to, device_id_type=MESH,
        )

    def await_bytes(ref, sem):
        pltpu.make_async_copy(ref, ref, sem).wait()

    def clear(slot, shard):
        for i in range(8):
            start = i * share + jnp.where(i < shard, 0, conv_rows)
            conv_w[slot, rows_at(start, share), :] = jnp.zeros((share, ch), bf16)

    opposite_shard = flip(frame, 4)
    clear(1, opposite_shard)
    partners = [at_frame(k) for k in range(1, frames)] + [mate, opposite]
    barrier = pltpu.get_barrier_semaphore()
    for to in partners:
        pl.semaphore_signal(barrier, inc=1, device_id=to, device_id_type=MESH)

    clear(0, frame)
    fills = [
        pltpu.make_async_copy(x_ref.at[0], x_own, local_sem.at[0]),
        pltpu.make_async_copy(conv_ref, conv_w.at[0, rows_at(frame * share, conv_rows)], local_sem.at[1]),
        pltpu.make_async_copy(time_ref, time_w.at[rows_at(frame * time_span, time_rows)], local_sem.at[2]),
        pltpu.make_async_copy(attn_ref, attn_w.at[rows_at(frame * attn_rows, attn_rows)], local_sem.at[3]),
        pltpu.make_async_copy(refs_ref, cache.at[r, frame], local_sem.at[4]),
    ]
    for f in fills:
        f.start()
    if time_span > time_rows:
        gap = time_span - time_rows
        time_w[rows_at(frame * time_span + time_rows, gap), :] = jnp.zeros((gap, ch), bf16)
    shifted[1, :, rows_at(r * (rows + 1) * columns, columns), :] = jnp.zeros((QUAD, columns, ch), bf16)

    def act(v, g):
        n = normalize(v, gains_ref[g:g + 1, :])
        return n / (1.0 + jnp.exp(-n))

    fills[0].wait()
    own_x = x_own[...].reshape(tokens, ch).astype(f32)
    shifted[1, own, columns:columns + tokens, :] = act(own_x, 0).astype(bf16)
    pl.semaphore_wait(barrier, len(partners))

    def act_copy(k):
        ref = shifted.at[1, own if k < 3 else flip(own, 1), columns:columns + tokens]
        return remote(ref, ref, act_send.at[k], act_recv.at[k], at_frame(min(k, 2)))

    def edge(k):
        slot = flip(own, k)
        return remote(
            shifted.at[1, slot, rows_at(rows * columns - r * (rows - 1) * columns, columns)],
            shifted.at[1, slot, rows_at(r * (rows + 1) * columns, columns)],
            edge_send.at[k], edge_recv.at[k], mate,
        )

    def edge_wait(k):
        slot = flip(own, k)
        await_bytes(shifted.at[1, slot, rows_at((1 - r) * (rows + 1) * columns, columns)], edge_recv.at[k])

    def conv_part(slot, shard, q, i=0, count=1):
        start = shard * share + q * conv_quarter + i * conv_chunk
        return conv_w.at[slot, rows_at(start, count * conv_chunk)]

    def send_conv(slot, shard, q, i, recv, to):
        remote(
            conv_part(slot, shard, q, i), conv_part(1, shard, q, i),
            conv_send.at[0], conv_recv.at[recv], to,
        ).start()

    def conv_from_lane(i):
        await_bytes(conv_part(1, opposite_shard, mine, i), conv_recv.at[i])
        send_conv(1, opposite_shard, mine, i, CHUNKS + i, opposite)
        send_conv(1, opposite_shard, mine, i, 2 * CHUNKS, mate)

    def conv_from_other(i):
        await_bytes(conv_part(1, opposite_shard, theirs, i), conv_recv.at[CHUNKS + i])
        send_conv(1, opposite_shard, theirs, i, 2 * CHUNKS, mate)

    def conv_from_mate():
        await_bytes(conv_w.at[1, 0:2 * conv_quarter], conv_recv.at[2 * CHUNKS])

    def time_part(d, q, count=1):
        return time_w.at[rows_at(d * time_span + q * time_quarter, count * time_quarter)]

    def attn_part(d, q, count=1):
        return attn_w.at[rows_at(d * attn_rows, attn_rows), pl.ds(pl.multiple_of(q * ch, 128), count * ch)]

    def pieces(w):
        return time_part if w == 0 else attn_part

    def send_weight(w, ref, recv_sem, to):
        remote(ref, ref, weight_send.at[w], recv_sem, to).start()

    def weights_across(w):
        send_weight(w, pieces(w)(frame, 2 * r, 2), cross_recv.at[w, 0], at_frame(1))

    def weights_along(w, k):
        send_weight(w, pieces(w)(frame, mine), lane_recv.at[w, k], at_frame(2 * k))

    def from_lane(w, k):
        ref = pieces(w)(flip(frame, 2 * k), mine)
        await_bytes(ref, lane_recv.at[w, k])
        if k == 3:
            send_weight(w, ref, lane_recv.at[w, 2], at_frame(2))
        send_weight(w, ref, cross_recv.at[w, k], at_frame(1))
        send_weight(w, ref, other_recv.at[w, 2 * k], opposite)
        send_weight(w, ref, mate_recv.at[w], mate)

    def from_cross(w, k):
        ref = pieces(w)(flip(frame, 1), 2 * r, 2) if k == 0 else pieces(w)(flip(frame, 2 * k + 1), mine)
        await_bytes(ref, cross_recv.at[w, k])
        if k > 0:
            send_weight(w, ref, other_recv.at[w, 2 * k + 1], opposite)
        send_weight(w, ref, mate_recv.at[w], mate)

    def from_other(w, k):
        ref = pieces(w)(flip(frame, k), theirs)
        await_bytes(ref, other_recv.at[w, k])
        send_weight(w, ref, mate_recv.at[w], mate)

    def weight_bytes(w, quarters):
        if w == 0:
            return time_w.at[0:quarters * time_quarter]
        return attn_w.at[0:quarters * attn_rows // 2, 0:2 * ch]

    def from_mate(w):
        await_bytes(weight_bytes(w, 14), mate_recv.at[w])

    def weights_sent(w):
        if w == 0:
            await_bytes(time_w.at[0:28 * time_quarter], weight_send.at[w])
        else:
            await_bytes(attn_w.at[0:7 * attn_rows], weight_send.at[w])

    def exchange(src, dst, k, to):
        return remote(src, dst, misc_send.at[k], misc_recv.at[k], to)

    def share_refs(k):
        return remote(cache.at[r, frame], cache.at[r, frame], cache_send.at[0], cache_recv.at[0], at_frame(k))

    act_copy(1).start()
    act_copy(2).start()
    edge(0).start()
    fills[1].wait()
    for i in range(CHUNKS):
        send_conv(0, frame, mine, i, i, at_frame(4))
    fills[2].wait()
    weights_across(0)
    fills[3].wait()
    weights_across(1)
    fills[4].wait()
    for k in range(1, frames):
        share_refs(k).start()

    def from_quad(k):
        slot = flip(own, k)
        await_bytes(shifted.at[1, slot, columns:columns + tokens], act_recv.at[k])
        if k == 1:
            act_copy(3).start()
        edge(k).start()

    from_quad(1)
    from_quad(2)
    conv_from_lane(0)
    conv_from_lane(1)
    from_quad(3)
    weights_along(0, 3)
    weights_along(0, 1)
    conv_from_lane(2)
    from_cross(0, 0)

    blank = jnp.zeros((1, ch), f32)

    def shift(k):
        slot = flip(own, k)
        edge_wait(k)
        for i in range(rows + 2):
            span = slice(i * columns, (i + 1) * columns)
            row = shifted[1, slot, span, :].astype(f32)
            shifted[0, slot, span, :] = jnp.concatenate([blank, row[:columns - 1]], axis=0).astype(bf16)
            shifted[2, slot, span, :] = jnp.concatenate([row[1:], blank], axis=0).astype(bf16)

    for k in range(QUAD):
        shift(k)

    def windows(shard, j, slot=None):
        tap = shard + j
        dy, dx = tap // 3, tap % 3
        if slot is None:
            return shifted[dx, :, rows_at(dy * columns, tokens), :].reshape(QUAD * tokens, ch)
        return shifted[dx, slot, rows_at(dy * columns, tokens), :]

    def partial_sum(slot, shard, j, place=None):
        return jnp.dot(windows(shard, j, place), conv_w[slot, j * ch:(j + 1) * ch, :], preferred_element_type=f32)

    part[...] = (partial_sum(0, frame, 0) + partial_sum(0, frame, 1)).reshape(QUAD, tokens, ch)

    weights_along(1, 3)
    for i in range(CHUNKS):
        conv_from_other(i)
    from_lane(0, 3)
    conv_from_mate()
    sums = {}
    total = part[...] + (
        partial_sum(1, opposite_shard, 0) + partial_sum(1, opposite_shard, 1)
    ).reshape(QUAD, tokens, ch)
    part[...] = total
    partial_out[...] = total.astype(bf16)
    for k in range(1, QUAD):
        sums[k] = remote(partial_out.at[flip(own, k)], partial_in.at[own], sum_send.at[k], sum_recv.at[k], at_frame(k))
        sums[k].start()

    weights_along(1, 1)
    from_lane(0, 1)
    from_cross(1, 0)
    from_lane(0, 2)
    from_cross(0, 3)
    from_cross(0, 1)
    from_other(0, 6)
    from_lane(1, 3)

    total = own_x + part[own]
    for k in range(1, QUAD):
        slot = flip(own, k)
        await_bytes(partial_in.at[slot], sum_recv.at[k])
        total = total + partial_in[slot].astype(f32)
    hidden = total.astype(bf16).astype(f32)
    mix[1] = act(hidden, 1).astype(bf16)

    @pl.when(frame == 0)
    def _():
        mix[0] = jnp.zeros((tokens, ch), bf16)

    @pl.when(frame == frames - 1)
    def _():
        mix[2] = jnp.zeros((tokens, ch), bf16)

    later = exchange(mix.at[1], mix.at[0], 1, {"frame": jnp.minimum(frame + 1, frames - 1)})
    earlier = exchange(mix.at[1], mix.at[2], 2, {"frame": jnp.maximum(frame - 1, 0)})

    @pl.when(frame < frames - 1)
    def _():
        later.start()

    @pl.when(frame > 0)
    def _():
        earlier.start()

    from_other(0, 2)
    from_cross(0, 2)
    from_other(0, 4)
    from_lane(1, 1)
    from_other(0, 7)
    from_other(0, 3)
    from_lane(1, 2)
    from_other(0, 5)
    from_cross(1, 3)
    from_other(1, 6)
    from_cross(1, 1)
    await_bytes(cache.at[r, 0:frames - 1], cache_recv.at[0])
    cache_mate = remote(cache.at[r], cache.at[r], cache_send.at[1], cache_recv.at[1], mate)
    cache_mate.start()
    from_mate(0)

    def time_tap(t):
        found = []
        at, left = t * ch, ch
        while left:
            shard, inside = at // time_rows, at % time_rows
            count = min(time_rows - inside, left)
            found.append(time_w[shard * time_span + inside:shard * time_span + inside + count, :])
            at, left = at + count, left - count
        return jnp.concatenate(found, axis=0)

    total = hidden + jnp.dot(mix[1], time_tap(1), preferred_element_type=f32)

    @pl.when(frame > 0)
    def _():
        later.wait_recv()

    @pl.when(frame < frames - 1)
    def _():
        earlier.wait_recv()

    total = total + jnp.dot(mix[0], time_tap(0), preferred_element_type=f32)
    total = total + jnp.dot(mix[2], time_tap(2), preferred_element_type=f32)
    blended = total.astype(bf16).astype(f32)
    normed = normalize(blended, gains_ref[2:3, :]).astype(bf16)
    from_other(1, 2)
    from_cross(1, 2)
    for k in (7, 4, 3, 5):
        from_other(1, k)
    from_mate(1)
    kv[r] = jnp.dot(normed, attn_w[:, ch:3 * ch], preferred_element_type=f32).astype(bf16)
    swap = exchange(kv.at[r], kv.at[r], 3, mate)
    swap.start()
    queries = jnp.dot(normed, attn_w[:, :ch], preferred_element_type=f32).astype(bf16)
    cache_mate.wait_send()
    await_bytes(cache.at[1 - r], cache_recv.at[1])
    pick = pick_ref[0]
    cached = cache[...].astype(f32).reshape((2 * frames,) + cache.shape[2:])
    picked_keys = jnp.zeros((2 * frames, ch), f32)
    picked_values = jnp.zeros((2 * frames, ch), f32)
    for i in range(images):
        picked_keys = jnp.where(pick == i, cached[:, i, :], picked_keys)
        picked_values = jnp.where(pick == i, cached[:, images + i, :], picked_values)
    picked_keys, picked_values = picked_keys.astype(bf16), picked_values.astype(bf16)
    for k in range(1, QUAD):
        act_copy(k).wait_send()
        sums[k].wait_send()
    for k in range(QUAD):
        edge(k).wait_send()
    await_bytes(conv_w.at[0, 0:4 * conv_quarter], conv_send.at[0])
    await_bytes(cache.at[r, 0:frames - 1], cache_send.at[0])
    weights_sent(0)
    weights_sent(1)
    swap.wait_send()
    await_bytes(kv.at[1 - r], misc_recv.at[3])
    keys = jnp.concatenate([kv[0, :, :ch], kv[1, :, :ch], picked_keys], axis=0)
    values = jnp.concatenate([kv[0, :, ch:], kv[1, :, ch:], picked_values], axis=0)
    for h in range(heads):
        at = slice(h * head_dim, (h + 1) * head_dim)
        scores = lax.dot_general(
            queries[:, at], keys[:, at], (((1,), (1,)), ((), ())), preferred_element_type=f32
        ) * head_dim ** (-0.5)
        weights = jnp.exp(scores - jnp.max(scores, axis=-1, keepdims=True))
        probs = (weights / jnp.sum(weights, axis=-1, keepdims=True)).astype(bf16)
        attended[:, at] = jnp.dot(probs, values[:, at], preferred_element_type=f32).astype(bf16)
    result = blended + jnp.dot(attended[...], attn_w[:, 3 * ch:], preferred_element_type=f32)
    out_ref[0] = result.astype(bf16).reshape(rows, columns, ch)

    @pl.when(frame < frames - 1)
    def _():
        later.wait_send()

    @pl.when(frame > 0)
    def _():
        earlier.wait_send()


def by_kernel(
    frame_count, frames_in, norm_gains, conv_weight, time_weight, attention_weight,
    reference_keys, reference_values, reference_pick,
):
    _, rows, columns, ch = frames_in.shape
    tokens = rows * columns
    images = reference_keys.shape[0]
    blank = jnp.zeros((-2 * images % 8, ch), reference_keys.dtype)
    refs = jnp.concatenate([reference_keys[:, 0], reference_values[:, 0], blank], axis=0)
    vmem = pl.BlockSpec(memory_space=pltpu.VMEM)
    hbm = pl.BlockSpec(memory_space=pl.ANY)
    dma = pltpu.SemaphoreType.DMA
    bf16 = jnp.bfloat16
    time_span = round_up(time_weight.shape[0], 64)
    conv_span = max(17 * ch // 8, 7 * ch // 8 + round_up(conv_weight.shape[0], 64 * CHUNKS))
    return pl.pallas_call(
        functools.partial(kernel, HEADS, images),
        out_shape=jax.ShapeDtypeStruct(frames_in.shape, bf16),
        in_specs=[hbm, vmem, hbm, pl.BlockSpec(memory_space=pltpu.SMEM), hbm, hbm, hbm],
        out_specs=vmem,
        scratch_shapes=[
            pltpu.VMEM((rows, columns, ch), bf16),
            pltpu.VMEM((2, conv_span, ch), bf16),
            pltpu.VMEM((frame_count * time_span, ch), bf16),
            pltpu.VMEM((frame_count * attention_weight.shape[0], 4 * ch), bf16),
            pltpu.VMEM((3, QUAD, tokens + 2 * columns, ch), bf16),
            pltpu.VMEM((QUAD, tokens, ch), jnp.float32),
            pltpu.VMEM((QUAD, tokens, ch), bf16),
            pltpu.VMEM((QUAD, tokens, ch), bf16),
            pltpu.VMEM((3, tokens, ch), bf16),
            pltpu.VMEM((2, tokens, 2 * ch), bf16),
            pltpu.VMEM((2, frame_count) + refs.shape, bf16),
            pltpu.VMEM((tokens, ch), bf16),
            dma((5,)),
            dma((QUAD,)),
            dma((QUAD,)),
            dma((QUAD,)),
            dma((QUAD,)),
            dma((1,)),
            dma((2 * CHUNKS + 1,)),
            dma((2, QUAD)),
            dma((2, QUAD)),
            dma((2, frame_count)),
            dma((2,)),
            dma((2,)),
            dma((QUAD,)),
            dma((QUAD,)),
            dma((4,)),
            dma((4,)),
            dma((2,)),
            dma((2,)),
        ],
        compiler_params=pltpu.CompilerParams(
            collective_id=0, has_side_effects=True, vmem_limit_bytes=60 * 2**20
        ),
    )(frames_in, norm_gains, refs, reference_pick, conv_weight, time_weight, attention_weight)


def on_device(sizes, *operands):
    frames_in, _, conv_weight, time_weight, attention_weight, keys, _, _ = operands
    count = sizes["frame"]
    rows, columns, channels = frames_in.shape[1:]
    share = channels // 8
    fits = (
        sizes["groups"] == 2 and sizes["row"] == 2 and count == 2 * QUAD
        and frames_in.shape[0] == 1 and rows == 2 and columns % 16 == 0 and keys.shape[1] == 1
        and channels % 128 == 0 and conv_weight.shape[0] == 9 * share
        and time_weight.shape[0] == 3 * share and attention_weight.shape[0] == share
    )
    if fits:
        return by_kernel(count, *operands)
    return by_collectives(*operands)


def solution(mesh):
    return jax.shard_map(
        functools.partial(on_device, dict(mesh.shape)),
        mesh=mesh,
        in_specs=(
            P(("groups", "frame"), "row", None, None),
            P(),
            P("frame", None),
            P("frame", None),
            P("frame", None),
            P("groups", ("frame", "row"), None),
            P("groups", ("frame", "row"), None),
            P(("groups", "frame")),
        ),
        out_specs=P(("groups", "frame"), "row", None, None),
        check_vma=False,
    )
```

```python
import functools

import jax
import jax.numpy as jnp
from jax import lax
from jax.experimental import pallas as pl
from jax.experimental.pallas import tpu as pltpu
from jax.sharding import PartitionSpec as P

HEADS = 10
LANES = 2
QUAD = 4
CHUNKS = 3
MESH = pl.DeviceIdType.MESH


def padded_2(x, sides, width):
    for axis, dim in sides:
        devices, length = (lax.axis_size(axis), x.shape[dim])
        up = [(i, (i + 1) % devices) for i in range(devices - 1)]
        down = [(j, i) for i, j in up]
        last = lax.slice_in_dim(x, length - width, length, axis=dim)
        initial = lax.slice_in_dim(x, 0, width, axis=dim)
        before = lax.ppermute(last, axis, up)
        after = lax.ppermute(initial, axis, down)
        x = jnp.concatenate([before, x, after], axis=dim)
    return x


def normalize(values, gain):
    scale = lax.rsqrt(jnp.mean(values * values, axis=-1, keepdims=True) + 1e-05)
    return values * scale * gain


def heads_first(block, head_dim):
    split = block.reshape(block.shape[0], block.shape[1], HEADS, head_dim)
    return jnp.transpose(split, (2, 0, 1, 3))


def by_collectives(
    frames_in,
    norm_gains,
    conv_weight,
    time_weight,
    attention_weight,
    reference_keys,
    reference_values,
    reference_pick,
):
    local_frames, local_rows, columns, channels = frames_in.shape
    head_dim = channels // HEADS
    tokens = local_frames * local_rows * columns
    row_count = lax.axis_size("row")
    row_place = lax.axis_index("row")

    def halve(matrix):
        share = matrix.shape[1] // row_count
        return lax.dynamic_slice_in_dim(matrix, row_place * share, share, 1)

    conv_half, time_half, attention_half = (
        lax.all_gather(halve(conv_weight), "frame", axis=0, tiled=True),
        lax.all_gather(halve(time_weight), "frame", axis=0, tiled=True),
        lax.all_gather(halve(attention_weight), "frame", axis=0, tiled=True),
    )
    conv_full, time_full, attention_full = (
        lax.all_gather(conv_half, "row", axis=1, tiled=True),
        lax.all_gather(time_half, "row", axis=1, tiled=True),
        lax.all_gather(attention_half, "row", axis=1, tiled=True),
    )
    inputs = frames_in.astype(jnp.float32)
    activated = jax.nn.silu(normalize(inputs, norm_gains[0])).astype(jnp.bfloat16)
    padded = padded_2(activated, (("row", 1),), 1)
    padded = jnp.pad(padded, ((0, 0), (0, 0), (1, 1), (0, 0)))
    spatial = jnp.zeros((tokens, channels), jnp.float32)
    for offset_row in range(3):
        for offset_col in range(3):
            window = padded[
                :, offset_row : offset_row + local_rows, offset_col : offset_col + columns, :
            ].reshape(tokens, channels)
            row_start = (3 * offset_row + offset_col) * channels
            spatial = spatial + jnp.dot(
                window,
                conv_full[row_start : row_start + channels],
                preferred_element_type=jnp.float32,
            )
    hidden = (inputs + spatial.reshape(inputs.shape)).astype(jnp.bfloat16)
    hidden_wide = hidden.astype(jnp.float32)
    mixed = jax.nn.silu(normalize(hidden_wide, norm_gains[1])).astype(jnp.bfloat16)
    nearby = padded_2(mixed, (("frame", 0),), 1)
    temporal = jnp.zeros((tokens, channels), jnp.float32)
    for offset_frame in range(3):
        window = nearby[offset_frame : offset_frame + local_frames].reshape(tokens, channels)
        temporal = temporal + jnp.dot(
            window,
            time_full[offset_frame * channels : (offset_frame + 1) * channels],
            preferred_element_type=jnp.float32,
        )
    blended = (hidden_wide + temporal.reshape(inputs.shape)).astype(jnp.bfloat16)
    blended_wide = blended.astype(jnp.float32)
    normed = normalize(blended_wide, norm_gains[2]).astype(jnp.bfloat16).reshape(tokens, channels)
    projected = jnp.dot(
        normed, attention_full[:, : 3 * channels], preferred_element_type=jnp.float32
    ).astype(jnp.bfloat16)
    projected = projected.reshape(local_frames, local_rows * columns, 3 * channels)
    queries = projected[:, :, :channels]
    own_keys = projected[:, :, channels : 2 * channels]
    own_values = projected[:, :, 2 * channels :]
    frame_keys, frame_values = (
        lax.all_gather(own_keys, "row", axis=1, tiled=True),
        lax.all_gather(own_values, "row", axis=1, tiled=True),
    )
    cache_keys, cache_values = (
        lax.all_gather(reference_keys, ("frame", "row"), axis=1, tiled=True),
        lax.all_gather(reference_values, ("frame", "row"), axis=1, tiled=True),
    )
    picked_keys = jnp.take(cache_keys, reference_pick, axis=0)
    picked_values = jnp.take(cache_values, reference_pick, axis=0)
    keys_all = jnp.concatenate([frame_keys, picked_keys], axis=1)
    values_all = jnp.concatenate([frame_values, picked_values], axis=1)

    def one_head(operands):
        query_head, key_head, value_head = operands
        scores = jnp.einsum(
            "fqd,fkd->fqk", query_head, key_head, preferred_element_type=jnp.float32
        ) * head_dim ** (-0.5)
        ceiling = jnp.max(scores, axis=-1, keepdims=True)
        weights = jnp.exp(scores - ceiling)
        probs = (weights / jnp.sum(weights, axis=-1, keepdims=True)).astype(jnp.bfloat16)
        return jnp.einsum(
            "fqk,fkd->fqd", probs, value_head, preferred_element_type=jnp.float32
        ).astype(jnp.bfloat16)

    per_head = lax.map(
        one_head,
        (
            heads_first(queries, head_dim),
            heads_first(keys_all, head_dim),
            heads_first(values_all, head_dim),
        ),
    )
    attended = jnp.transpose(per_head, (1, 2, 0, 3)).reshape(tokens, channels)
    output = jnp.dot(
        attended, attention_full[:, 3 * channels :], preferred_element_type=jnp.float32
    )
    return (blended_wide + output.reshape(inputs.shape)).astype(jnp.bfloat16)


def round_up(value, unit):
    return -(-value // unit) * unit


def flip(frame, k):
    z, x = frame // LANES, frame % LANES
    kz, kx = k // LANES, k % LANES
    high = (z // 2 + kz // 2) % 2
    low = (z % 2 + kz % 2) % 2
    return (2 * high + low) * LANES + (x + kx) % 2


def kernel(
    heads, images,
    x_ref, gains_ref, keys_ref, values_ref, pick_ref, conv_ref, time_ref, attn_ref,
    out_ref,
    x_own, conv_w, time_w, attn_w, shifted, part, partial_out, partial_in, mix, kv, cache, attended,
    local_sem, act_send, act_recv, edge_send, edge_recv, conv_send, conv_recv,
    lane_recv, cross_recv, other_recv, mate_recv, weight_send,
    sum_send, sum_recv, misc_send, misc_recv, cache_send, cache_recv,
):
    y, frame, r = lax.axis_index("groups"), lax.axis_index("frame"), lax.axis_index("row")
    frames = 2 * QUAD
    _, rows, columns, ch = x_ref.shape
    tokens = rows * columns
    head_dim = ch // heads
    share = ch // 8
    conv_rows, time_rows, attn_rows = conv_ref.shape[0], time_ref.shape[0], attn_ref.shape[0]
    conv_quarter = round_up(conv_rows, 64 * CHUNKS) // 4
    conv_chunk = conv_quarter // CHUNKS
    time_quarter = round_up(time_rows, 64) // 4
    time_span = 4 * time_quarter
    f32, bf16 = jnp.float32, jnp.bfloat16
    own = frame % QUAD
    mine, theirs = 2 * y + r, 2 * (1 - y) + r
    mate = {"row": 1 - r}
    opposite = {"groups": 1 - y}

    def rows_at(start, size):
        return pl.ds(pl.multiple_of(start, 16), size)

    def at_frame(k):
        return {"frame": flip(frame, k)}

    def remote(src, dst, send_sem, recv_sem, to):
        return pltpu.make_async_remote_copy(
            src_ref=src, dst_ref=dst, send_sem=send_sem, recv_sem=recv_sem,
            device_id=to, device_id_type=MESH,
        )

    def await_bytes(ref, sem):
        pltpu.make_async_copy(ref, ref, sem).wait()

    def clear(slot, shard):
        for i in range(8):
            start = i * share + jnp.where(i < shard, 0, conv_rows)
            conv_w[slot, rows_at(start, share), :] = jnp.zeros((share, ch), bf16)

    opposite_shard = flip(frame, 4)
    clear(1, opposite_shard)
    partners = [at_frame(k) for k in range(1, frames)] + [mate, opposite]
    barrier = pltpu.get_barrier_semaphore()
    for to in partners:
        pl.semaphore_signal(barrier, inc=1, device_id=to, device_id_type=MESH)

    clear(0, frame)
    fills = [
        pltpu.make_async_copy(x_ref.at[0], x_own, local_sem.at[0]),
        pltpu.make_async_copy(conv_ref, conv_w.at[0, rows_at(frame * share, conv_rows)], local_sem.at[1]),
        pltpu.make_async_copy(time_ref, time_w.at[rows_at(frame * time_span, time_rows)], local_sem.at[2]),
        pltpu.make_async_copy(attn_ref, attn_w.at[rows_at(frame * attn_rows, attn_rows)], local_sem.at[3]),
        pltpu.make_async_copy(keys_ref, cache.at[r, frame, 0], local_sem.at[4]),
        pltpu.make_async_copy(values_ref, cache.at[r, frame, 1], local_sem.at[5]),
    ]
    for f in fills:
        f.start()
    if time_span > time_rows:
        gap = time_span - time_rows
        time_w[rows_at(frame * time_span + time_rows, gap), :] = jnp.zeros((gap, ch), bf16)
    shifted[1, :, rows_at(r * (rows + 1) * columns, columns), :] = jnp.zeros((QUAD, columns, ch), bf16)

    def act(v, g):
        n = normalize(v, gains_ref[g:g + 1, :])
        return n / (1.0 + jnp.exp(-n))

    fills[0].wait()
    own_x = x_own[...].reshape(tokens, ch).astype(f32)
    shifted[1, own, columns:columns + tokens, :] = act(own_x, 0).astype(bf16)
    pl.semaphore_wait(barrier, len(partners))

    def act_copy(k):
        ref = shifted.at[1, own if k < 3 else flip(own, 1), columns:columns + tokens]
        return remote(ref, ref, act_send.at[k], act_recv.at[k], at_frame(min(k, 2)))

    def edge(k):
        slot = flip(own, k)
        return remote(
            shifted.at[1, slot, rows_at(rows * columns - r * (rows - 1) * columns, columns)],
            shifted.at[1, slot, rows_at(r * (rows + 1) * columns, columns)],
            edge_send.at[k], edge_recv.at[k], mate,
        )

    def edge_wait(k):
        slot = flip(own, k)
        await_bytes(shifted.at[1, slot, rows_at((1 - r) * (rows + 1) * columns, columns)], edge_recv.at[k])

    def conv_part(slot, shard, q, i=0, count=1):
        start = shard * share + q * conv_quarter + i * conv_chunk
        return conv_w.at[slot, rows_at(start, count * conv_chunk)]

    def send_conv(slot, shard, q, i, recv, to):
        remote(
            conv_part(slot, shard, q, i), conv_part(1, shard, q, i),
            conv_send.at[0], conv_recv.at[recv], to,
        ).start()

    def conv_from_lane(i):
        await_bytes(conv_part(1, opposite_shard, mine, i), conv_recv.at[i])
        send_conv(1, opposite_shard, mine, i, CHUNKS + i, opposite)
        send_conv(1, opposite_shard, mine, i, 2 * CHUNKS, mate)

    def conv_from_other(i):
        await_bytes(conv_part(1, opposite_shard, theirs, i), conv_recv.at[CHUNKS + i])
        send_conv(1, opposite_shard, theirs, i, 2 * CHUNKS, mate)

    def conv_from_mate():
        await_bytes(conv_w.at[1, 0:2 * conv_quarter], conv_recv.at[2 * CHUNKS])

    def time_part(d, q, count=1):
        return time_w.at[rows_at(d * time_span + q * time_quarter, count * time_quarter)]

    def attn_part(d, q, count=1):
        return attn_w.at[rows_at(d * attn_rows, attn_rows), pl.ds(pl.multiple_of(q * ch, 128), count * ch)]

    def pieces(w):
        return time_part if w == 0 else attn_part

    def send_weight(w, ref, recv_sem, to):
        remote(ref, ref, weight_send.at[w], recv_sem, to).start()

    def weights_across(w):
        send_weight(w, pieces(w)(frame, 2 * r, 2), cross_recv.at[w, 0], at_frame(1))

    def weights_along(w, k):
        send_weight(w, pieces(w)(frame, mine), lane_recv.at[w, k], at_frame(2 * k))

    def from_lane(w, k):
        ref = pieces(w)(flip(frame, 2 * k), mine)
        await_bytes(ref, lane_recv.at[w, k])
        if k == 3:
            send_weight(w, ref, lane_recv.at[w, 2], at_frame(2))
        send_weight(w, ref, cross_recv.at[w, k], at_frame(1))
        send_weight(w, ref, other_recv.at[w, 2 * k], opposite)
        send_weight(w, ref, mate_recv.at[w], mate)

    def from_cross(w, k):
        ref = pieces(w)(flip(frame, 1), 2 * r, 2) if k == 0 else pieces(w)(flip(frame, 2 * k + 1), mine)
        await_bytes(ref, cross_recv.at[w, k])
        if k > 0:
            send_weight(w, ref, other_recv.at[w, 2 * k + 1], opposite)
        send_weight(w, ref, mate_recv.at[w], mate)

    def from_other(w, k):
        ref = pieces(w)(flip(frame, k), theirs)
        await_bytes(ref, other_recv.at[w, k])
        send_weight(w, ref, mate_recv.at[w], mate)

    def weight_bytes(w, quarters):
        if w == 0:
            return time_w.at[0:quarters * time_quarter]
        return attn_w.at[0:quarters * attn_rows // 2, 0:2 * ch]

    def from_mate(w):
        await_bytes(weight_bytes(w, 14), mate_recv.at[w])

    def weights_sent(w):
        if w == 0:
            await_bytes(time_w.at[0:28 * time_quarter], weight_send.at[w])
        else:
            await_bytes(attn_w.at[0:7 * attn_rows], weight_send.at[w])

    def exchange(src, dst, k, to):
        return remote(src, dst, misc_send.at[k], misc_recv.at[k], to)

    def share_refs(k):
        return remote(cache.at[r, frame], cache.at[r, frame], cache_send.at[0], cache_recv.at[0], at_frame(k))

    act_copy(1).start()
    act_copy(2).start()
    edge(0).start()
    fills[1].wait()
    for i in range(CHUNKS):
        send_conv(0, frame, mine, i, i, at_frame(4))
    fills[2].wait()
    fills[3].wait()
    fills[4].wait()
    fills[5].wait()
    for k in range(1, frames):
        share_refs(k).start()

    def from_quad(k):
        slot = flip(own, k)
        await_bytes(shifted.at[1, slot, columns:columns + tokens], act_recv.at[k])
        if k == 1:
            act_copy(3).start()
        edge(k).start()

    from_quad(1)
    weights_across(0)
    weights_across(1)
    from_quad(2)
    conv_from_lane(0)
    conv_from_lane(1)
    from_quad(3)
    weights_along(0, 3)
    weights_along(0, 1)
    conv_from_lane(2)
    weights_along(1, 3)
    weights_along(1, 1)
    from_cross(0, 0)
    conv_from_other(0)

    blank = jnp.zeros((1, ch), f32)

    def shift(k):
        slot = flip(own, k)
        edge_wait(k)
        for i in range(rows + 2):
            span = slice(i * columns, (i + 1) * columns)
            row = shifted[1, slot, span, :].astype(f32)
            shifted[0, slot, span, :] = jnp.concatenate([blank, row[:columns - 1]], axis=0).astype(bf16)
            shifted[2, slot, span, :] = jnp.concatenate([row[1:], blank], axis=0).astype(bf16)

    for k in range(QUAD):
        shift(k)

    def windows(shard, j, slot=None):
        tap = shard + j
        dy, dx = tap // 3, tap % 3
        if slot is None:
            return shifted[dx, :, rows_at(dy * columns, tokens), :].reshape(QUAD * tokens, ch)
        return shifted[dx, slot, rows_at(dy * columns, tokens), :]

    def partial_sum(slot, shard, j, place=None):
        return jnp.dot(windows(shard, j, place), conv_w[slot, j * ch:(j + 1) * ch, :], preferred_element_type=f32)

    part[...] = (partial_sum(0, frame, 0) + partial_sum(0, frame, 1)).reshape(QUAD, tokens, ch)

    for i in range(1, CHUNKS):
        conv_from_other(i)
    from_lane(0, 3)
    from_lane(0, 1)
    conv_from_mate()
    sums = {}
    total = part[...] + (
        partial_sum(1, opposite_shard, 0) + partial_sum(1, opposite_shard, 1)
    ).reshape(QUAD, tokens, ch)
    part[...] = total
    partial_out[...] = total.astype(bf16)
    for k in range(1, QUAD):
        sums[k] = remote(partial_out.at[flip(own, k)], partial_in.at[own], sum_send.at[k], sum_recv.at[k], at_frame(k))
        sums[k].start()

    from_cross(1, 0)
    from_lane(0, 2)
    from_cross(0, 3)
    from_cross(0, 1)
    from_lane(1, 3)
    from_other(0, 6)
    from_lane(1, 1)
    from_other(0, 2)

    total = own_x + part[own]
    for k in range(1, QUAD):
        slot = flip(own, k)
        await_bytes(partial_in.at[slot], sum_recv.at[k])
        total = total + partial_in[slot].astype(f32)
    hidden = total.astype(bf16).astype(f32)
    mix[1] = act(hidden, 1).astype(bf16)

    @pl.when(frame == 0)
    def _():
        mix[0] = jnp.zeros((tokens, ch), bf16)

    @pl.when(frame == frames - 1)
    def _():
        mix[2] = jnp.zeros((tokens, ch), bf16)

    later = exchange(mix.at[1], mix.at[0], 1, {"frame": jnp.minimum(frame + 1, frames - 1)})
    earlier = exchange(mix.at[1], mix.at[2], 2, {"frame": jnp.maximum(frame - 1, 0)})

    @pl.when(frame < frames - 1)
    def _():
        later.start()

    @pl.when(frame > 0)
    def _():
        earlier.start()

    from_cross(0, 2)
    from_other(0, 7)
    from_other(0, 3)
    from_other(0, 4)
    from_lane(1, 2)
    from_cross(1, 3)
    from_other(0, 5)
    from_cross(1, 1)
    from_other(1, 6)
    await_bytes(cache.at[r, 0:frames - 1], cache_recv.at[0])
    cache_mate = remote(cache.at[r], cache.at[r], cache_send.at[1], cache_recv.at[1], mate)
    cache_mate.start()
    from_mate(0)

    def time_tap(t):
        found = []
        at, left = t * ch, ch
        while left:
            shard, inside = at // time_rows, at % time_rows
            count = min(time_rows - inside, left)
            found.append(time_w[shard * time_span + inside:shard * time_span + inside + count, :])
            at, left = at + count, left - count
        return jnp.concatenate(found, axis=0)

    total = hidden + jnp.dot(mix[1], time_tap(1), preferred_element_type=f32)

    @pl.when(frame > 0)
    def _():
        later.wait_recv()

    @pl.when(frame < frames - 1)
    def _():
        earlier.wait_recv()

    total = total + jnp.dot(mix[0], time_tap(0), preferred_element_type=f32)
    total = total + jnp.dot(mix[2], time_tap(2), preferred_element_type=f32)
    blended = total.astype(bf16).astype(f32)
    normed = normalize(blended, gains_ref[2:3, :]).astype(bf16)
    await_bytes(cache.at[1 - r], cache_recv.at[1])
    pick = pick_ref[0]
    cached = cache[...].astype(f32).reshape(2 * frames, 2, images, ch)
    picked_keys = jnp.zeros((2 * frames, ch), f32)
    picked_values = jnp.zeros((2 * frames, ch), f32)
    for i in range(images):
        picked_keys = jnp.where(pick == i, cached[:, 0, i, :], picked_keys)
        picked_values = jnp.where(pick == i, cached[:, 1, i, :], picked_values)
    picked_keys, picked_values = picked_keys.astype(bf16), picked_values.astype(bf16)
    from_cross(1, 2)
    from_other(1, 2)
    for k in (7, 3, 4, 5):
        from_other(1, k)
    from_mate(1)
    own_keys, own_values = kv.at[0, r], kv.at[1, r]
    own_keys[...] = jnp.dot(normed, attn_w[:, ch:2 * ch], preferred_element_type=f32).astype(bf16)
    swap_keys = exchange(own_keys, own_keys, 0, mate)
    swap_keys.start()
    own_values[...] = jnp.dot(normed, attn_w[:, 2 * ch:3 * ch], preferred_element_type=f32).astype(bf16)
    swap_values = exchange(own_values, own_values, 3, mate)
    swap_values.start()
    queries = jnp.dot(normed, attn_w[:, :ch], preferred_element_type=f32).astype(bf16) * head_dim ** (-0.5)
    first_head = lax.broadcasted_iota(jnp.int32, (tokens, 2 * head_dim), 1) < head_dim
    none = jnp.zeros((tokens, 2 * head_dim), bf16)
    ones = jnp.ones((2 * (tokens + frames), 2 * head_dim), bf16)
    pairs = [slice(2 * h * head_dim, 2 * (h + 1) * head_dim) for h in range(heads // 2)]
    await_bytes(kv.at[0, 1 - r], misc_recv.at[0])
    weights = []
    for at in pairs:
        both = jnp.concatenate([
            jnp.where(first_head, queries[:, at], none), jnp.where(first_head, none, queries[:, at]),
        ], axis=0)
        keys = jnp.concatenate([kv[0, 0, :, at], kv[0, 1, :, at], picked_keys[:, at]], axis=0)
        scores = lax.dot_general(both, keys, (((1,), (1,)), ((), ())), preferred_element_type=f32)
        weights.append(jnp.exp(scores - jnp.max(scores, axis=-1, keepdims=True)).astype(bf16))
    await_bytes(kv.at[1, 1 - r], misc_recv.at[3])
    for at, probs in zip(pairs, weights):
        values = jnp.concatenate([kv[1, 0, :, at], kv[1, 1, :, at], picked_values[:, at]], axis=0)
        mixed = jnp.dot(probs, jnp.concatenate([values, ones], axis=1), preferred_element_type=f32)
        mixed = mixed[:, :2 * head_dim] / mixed[:, 2 * head_dim:]
        attended[:, at] = jnp.where(first_head, mixed[:tokens], mixed[tokens:]).astype(bf16)
    result = blended + jnp.dot(attended[...], attn_w[:, 3 * ch:], preferred_element_type=f32)
    out_ref[0] = result.astype(bf16).reshape(rows, columns, ch)

    for k in range(1, QUAD):
        act_copy(k).wait_send()
        sums[k].wait_send()
    for k in range(QUAD):
        edge(k).wait_send()
    await_bytes(conv_w.at[0, 0:4 * conv_quarter], conv_send.at[0])
    await_bytes(cache.at[r, 0:frames - 1], cache_send.at[0])
    cache_mate.wait_send()
    weights_sent(0)
    weights_sent(1)
    swap_keys.wait_send()
    swap_values.wait_send()

    @pl.when(frame < frames - 1)
    def _():
        later.wait_send()

    @pl.when(frame > 0)
    def _():
        earlier.wait_send()


def by_kernel(
    frame_count, frames_in, norm_gains, conv_weight, time_weight, attention_weight,
    reference_keys, reference_values, reference_pick,
):
    _, rows, columns, ch = frames_in.shape
    tokens = rows * columns
    images = reference_keys.shape[0]
    vmem = pl.BlockSpec(memory_space=pltpu.VMEM)
    hbm = pl.BlockSpec(memory_space=pl.ANY)
    dma = pltpu.SemaphoreType.DMA
    bf16 = jnp.bfloat16
    time_span = round_up(time_weight.shape[0], 64)
    conv_span = max(17 * ch // 8, 7 * ch // 8 + round_up(conv_weight.shape[0], 64 * CHUNKS))
    return pl.pallas_call(
        functools.partial(kernel, HEADS, images),
        out_shape=jax.ShapeDtypeStruct(frames_in.shape, bf16),
        in_specs=[hbm, vmem, hbm, hbm, pl.BlockSpec(memory_space=pltpu.SMEM), hbm, hbm, hbm],
        out_specs=vmem,
        scratch_shapes=[
            pltpu.VMEM((rows, columns, ch), bf16),
            pltpu.VMEM((2, conv_span, ch), bf16),
            pltpu.VMEM((frame_count * time_span, ch), bf16),
            pltpu.VMEM((frame_count * attention_weight.shape[0], 4 * ch), bf16),
            pltpu.VMEM((3, QUAD, tokens + 2 * columns, ch), bf16),
            pltpu.VMEM((QUAD, tokens, ch), jnp.float32),
            pltpu.VMEM((QUAD, tokens, ch), bf16),
            pltpu.VMEM((QUAD, tokens, ch), bf16),
            pltpu.VMEM((3, tokens, ch), bf16),
            pltpu.VMEM((2, 2, tokens, ch), bf16),
            pltpu.VMEM((2, frame_count, 2, images, ch), bf16),
            pltpu.VMEM((tokens, ch), bf16),
            dma((6,)),
            dma((QUAD,)),
            dma((QUAD,)),
            dma((QUAD,)),
            dma((QUAD,)),
            dma((1,)),
            dma((2 * CHUNKS + 1,)),
            dma((2, QUAD)),
            dma((2, QUAD)),
            dma((2, frame_count)),
            dma((2,)),
            dma((2,)),
            dma((QUAD,)),
            dma((QUAD,)),
            dma((4,)),
            dma((4,)),
            dma((2,)),
            dma((2,)),
        ],
        compiler_params=pltpu.CompilerParams(
            collective_id=0, has_side_effects=True, vmem_limit_bytes=60 * 2**20
        ),
    )(frames_in, norm_gains, reference_keys[:, 0], reference_values[:, 0], reference_pick, conv_weight, time_weight, attention_weight)


def on_device(sizes, *operands):
    frames_in, _, conv_weight, time_weight, attention_weight, keys, _, _ = operands
    count = sizes["frame"]
    rows, columns, channels = frames_in.shape[1:]
    share = channels // 8
    fits = (
        sizes["groups"] == 2 and sizes["row"] == 2 and count == 2 * QUAD
        and frames_in.shape[0] == 1 and rows == 2 and columns % 16 == 0 and keys.shape[1] == 1
        and channels == 64 * HEADS and HEADS % 2 == 0 and channels % 128 == 0 and conv_weight.shape[0] == 9 * share
        and time_weight.shape[0] == 3 * share and attention_weight.shape[0] == share
    )
    if fits:
        return by_kernel(count, *operands)
    return by_collectives(*operands)


def solution(mesh):
    return jax.shard_map(
        functools.partial(on_device, dict(mesh.shape)),
        mesh=mesh,
        in_specs=(
            P(("groups", "frame"), "row", None, None),
            P(),
            P("frame", None),
            P("frame", None),
            P("frame", None),
            P("groups", ("frame", "row"), None),
            P("groups", ("frame", "row"), None),
            P(("groups", "frame")),
        ),
        out_specs=P(("groups", "frame"), "row", None, None),
        check_vma=False,
    )
```

```python
import functools

import jax
import jax.numpy as jnp
from jax import lax
from jax.experimental import pallas as pl
from jax.experimental.pallas import tpu as pltpu
from jax.sharding import PartitionSpec as P

HEADS = 10
LANES = 2
QUAD = 4
CHUNKS = 3
MESH = pl.DeviceIdType.MESH


def padded_2(x, sides, width):
    for axis, dim in sides:
        devices, length = (lax.axis_size(axis), x.shape[dim])
        up = [(i, (i + 1) % devices) for i in range(devices - 1)]
        down = [(j, i) for i, j in up]
        last = lax.slice_in_dim(x, length - width, length, axis=dim)
        initial = lax.slice_in_dim(x, 0, width, axis=dim)
        before = lax.ppermute(last, axis, up)
        after = lax.ppermute(initial, axis, down)
        x = jnp.concatenate([before, x, after], axis=dim)
    return x


def normalize(values, gain):
    scale = lax.rsqrt(jnp.mean(values * values, axis=-1, keepdims=True) + 1e-05)
    return values * scale * gain


def heads_first(block, head_dim):
    split = block.reshape(block.shape[0], block.shape[1], HEADS, head_dim)
    return jnp.transpose(split, (2, 0, 1, 3))


def by_collectives(
    frames_in,
    norm_gains,
    conv_weight,
    time_weight,
    attention_weight,
    reference_keys,
    reference_values,
    reference_pick,
):
    local_frames, local_rows, columns, channels = frames_in.shape
    head_dim = channels // HEADS
    tokens = local_frames * local_rows * columns
    row_count = lax.axis_size("row")
    row_place = lax.axis_index("row")

    def halve(matrix):
        share = matrix.shape[1] // row_count
        return lax.dynamic_slice_in_dim(matrix, row_place * share, share, 1)

    conv_half, time_half, attention_half = (
        lax.all_gather(halve(conv_weight), "frame", axis=0, tiled=True),
        lax.all_gather(halve(time_weight), "frame", axis=0, tiled=True),
        lax.all_gather(halve(attention_weight), "frame", axis=0, tiled=True),
    )
    conv_full, time_full, attention_full = (
        lax.all_gather(conv_half, "row", axis=1, tiled=True),
        lax.all_gather(time_half, "row", axis=1, tiled=True),
        lax.all_gather(attention_half, "row", axis=1, tiled=True),
    )
    inputs = frames_in.astype(jnp.float32)
    activated = jax.nn.silu(normalize(inputs, norm_gains[0])).astype(jnp.bfloat16)
    padded = padded_2(activated, (("row", 1),), 1)
    padded = jnp.pad(padded, ((0, 0), (0, 0), (1, 1), (0, 0)))
    spatial = jnp.zeros((tokens, channels), jnp.float32)
    for offset_row in range(3):
        for offset_col in range(3):
            window = padded[
                :, offset_row : offset_row + local_rows, offset_col : offset_col + columns, :
            ].reshape(tokens, channels)
            row_start = (3 * offset_row + offset_col) * channels
            spatial = spatial + jnp.dot(
                window,
                conv_full[row_start : row_start + channels],
                preferred_element_type=jnp.float32,
            )
    hidden = (inputs + spatial.reshape(inputs.shape)).astype(jnp.bfloat16)
    hidden_wide = hidden.astype(jnp.float32)
    mixed = jax.nn.silu(normalize(hidden_wide, norm_gains[1])).astype(jnp.bfloat16)
    nearby = padded_2(mixed, (("frame", 0),), 1)
    temporal = jnp.zeros((tokens, channels), jnp.float32)
    for offset_frame in range(3):
        window = nearby[offset_frame : offset_frame + local_frames].reshape(tokens, channels)
        temporal = temporal + jnp.dot(
            window,
            time_full[offset_frame * channels : (offset_frame + 1) * channels],
            preferred_element_type=jnp.float32,
        )
    blended = (hidden_wide + temporal.reshape(inputs.shape)).astype(jnp.bfloat16)
    blended_wide = blended.astype(jnp.float32)
    normed = normalize(blended_wide, norm_gains[2]).astype(jnp.bfloat16).reshape(tokens, channels)
    projected = jnp.dot(
        normed, attention_full[:, : 3 * channels], preferred_element_type=jnp.float32
    ).astype(jnp.bfloat16)
    projected = projected.reshape(local_frames, local_rows * columns, 3 * channels)
    queries = projected[:, :, :channels]
    own_keys = projected[:, :, channels : 2 * channels]
    own_values = projected[:, :, 2 * channels :]
    frame_keys, frame_values = (
        lax.all_gather(own_keys, "row", axis=1, tiled=True),
        lax.all_gather(own_values, "row", axis=1, tiled=True),
    )
    cache_keys, cache_values = (
        lax.all_gather(reference_keys, ("frame", "row"), axis=1, tiled=True),
        lax.all_gather(reference_values, ("frame", "row"), axis=1, tiled=True),
    )
    picked_keys = jnp.take(cache_keys, reference_pick, axis=0)
    picked_values = jnp.take(cache_values, reference_pick, axis=0)
    keys_all = jnp.concatenate([frame_keys, picked_keys], axis=1)
    values_all = jnp.concatenate([frame_values, picked_values], axis=1)

    def one_head(operands):
        query_head, key_head, value_head = operands
        scores = jnp.einsum(
            "fqd,fkd->fqk", query_head, key_head, preferred_element_type=jnp.float32
        ) * head_dim ** (-0.5)
        ceiling = jnp.max(scores, axis=-1, keepdims=True)
        weights = jnp.exp(scores - ceiling)
        probs = (weights / jnp.sum(weights, axis=-1, keepdims=True)).astype(jnp.bfloat16)
        return jnp.einsum(
            "fqk,fkd->fqd", probs, value_head, preferred_element_type=jnp.float32
        ).astype(jnp.bfloat16)

    per_head = lax.map(
        one_head,
        (
            heads_first(queries, head_dim),
            heads_first(keys_all, head_dim),
            heads_first(values_all, head_dim),
        ),
    )
    attended = jnp.transpose(per_head, (1, 2, 0, 3)).reshape(tokens, channels)
    output = jnp.dot(
        attended, attention_full[:, 3 * channels :], preferred_element_type=jnp.float32
    )
    return (blended_wide + output.reshape(inputs.shape)).astype(jnp.bfloat16)


def round_up(value, unit):
    return -(-value // unit) * unit


def flip(frame, k):
    z, x = frame // LANES, frame % LANES
    kz, kx = k // LANES, k % LANES
    high = (z // 2 + kz // 2) % 2
    low = (z % 2 + kz % 2) % 2
    return (2 * high + low) * LANES + (x + kx) % 2


def kernel(
    heads, images,
    x_ref, gains_ref, keys_ref, values_ref, pick_ref, conv_ref, time_ref, attn_ref,
    out_ref,
    x_own, conv_w, time_w, attn_w, shifted, part, partial_out, partial_in, mix, given, kv, cache, attended,
    local_sem, act_send, act_recv, edge_send, edge_recv, conv_send, conv_recv,
    lane_recv, cross_recv, other_recv, mate_recv, weight_send,
    sum_send, sum_recv, misc_send, misc_recv, cache_send, cache_recv,
):
    y, frame, r = lax.axis_index("groups"), lax.axis_index("frame"), lax.axis_index("row")
    frames = 2 * QUAD
    _, rows, columns, ch = x_ref.shape
    tokens = rows * columns
    head_dim = ch // heads
    share = ch // 8
    conv_rows, time_rows, attn_rows = conv_ref.shape[0], time_ref.shape[0], attn_ref.shape[0]
    conv_quarter = round_up(conv_rows, 64 * CHUNKS) // 4
    conv_chunk = conv_quarter // CHUNKS
    time_quarter = round_up(time_rows, 64) // 4
    time_span = 4 * time_quarter
    f32, bf16 = jnp.float32, jnp.bfloat16
    own = frame % QUAD
    mine, theirs = 2 * y + r, 2 * (1 - y) + r
    mate = {"row": 1 - r}
    opposite = {"groups": 1 - y}

    def rows_at(start, size):
        return pl.ds(pl.multiple_of(start, 16), size)

    def at_frame(k):
        return {"frame": flip(frame, k)}

    def remote(src, dst, send_sem, recv_sem, to):
        return pltpu.make_async_remote_copy(
            src_ref=src, dst_ref=dst, send_sem=send_sem, recv_sem=recv_sem,
            device_id=to, device_id_type=MESH,
        )

    def await_bytes(ref, sem):
        pltpu.make_async_copy(ref, ref, sem).wait()

    def clear(slot, shard):
        for i in range(8):
            start = i * share + jnp.where(i < shard, 0, conv_rows)
            conv_w[slot, rows_at(start, share), :] = jnp.zeros((share, ch), bf16)

    opposite_shard = flip(frame, 4)
    clear(1, opposite_shard)
    partners = [at_frame(k) for k in range(1, frames)] + [mate, opposite]
    barrier = pltpu.get_barrier_semaphore()
    for to in partners:
        pl.semaphore_signal(barrier, inc=1, device_id=to, device_id_type=MESH)

    clear(0, frame)
    fills = [
        pltpu.make_async_copy(x_ref.at[0], x_own, local_sem.at[0]),
        pltpu.make_async_copy(conv_ref, conv_w.at[0, rows_at(frame * share, conv_rows)], local_sem.at[1]),
        pltpu.make_async_copy(time_ref, time_w.at[rows_at(frame * time_span, time_rows)], local_sem.at[2]),
        pltpu.make_async_copy(attn_ref, attn_w.at[rows_at(frame * attn_rows, attn_rows)], local_sem.at[3]),
        pltpu.make_async_copy(keys_ref, cache.at[r, frame, 0], local_sem.at[4]),
        pltpu.make_async_copy(values_ref, cache.at[r, frame, 1], local_sem.at[5]),
    ]
    for f in fills:
        f.start()
    if time_span > time_rows:
        gap = time_span - time_rows
        time_w[rows_at(frame * time_span + time_rows, gap), :] = jnp.zeros((gap, ch), bf16)
    shifted[1, :, rows_at(r * (rows + 1) * columns, columns), :] = jnp.zeros((QUAD, columns, ch), bf16)

    def act(v, g):
        n = normalize(v, gains_ref[g:g + 1, :])
        return n / (1.0 + jnp.exp(-n))

    fills[0].wait()
    own_x = x_own[...].reshape(tokens, ch).astype(f32)
    shifted[1, own, columns:columns + tokens, :] = act(own_x, 0).astype(bf16)
    pl.semaphore_wait(barrier, len(partners))

    def act_copy(k):
        ref = shifted.at[1, own if k < 3 else flip(own, 1), columns:columns + tokens]
        return remote(ref, ref, act_send.at[k], act_recv.at[k], at_frame(min(k, 2)))

    def edge(k):
        slot = flip(own, k)
        return remote(
            shifted.at[1, slot, rows_at(rows * columns - r * (rows - 1) * columns, columns)],
            shifted.at[1, slot, rows_at(r * (rows + 1) * columns, columns)],
            edge_send.at[k], edge_recv.at[k], mate,
        )

    def edge_wait(k):
        slot = flip(own, k)
        await_bytes(shifted.at[1, slot, rows_at((1 - r) * (rows + 1) * columns, columns)], edge_recv.at[k])

    def conv_part(slot, shard, q, i=0, count=1):
        start = shard * share + q * conv_quarter + i * conv_chunk
        return conv_w.at[slot, rows_at(start, count * conv_chunk)]

    def send_conv(slot, shard, q, i, recv, to):
        remote(
            conv_part(slot, shard, q, i), conv_part(1, shard, q, i),
            conv_send.at[0], conv_recv.at[recv], to,
        ).start()

    def conv_from_lane(i):
        await_bytes(conv_part(1, opposite_shard, mine, i), conv_recv.at[i])
        send_conv(1, opposite_shard, mine, i, CHUNKS + i, opposite)
        send_conv(1, opposite_shard, mine, i, 2 * CHUNKS, mate)

    def conv_from_other(i):
        await_bytes(conv_part(1, opposite_shard, theirs, i), conv_recv.at[CHUNKS + i])
        send_conv(1, opposite_shard, theirs, i, 2 * CHUNKS, mate)

    def conv_from_mate():
        await_bytes(conv_w.at[1, 0:2 * conv_quarter], conv_recv.at[2 * CHUNKS])

    def time_part(d, q, count=1):
        return time_w.at[rows_at(d * time_span + q * time_quarter, count * time_quarter)]

    def attn_part(d, q, count=1):
        return attn_w.at[rows_at(d * attn_rows, attn_rows), pl.ds(pl.multiple_of(q * ch, 128), count * ch)]

    def pieces(w):
        return time_part if w == 0 else attn_part

    def send_weight(w, ref, recv_sem, to):
        remote(ref, ref, weight_send.at[w], recv_sem, to).start()

    def weights_across():
        send_weight(1, attn_part(frame, 2 * r, 2), cross_recv.at[0], at_frame(1))

    def weights_along(w, k):
        send_weight(w, pieces(w)(frame, mine), lane_recv.at[w, k], at_frame(2 * k))

    def from_lane(w, k):
        ref = pieces(w)(flip(frame, 2 * k), mine)
        await_bytes(ref, lane_recv.at[w, k])
        if k == 3:
            send_weight(w, ref, lane_recv.at[w, 2], at_frame(2))
        if w == 1:
            send_weight(w, ref, cross_recv.at[k], at_frame(1))
        send_weight(w, ref, other_recv.at[w, 2 * k], opposite)
        send_weight(w, ref, mate_recv.at[w], mate)

    def from_cross(k):
        ref = attn_part(flip(frame, 1), 2 * r, 2) if k == 0 else attn_part(flip(frame, 2 * k + 1), mine)
        await_bytes(ref, cross_recv.at[k])
        if k > 0:
            send_weight(1, ref, other_recv.at[1, 2 * k + 1], opposite)
        send_weight(1, ref, mate_recv.at[1], mate)

    def from_other(w, k):
        ref = pieces(w)(flip(frame, k), theirs)
        await_bytes(ref, other_recv.at[w, k])
        send_weight(w, ref, mate_recv.at[w], mate)

    def weight_bytes(w, quarters):
        if w == 0:
            return time_w.at[0:quarters * time_quarter]
        return attn_w.at[0:quarters * attn_rows // 2, 0:2 * ch]

    def from_mate(w):
        await_bytes(weight_bytes(w, (6, 14)[w]), mate_recv.at[w])

    def weights_sent(w):
        if w == 0:
            await_bytes(time_w.at[0:12 * time_quarter], weight_send.at[w])
        else:
            await_bytes(attn_w.at[0:7 * attn_rows], weight_send.at[w])

    def exchange(src, dst, k, to):
        return remote(src, dst, misc_send.at[k], misc_recv.at[k], to)

    def share_refs(k):
        return remote(cache.at[r, frame], cache.at[r, frame], cache_send.at[0], cache_recv.at[0], at_frame(k))

    act_copy(1).start()
    act_copy(2).start()
    edge(0).start()
    fills[1].wait()
    for i in range(CHUNKS):
        send_conv(0, frame, mine, i, i, at_frame(4))
    fills[2].wait()
    fills[3].wait()
    fills[4].wait()
    fills[5].wait()
    for k in range(1, frames):
        share_refs(k).start()

    def from_quad(k):
        slot = flip(own, k)
        await_bytes(shifted.at[1, slot, columns:columns + tokens], act_recv.at[k])
        if k == 1:
            act_copy(3).start()
        edge(k).start()

    for k in range(1, frames, 2):
        time_w[rows_at(flip(frame, k) * time_span, time_span), :] = jnp.zeros((time_span, ch), bf16)

    from_quad(1)
    weights_across()
    from_quad(2)
    conv_from_lane(0)
    conv_from_lane(1)
    from_quad(3)
    weights_along(0, 3)
    weights_along(0, 1)
    conv_from_lane(2)
    weights_along(1, 3)
    weights_along(1, 1)
    conv_from_other(0)

    blank = jnp.zeros((1, ch), f32)

    def shift(k):
        slot = flip(own, k)
        edge_wait(k)
        for i in range(rows + 2):
            span = slice(i * columns, (i + 1) * columns)
            row = shifted[1, slot, span, :].astype(f32)
            shifted[0, slot, span, :] = jnp.concatenate([blank, row[:columns - 1]], axis=0).astype(bf16)
            shifted[2, slot, span, :] = jnp.concatenate([row[1:], blank], axis=0).astype(bf16)

    for k in range(QUAD):
        shift(k)

    def windows(shard, j, slot=None):
        tap = shard + j
        dy, dx = tap // 3, tap % 3
        if slot is None:
            return shifted[dx, :, rows_at(dy * columns, tokens), :].reshape(QUAD * tokens, ch)
        return shifted[dx, slot, rows_at(dy * columns, tokens), :]

    def partial_sum(slot, shard, j, place=None):
        return jnp.dot(windows(shard, j, place), conv_w[slot, j * ch:(j + 1) * ch, :], preferred_element_type=f32)

    part[...] = (partial_sum(0, frame, 0) + partial_sum(0, frame, 1)).reshape(QUAD, tokens, ch)

    for i in range(1, CHUNKS):
        conv_from_other(i)
    from_lane(0, 3)
    from_lane(0, 1)
    conv_from_mate()
    sums = {}
    total = part[...] + (
        partial_sum(1, opposite_shard, 0) + partial_sum(1, opposite_shard, 1)
    ).reshape(QUAD, tokens, ch)
    part[...] = total
    partial_out[...] = total.astype(bf16)
    for k in range(1, QUAD):
        sums[k] = remote(partial_out.at[flip(own, k)], partial_in.at[own], sum_send.at[k], sum_recv.at[k], at_frame(k))
        sums[k].start()

    from_cross(0)
    from_lane(0, 2)
    from_lane(1, 3)
    from_lane(1, 1)
    from_other(0, 6)
    from_other(0, 2)

    total = own_x + part[own]
    for k in range(1, QUAD):
        slot = flip(own, k)
        await_bytes(partial_in.at[slot], sum_recv.at[k])
        total = total + partial_in[slot].astype(f32)
    hidden = total.astype(bf16).astype(f32)
    z, x = frame // LANES, frame % LANES
    depth = frames // LANES
    mix[1 + x] = act(hidden, 1).astype(bf16)

    gives = jnp.where(x == 0, z > 0, z < depth - 1)
    takes = jnp.where(x == 0, z < depth - 1, z > 0)
    far = mix.at[3 * (1 - x)]
    beside = exchange(mix.at[1 + x], mix.at[1 + x], 1, at_frame(1))
    beyond = exchange(mix.at[1 + x], far, 2, {"frame": jnp.clip(frame + 4 * x - 2, 0, frames - 1)})
    relay = exchange(far, far, 4, at_frame(1))

    @pl.when(gives)
    def _():
        beyond.start()

    beside.start()

    @pl.when(z == 0)
    def _():
        mix[0] = jnp.zeros((tokens, ch), bf16)

    @pl.when(z == depth - 1)
    def _():
        mix[3] = jnp.zeros((tokens, ch), bf16)

    from_lane(1, 2)
    from_other(0, 4)
    from_cross(3)

    @pl.when(takes)
    def _():
        beyond.wait_recv()
        relay.start()

    from_cross(1)
    from_other(1, 6)
    await_bytes(cache.at[r, 0:frames - 1], cache_recv.at[0])
    cache_mate = remote(cache.at[r], cache.at[r], cache_send.at[1], cache_recv.at[1], mate)
    cache_mate.start()
    from_mate(0)

    def time_rows_of(t):
        found = []
        at, left = t * ch, ch
        while left:
            shard, inside = at // time_rows, at % time_rows
            count = min(time_rows - inside, left)
            found.append(time_w[shard * time_span + inside:shard * time_span + inside + count, :])
            at, left = at + count, left - count
        return jnp.concatenate(found, axis=0)

    def temporal(lane):
        total = jnp.dot(mix[lane + 1], time_rows_of(1), preferred_element_type=f32)
        total = total + jnp.dot(mix[lane], time_rows_of(0), preferred_element_type=f32)
        return total + jnp.dot(mix[lane + 2], time_rows_of(2), preferred_element_type=f32)

    await_bytes(mix.at[2 - x], misc_recv.at[1])
    given[0] = temporal(1 - x).astype(bf16)
    temporal_swap = exchange(given.at[0], given.at[1], 5, at_frame(1))
    temporal_swap.start()
    await_bytes(cache.at[1 - r], cache_recv.at[1])
    pick = pick_ref[0]
    cached = cache[...].astype(f32).reshape(2 * frames, 2, images, ch)
    picked_keys = jnp.zeros((2 * frames, ch), f32)
    picked_values = jnp.zeros((2 * frames, ch), f32)
    for i in range(images):
        picked_keys = jnp.where(pick == i, cached[:, 0, i, :], picked_keys)
        picked_values = jnp.where(pick == i, cached[:, 1, i, :], picked_values)
    picked_keys, picked_values = picked_keys.astype(bf16), picked_values.astype(bf16)
    from_other(1, 2)
    from_cross(2)
    from_other(1, 7)

    @pl.when(gives)
    def _():
        await_bytes(mix.at[3 * x], misc_recv.at[4])

    own_temporal = temporal(x)
    for k in (3, 4, 5):
        from_other(1, k)
    temporal_swap.wait_recv()
    total = hidden + own_temporal + given[1].astype(f32)
    blended = total.astype(bf16).astype(f32)
    normed = normalize(blended, gains_ref[2:3, :]).astype(bf16)
    from_mate(1)
    own_keys, own_values = kv.at[0, r], kv.at[1, r]
    own_keys[...] = jnp.dot(normed, attn_w[:, ch:2 * ch], preferred_element_type=f32).astype(bf16)
    swap_keys = exchange(own_keys, own_keys, 0, mate)
    swap_keys.start()
    own_values[...] = jnp.dot(normed, attn_w[:, 2 * ch:3 * ch], preferred_element_type=f32).astype(bf16)
    swap_values = exchange(own_values, own_values, 3, mate)
    swap_values.start()
    queries = jnp.dot(normed, attn_w[:, :ch], preferred_element_type=f32).astype(bf16) * head_dim ** (-0.5)
    first_head = lax.broadcasted_iota(jnp.int32, (tokens, 2 * head_dim), 1) < head_dim
    none = jnp.zeros((tokens, 2 * head_dim), bf16)
    ones = jnp.ones((2 * (tokens + frames), 2 * head_dim), bf16)
    pairs = [slice(2 * h * head_dim, 2 * (h + 1) * head_dim) for h in range(heads // 2)]
    await_bytes(kv.at[0, 1 - r], misc_recv.at[0])
    weights = []
    for at in pairs:
        both = jnp.concatenate([
            jnp.where(first_head, queries[:, at], none), jnp.where(first_head, none, queries[:, at]),
        ], axis=0)
        keys = jnp.concatenate([kv[0, 0, :, at], kv[0, 1, :, at], picked_keys[:, at]], axis=0)
        scores = lax.dot_general(both, keys, (((1,), (1,)), ((), ())), preferred_element_type=f32)
        weights.append(jnp.exp(scores - jnp.max(scores, axis=-1, keepdims=True)).astype(bf16))
    await_bytes(kv.at[1, 1 - r], misc_recv.at[3])
    for at, probs in zip(pairs, weights):
        values = jnp.concatenate([kv[1, 0, :, at], kv[1, 1, :, at], picked_values[:, at]], axis=0)
        mixed = jnp.dot(probs, jnp.concatenate([values, ones], axis=1), preferred_element_type=f32)
        mixed = mixed[:, :2 * head_dim] / mixed[:, 2 * head_dim:]
        attended[:, at] = jnp.where(first_head, mixed[:tokens], mixed[tokens:]).astype(bf16)
    result = blended + jnp.dot(attended[...], attn_w[:, 3 * ch:], preferred_element_type=f32)
    out_ref[0] = result.astype(bf16).reshape(rows, columns, ch)

    for k in range(1, QUAD):
        act_copy(k).wait_send()
        sums[k].wait_send()
    for k in range(QUAD):
        edge(k).wait_send()
    await_bytes(conv_w.at[0, 0:4 * conv_quarter], conv_send.at[0])
    await_bytes(cache.at[r, 0:frames - 1], cache_send.at[0])
    cache_mate.wait_send()
    weights_sent(0)
    weights_sent(1)
    swap_keys.wait_send()
    swap_values.wait_send()

    beside.wait_send()
    temporal_swap.wait_send()

    @pl.when(gives)
    def _():
        beyond.wait_send()

    @pl.when(takes)
    def _():
        relay.wait_send()


def by_kernel(
    frame_count, frames_in, norm_gains, conv_weight, time_weight, attention_weight,
    reference_keys, reference_values, reference_pick,
):
    _, rows, columns, ch = frames_in.shape
    tokens = rows * columns
    images = reference_keys.shape[0]
    vmem = pl.BlockSpec(memory_space=pltpu.VMEM)
    hbm = pl.BlockSpec(memory_space=pl.ANY)
    dma = pltpu.SemaphoreType.DMA
    bf16 = jnp.bfloat16
    time_span = round_up(time_weight.shape[0], 64)
    conv_span = max(17 * ch // 8, 7 * ch // 8 + round_up(conv_weight.shape[0], 64 * CHUNKS))
    return pl.pallas_call(
        functools.partial(kernel, HEADS, images),
        out_shape=jax.ShapeDtypeStruct(frames_in.shape, bf16),
        in_specs=[hbm, vmem, hbm, hbm, pl.BlockSpec(memory_space=pltpu.SMEM), hbm, hbm, hbm],
        out_specs=vmem,
        scratch_shapes=[
            pltpu.VMEM((rows, columns, ch), bf16),
            pltpu.VMEM((2, conv_span, ch), bf16),
            pltpu.VMEM((frame_count * time_span, ch), bf16),
            pltpu.VMEM((frame_count * attention_weight.shape[0], 4 * ch), bf16),
            pltpu.VMEM((3, QUAD, tokens + 2 * columns, ch), bf16),
            pltpu.VMEM((QUAD, tokens, ch), jnp.float32),
            pltpu.VMEM((QUAD, tokens, ch), bf16),
            pltpu.VMEM((QUAD, tokens, ch), bf16),
            pltpu.VMEM((LANES + 2, tokens, ch), bf16),
            pltpu.VMEM((2, tokens, ch), bf16),
            pltpu.VMEM((2, 2, tokens, ch), bf16),
            pltpu.VMEM((2, frame_count, 2, images, ch), bf16),
            pltpu.VMEM((tokens, ch), bf16),
            dma((6,)),
            dma((QUAD,)),
            dma((QUAD,)),
            dma((QUAD,)),
            dma((QUAD,)),
            dma((1,)),
            dma((2 * CHUNKS + 1,)),
            dma((2, QUAD)),
            dma((QUAD,)),
            dma((2, frame_count)),
            dma((2,)),
            dma((2,)),
            dma((QUAD,)),
            dma((QUAD,)),
            dma((6,)),
            dma((6,)),
            dma((2,)),
            dma((2,)),
        ],
        compiler_params=pltpu.CompilerParams(
            collective_id=0, has_side_effects=True, vmem_limit_bytes=60 * 2**20
        ),
    )(frames_in, norm_gains, reference_keys[:, 0], reference_values[:, 0], reference_pick, conv_weight, time_weight, attention_weight)


def on_device(sizes, *operands):
    frames_in, _, conv_weight, time_weight, attention_weight, keys, _, _ = operands
    count = sizes["frame"]
    rows, columns, channels = frames_in.shape[1:]
    share = channels // 8
    fits = (
        sizes["groups"] == 2 and sizes["row"] == 2 and count == 2 * QUAD
        and frames_in.shape[0] == 1 and rows == 2 and columns % 16 == 0 and keys.shape[1] == 1
        and channels == 64 * HEADS and HEADS % 2 == 0 and channels % 128 == 0 and conv_weight.shape[0] == 9 * share
        and time_weight.shape[0] == 3 * share and attention_weight.shape[0] == share
    )
    if fits:
        return by_kernel(count, *operands)
    return by_collectives(*operands)


def solution(mesh):
    return jax.shard_map(
        functools.partial(on_device, dict(mesh.shape)),
        mesh=mesh,
        in_specs=(
            P(("groups", "frame"), "row", None, None),
            P(),
            P("frame", None),
            P("frame", None),
            P("frame", None),
            P("groups", ("frame", "row"), None),
            P("groups", ("frame", "row"), None),
            P(("groups", "frame")),
        ),
        out_specs=P(("groups", "frame"), "row", None, None),
        check_vma=False,
    )
```

```python
import functools

import jax
import jax.numpy as jnp
from jax import lax
from jax.experimental import pallas as pl
from jax.experimental.pallas import tpu as pltpu
from jax.sharding import PartitionSpec as P

HEADS = 10
LANES = 2
QUAD = 4
CHUNKS = 3
MESH = pl.DeviceIdType.MESH


def padded_2(x, sides, width):
    for axis, dim in sides:
        devices, length = (lax.axis_size(axis), x.shape[dim])
        up = [(i, (i + 1) % devices) for i in range(devices - 1)]
        down = [(j, i) for i, j in up]
        last = lax.slice_in_dim(x, length - width, length, axis=dim)
        initial = lax.slice_in_dim(x, 0, width, axis=dim)
        before = lax.ppermute(last, axis, up)
        after = lax.ppermute(initial, axis, down)
        x = jnp.concatenate([before, x, after], axis=dim)
    return x


def normalize(values, gain):
    scale = lax.rsqrt(jnp.mean(values * values, axis=-1, keepdims=True) + 1e-05)
    return values * scale * gain


def heads_first(block, head_dim):
    split = block.reshape(block.shape[0], block.shape[1], HEADS, head_dim)
    return jnp.transpose(split, (2, 0, 1, 3))


def by_collectives(
    frames_in,
    norm_gains,
    conv_weight,
    time_weight,
    attention_weight,
    reference_keys,
    reference_values,
    reference_pick,
):
    local_frames, local_rows, columns, channels = frames_in.shape
    head_dim = channels // HEADS
    tokens = local_frames * local_rows * columns
    row_count = lax.axis_size("row")
    row_place = lax.axis_index("row")

    def halve(matrix):
        share = matrix.shape[1] // row_count
        return lax.dynamic_slice_in_dim(matrix, row_place * share, share, 1)

    conv_half, time_half, attention_half = (
        lax.all_gather(halve(conv_weight), "frame", axis=0, tiled=True),
        lax.all_gather(halve(time_weight), "frame", axis=0, tiled=True),
        lax.all_gather(halve(attention_weight), "frame", axis=0, tiled=True),
    )
    conv_full, time_full, attention_full = (
        lax.all_gather(conv_half, "row", axis=1, tiled=True),
        lax.all_gather(time_half, "row", axis=1, tiled=True),
        lax.all_gather(attention_half, "row", axis=1, tiled=True),
    )
    inputs = frames_in.astype(jnp.float32)
    activated = jax.nn.silu(normalize(inputs, norm_gains[0])).astype(jnp.bfloat16)
    padded = padded_2(activated, (("row", 1),), 1)
    padded = jnp.pad(padded, ((0, 0), (0, 0), (1, 1), (0, 0)))
    spatial = jnp.zeros((tokens, channels), jnp.float32)
    for offset_row in range(3):
        for offset_col in range(3):
            window = padded[
                :, offset_row : offset_row + local_rows, offset_col : offset_col + columns, :
            ].reshape(tokens, channels)
            row_start = (3 * offset_row + offset_col) * channels
            spatial = spatial + jnp.dot(
                window,
                conv_full[row_start : row_start + channels],
                preferred_element_type=jnp.float32,
            )
    hidden = (inputs + spatial.reshape(inputs.shape)).astype(jnp.bfloat16)
    hidden_wide = hidden.astype(jnp.float32)
    mixed = jax.nn.silu(normalize(hidden_wide, norm_gains[1])).astype(jnp.bfloat16)
    nearby = padded_2(mixed, (("frame", 0),), 1)
    temporal = jnp.zeros((tokens, channels), jnp.float32)
    for offset_frame in range(3):
        window = nearby[offset_frame : offset_frame + local_frames].reshape(tokens, channels)
        temporal = temporal + jnp.dot(
            window,
            time_full[offset_frame * channels : (offset_frame + 1) * channels],
            preferred_element_type=jnp.float32,
        )
    blended = (hidden_wide + temporal.reshape(inputs.shape)).astype(jnp.bfloat16)
    blended_wide = blended.astype(jnp.float32)
    normed = normalize(blended_wide, norm_gains[2]).astype(jnp.bfloat16).reshape(tokens, channels)
    projected = jnp.dot(
        normed, attention_full[:, : 3 * channels], preferred_element_type=jnp.float32
    ).astype(jnp.bfloat16)
    projected = projected.reshape(local_frames, local_rows * columns, 3 * channels)
    queries = projected[:, :, :channels]
    own_keys = projected[:, :, channels : 2 * channels]
    own_values = projected[:, :, 2 * channels :]
    frame_keys, frame_values = (
        lax.all_gather(own_keys, "row", axis=1, tiled=True),
        lax.all_gather(own_values, "row", axis=1, tiled=True),
    )
    cache_keys, cache_values = (
        lax.all_gather(reference_keys, ("frame", "row"), axis=1, tiled=True),
        lax.all_gather(reference_values, ("frame", "row"), axis=1, tiled=True),
    )
    picked_keys = jnp.take(cache_keys, reference_pick, axis=0)
    picked_values = jnp.take(cache_values, reference_pick, axis=0)
    keys_all = jnp.concatenate([frame_keys, picked_keys], axis=1)
    values_all = jnp.concatenate([frame_values, picked_values], axis=1)

    def one_head(operands):
        query_head, key_head, value_head = operands
        scores = jnp.einsum(
            "fqd,fkd->fqk", query_head, key_head, preferred_element_type=jnp.float32
        ) * head_dim ** (-0.5)
        ceiling = jnp.max(scores, axis=-1, keepdims=True)
        weights = jnp.exp(scores - ceiling)
        probs = (weights / jnp.sum(weights, axis=-1, keepdims=True)).astype(jnp.bfloat16)
        return jnp.einsum(
            "fqk,fkd->fqd", probs, value_head, preferred_element_type=jnp.float32
        ).astype(jnp.bfloat16)

    per_head = lax.map(
        one_head,
        (
            heads_first(queries, head_dim),
            heads_first(keys_all, head_dim),
            heads_first(values_all, head_dim),
        ),
    )
    attended = jnp.transpose(per_head, (1, 2, 0, 3)).reshape(tokens, channels)
    output = jnp.dot(
        attended, attention_full[:, 3 * channels :], preferred_element_type=jnp.float32
    )
    return (blended_wide + output.reshape(inputs.shape)).astype(jnp.bfloat16)


def round_up(value, unit):
    return -(-value // unit) * unit


def flip(frame, k):
    z, x = frame // LANES, frame % LANES
    kz, kx = k // LANES, k % LANES
    high = (z // 2 + kz // 2) % 2
    low = (z % 2 + kz % 2) % 2
    return (2 * high + low) * LANES + (x + kx) % 2


def kernel(
    heads, images,
    x_ref, gains_hbm, keys_ref, values_ref, pick_ref, conv_ref, time_ref, attn_ref,
    out_ref,
    x_own, gains_ref, conv_w, time_w, attn_w, shifted, part, partial_out, partial_in, mix, given, kv, cache, attended,
    local_sem, act_send, act_recv, edge_send, edge_recv, conv_send, conv_recv,
    lane_recv, cross_recv, other_recv, mate_recv, weight_send,
    sum_send, sum_recv, misc_send, misc_recv, cache_send, cache_recv,
):
    y, frame, r = lax.axis_index("groups"), lax.axis_index("frame"), lax.axis_index("row")
    frames = 2 * QUAD
    _, rows, columns, ch = x_ref.shape
    tokens = rows * columns
    head_dim = ch // heads
    share = ch // 8
    conv_rows, time_rows, attn_rows = conv_ref.shape[0], time_ref.shape[0], attn_ref.shape[0]
    conv_quarter = round_up(conv_rows, 64) // 4
    conv_first = conv_quarter // 2 // 16 * 16
    conv_last = max(conv_quarter // 6 // 16 * 16, 16)
    conv_chunks = (
        (0, conv_first), (conv_first, conv_quarter - conv_first - conv_last),
        (conv_quarter - conv_last, conv_last),
    )
    time_quarter = round_up(time_rows, 64) // 4
    time_span = 4 * time_quarter
    f32, bf16 = jnp.float32, jnp.bfloat16
    own = frame % QUAD
    mine, theirs = 2 * y + r, 2 * (1 - y) + r
    mate = {"row": 1 - r}
    opposite = {"groups": 1 - y}

    def rows_at(start, size):
        return pl.ds(pl.multiple_of(start, 16), size)

    def at_frame(k):
        return {"frame": flip(frame, k)}

    def remote(src, dst, send_sem, recv_sem, to):
        return pltpu.make_async_remote_copy(
            src_ref=src, dst_ref=dst, send_sem=send_sem, recv_sem=recv_sem,
            device_id=to, device_id_type=MESH,
        )

    def await_bytes(ref, sem):
        pltpu.make_async_copy(ref, ref, sem).wait()

    def clear(slot, shard, covered, blocks):
        for i in range(blocks):
            start = i * share + jnp.where(i < shard, 0, covered)
            conv_w[slot, rows_at(start, share), :] = jnp.zeros((share, ch), bf16)

    early = [
        pltpu.make_async_copy(x_ref.at[0], x_own, local_sem.at[0]),
        pltpu.make_async_copy(gains_hbm, gains_ref, local_sem.at[6]),
    ]
    for f in early:
        f.start()
    partners = [at_frame(k) for k in range(1, frames)] + [mate, opposite]
    barrier = pltpu.get_barrier_semaphore()
    for to in partners:
        pl.semaphore_signal(barrier, inc=1, device_id=to, device_id_type=MESH)

    opposite_shard = flip(frame, 4)
    clear(0, frame, conv_rows, 8)
    fills = [
        pltpu.make_async_copy(conv_ref, conv_w.at[0, rows_at(frame * share, conv_rows)], local_sem.at[1]),
        pltpu.make_async_copy(time_ref, time_w.at[rows_at(frame * time_span, time_rows)], local_sem.at[2]),
        pltpu.make_async_copy(attn_ref, attn_w.at[rows_at(frame * attn_rows, attn_rows)], local_sem.at[3]),
        pltpu.make_async_copy(keys_ref, cache.at[r, frame, 0], local_sem.at[4]),
        pltpu.make_async_copy(values_ref, cache.at[r, frame, 1], local_sem.at[5]),
    ]
    for f in fills:
        f.start()
    clear(1, opposite_shard, 4 * conv_quarter, 7)
    if time_span > time_rows:
        gap = time_span - time_rows
        time_w[rows_at(frame * time_span + time_rows, gap), :] = jnp.zeros((gap, ch), bf16)
    shifted[1, :, rows_at(r * (rows + 1) * columns, columns), :] = jnp.zeros((QUAD, columns, ch), bf16)

    def act(v, g):
        n = normalize(v, gains_ref[g:g + 1, :])
        return n / (1.0 + jnp.exp(-n))

    for f in early:
        f.wait()
    own_x = x_own[...].reshape(tokens, ch).astype(f32)
    shifted[1, own, columns:columns + tokens, :] = act(own_x, 0).astype(bf16)
    pl.semaphore_wait(barrier, len(partners))

    def act_copy(k):
        ref = shifted.at[1, own if k < 3 else flip(own, 1), columns:columns + tokens]
        return remote(ref, ref, act_send.at[k], act_recv.at[k], at_frame(min(k, 2)))

    def edge(k):
        slot = flip(own, k)
        return remote(
            shifted.at[1, slot, rows_at(rows * columns - r * (rows - 1) * columns, columns)],
            shifted.at[1, slot, rows_at(r * (rows + 1) * columns, columns)],
            edge_send.at[k], edge_recv.at[k], mate,
        )

    def edge_wait(k):
        slot = flip(own, k)
        await_bytes(shifted.at[1, slot, rows_at((1 - r) * (rows + 1) * columns, columns)], edge_recv.at[k])

    def conv_part(slot, shard, q, i):
        first, count = conv_chunks[i]
        return conv_w.at[slot, rows_at(shard * share + q * conv_quarter + first, count)]

    def send_conv(slot, shard, q, i, recv, to):
        remote(
            conv_part(slot, shard, q, i), conv_part(1, shard, q, i),
            conv_send.at[0], conv_recv.at[recv], to,
        ).start()

    def conv_from_lane(i):
        await_bytes(conv_part(1, opposite_shard, mine, i), conv_recv.at[i])
        send_conv(1, opposite_shard, mine, i, CHUNKS + i, opposite)
        send_conv(1, opposite_shard, mine, i, 2 * CHUNKS, mate)

    def conv_from_other(i):
        await_bytes(conv_part(1, opposite_shard, theirs, i), conv_recv.at[CHUNKS + i])
        send_conv(1, opposite_shard, theirs, i, 2 * CHUNKS, mate)

    def conv_from_mate():
        await_bytes(conv_w.at[1, 0:2 * conv_quarter], conv_recv.at[2 * CHUNKS])

    def time_part(d, q, count=1):
        return time_w.at[rows_at(d * time_span + q * time_quarter, count * time_quarter)]

    def attn_part(d, q, count=1):
        return attn_w.at[rows_at(d * attn_rows, attn_rows), pl.ds(pl.multiple_of(q * ch, 128), count * ch)]

    def pieces(w):
        return time_part if w == 0 else attn_part

    def send_weight(w, ref, recv_sem, to):
        remote(ref, ref, weight_send.at[w], recv_sem, to).start()

    def weights_across():
        send_weight(1, attn_part(frame, 2 * r, 2), cross_recv.at[0], at_frame(1))

    def weights_along(w, k):
        send_weight(w, pieces(w)(frame, mine), lane_recv.at[w, k], at_frame(2 * k))

    def from_lane(w, k):
        ref = pieces(w)(flip(frame, 2 * k), mine)
        await_bytes(ref, lane_recv.at[w, k])
        if w == 1:
            send_weight(w, ref, cross_recv.at[k], at_frame(1))
        send_weight(w, ref, other_recv.at[w, 2 * k], opposite)
        send_weight(w, ref, mate_recv.at[w], mate)

    def relay_lane(w):
        send_weight(w, pieces(w)(flip(frame, 6), mine), lane_recv.at[w, 2], at_frame(2))

    def from_cross(k):
        ref = attn_part(flip(frame, 1), 2 * r, 2) if k == 0 else attn_part(flip(frame, 2 * k + 1), mine)
        await_bytes(ref, cross_recv.at[k])
        if k > 0:
            send_weight(1, ref, other_recv.at[1, 2 * k + 1], opposite)
        send_weight(1, ref, mate_recv.at[1], mate)

    def from_other(w, k):
        ref = pieces(w)(flip(frame, k), theirs)
        await_bytes(ref, other_recv.at[w, k])
        send_weight(w, ref, mate_recv.at[w], mate)

    def weight_bytes(w, quarters):
        if w == 0:
            return time_w.at[0:quarters * time_quarter]
        return attn_w.at[0:quarters * attn_rows // 2, 0:2 * ch]

    def from_mate(w):
        await_bytes(weight_bytes(w, (6, 14)[w]), mate_recv.at[w])

    def weights_sent(w):
        if w == 0:
            await_bytes(time_w.at[0:12 * time_quarter], weight_send.at[w])
        else:
            await_bytes(attn_w.at[0:7 * attn_rows], weight_send.at[w])

    def exchange(src, dst, k, to):
        return remote(src, dst, misc_send.at[k], misc_recv.at[k], to)

    def share_refs(k):
        return remote(cache.at[r, frame], cache.at[r, frame], cache_send.at[0], cache_recv.at[0], at_frame(k))

    act_copy(1).start()
    act_copy(2).start()
    edge(0).start()
    fills[0].wait()
    for i in range(CHUNKS):
        send_conv(0, frame, mine, i, i, at_frame(4))
    for f in fills[1:]:
        f.wait()
    for k in range(1, frames):
        share_refs(k).start()

    def from_quad(k):
        slot = flip(own, k)
        await_bytes(shifted.at[1, slot, columns:columns + tokens], act_recv.at[k])
        if k == 1:
            act_copy(3).start()
        edge(k).start()

    for k in range(1, frames, 2):
        time_w[rows_at(flip(frame, k) * time_span, time_span), :] = jnp.zeros((time_span, ch), bf16)

    from_quad(1)
    weights_across()
    from_quad(2)
    conv_from_lane(0)
    conv_from_lane(1)
    from_quad(3)
    weights_along(0, 3)
    weights_along(1, 3)
    weights_along(1, 1)
    weights_along(0, 1)
    conv_from_lane(2)
    conv_from_other(0)

    blank = jnp.zeros((1, ch), f32)

    def shift(k):
        slot = flip(own, k)
        edge_wait(k)
        for i in range(rows + 2):
            span = slice(i * columns, (i + 1) * columns)
            row = shifted[1, slot, span, :].astype(f32)
            shifted[0, slot, span, :] = jnp.concatenate([blank, row[:columns - 1]], axis=0).astype(bf16)
            shifted[2, slot, span, :] = jnp.concatenate([row[1:], blank], axis=0).astype(bf16)

    for k in range(QUAD):
        shift(k)

    def windows(shard, j, slot=None):
        tap = shard + j
        dy, dx = tap // 3, tap % 3
        if slot is None:
            return shifted[dx, :, rows_at(dy * columns, tokens), :].reshape(QUAD * tokens, ch)
        return shifted[dx, pl.ds(slot, LANES), rows_at(dy * columns, tokens), :].reshape(LANES * tokens, ch)

    def partial_sum(slot, shard, j, place=None):
        return jnp.dot(windows(shard, j, place), conv_w[slot, j * ch:(j + 1) * ch, :], preferred_element_type=f32)

    part[...] = (partial_sum(0, frame, 0) + partial_sum(0, frame, 1)).reshape(QUAD, tokens, ch)

    for i in range(1, CHUNKS):
        conv_from_other(i)
    conv_from_mate()
    sums = {}
    for near in (1, 0):
        pair = flip(own, 2 * near) // LANES * LANES
        total = part[pl.ds(pair, LANES)] + (
            partial_sum(1, opposite_shard, 0, pair) + partial_sum(1, opposite_shard, 1, pair)
        ).reshape(LANES, tokens, ch)
        partial_out[pl.ds(pair, LANES)] = total.astype(bf16)
        if near == 0:
            part[pl.ds(pair, LANES)] = total
        for k in (2 * near + 1, 2 * near):
            if k:
                slot = flip(own, k)
                sums[k] = remote(partial_out.at[slot], partial_in.at[own], sum_send.at[k], sum_recv.at[k], at_frame(k))
                sums[k].start()

    from_lane(0, 3)
    relay_lane(0)
    from_lane(1, 3)
    relay_lane(1)
    from_lane(1, 1)
    from_lane(0, 1)
    from_cross(0)

    total = own_x + part[own]
    for k in range(1, QUAD):
        slot = flip(own, k)
        await_bytes(partial_in.at[slot], sum_recv.at[k])
        total = total + partial_in[slot].astype(f32)
    hidden = total.astype(bf16).astype(f32)
    z, x = frame // LANES, frame % LANES
    depth = frames // LANES
    mix[1 + x] = act(hidden, 1).astype(bf16)

    gives = jnp.where(x == 0, z > 0, z < depth - 1)
    takes = jnp.where(x == 0, z < depth - 1, z > 0)
    far = mix.at[3 * (1 - x)]
    beside = exchange(mix.at[1 + x], mix.at[1 + x], 1, at_frame(1))
    beyond = exchange(mix.at[1 + x], far, 2, {"frame": jnp.clip(frame + 4 * x - 2, 0, frames - 1)})
    relay = exchange(far, far, 4, at_frame(1))

    @pl.when(gives)
    def _():
        beyond.start()

    beside.start()

    @pl.when(z == 0)
    def _():
        mix[0] = jnp.zeros((tokens, ch), bf16)

    @pl.when(z == depth - 1)
    def _():
        mix[3] = jnp.zeros((tokens, ch), bf16)

    from_lane(0, 2)
    from_other(0, 6)
    from_other(0, 2)
    from_cross(3)
    from_cross(1)
    from_lane(1, 2)
    from_other(0, 4)
    from_other(1, 6)
    from_other(1, 2)

    @pl.when(takes)
    def _():
        beyond.wait_recv()
        relay.start()

    await_bytes(cache.at[r, 0:frames - 1], cache_recv.at[0])
    cache_mate = remote(cache.at[r], cache.at[r], cache_send.at[1], cache_recv.at[1], mate)
    cache_mate.start()
    from_mate(0)

    def time_rows_of(t):
        found = []
        at, left = t * ch, ch
        while left:
            shard, inside = at // time_rows, at % time_rows
            count = min(time_rows - inside, left)
            found.append(time_w[shard * time_span + inside:shard * time_span + inside + count, :])
            at, left = at + count, left - count
        return jnp.concatenate(found, axis=0)

    def temporal(lane):
        total = jnp.dot(mix[lane + 1], time_rows_of(1), preferred_element_type=f32)
        total = total + jnp.dot(mix[lane], time_rows_of(0), preferred_element_type=f32)
        return total + jnp.dot(mix[lane + 2], time_rows_of(2), preferred_element_type=f32)

    await_bytes(mix.at[2 - x], misc_recv.at[1])
    given[0] = temporal(1 - x).astype(bf16)
    temporal_swap = exchange(given.at[0], given.at[1], 5, at_frame(1))
    temporal_swap.start()
    await_bytes(cache.at[1 - r], cache_recv.at[1])
    pick = pick_ref[0]
    cached = cache[...].astype(f32).reshape(2 * frames, 2, images, ch)
    picked_keys = jnp.zeros((2 * frames, ch), f32)
    picked_values = jnp.zeros((2 * frames, ch), f32)
    for i in range(images):
        picked_keys = jnp.where(pick == i, cached[:, 0, i, :], picked_keys)
        picked_values = jnp.where(pick == i, cached[:, 1, i, :], picked_values)
    picked_keys, picked_values = picked_keys.astype(bf16), picked_values.astype(bf16)
    from_cross(2)
    from_other(1, 7)
    from_other(1, 3)
    from_other(1, 4)

    @pl.when(gives)
    def _():
        await_bytes(mix.at[3 * x], misc_recv.at[4])

    own_temporal = temporal(x)
    from_other(1, 5)
    temporal_swap.wait_recv()
    total = hidden + own_temporal + given[1].astype(f32)
    blended = total.astype(bf16).astype(f32)
    normed = normalize(blended, gains_ref[2:3, :]).astype(bf16)
    from_mate(1)
    own_keys, own_values = kv.at[0, r], kv.at[1, r]
    own_keys[...] = jnp.dot(normed, attn_w[:, ch:2 * ch], preferred_element_type=f32).astype(bf16)
    swap_keys = exchange(own_keys, own_keys, 0, mate)
    swap_keys.start()
    own_values[...] = jnp.dot(normed, attn_w[:, 2 * ch:3 * ch], preferred_element_type=f32).astype(bf16)
    swap_values = exchange(own_values, own_values, 3, mate)
    swap_values.start()
    queries = jnp.dot(normed, attn_w[:, :ch], preferred_element_type=f32).astype(bf16) * head_dim ** (-0.5)
    first_head = lax.broadcasted_iota(jnp.int32, (tokens, 2 * head_dim), 1) < head_dim
    none = jnp.zeros((tokens, 2 * head_dim), bf16)
    ones = jnp.ones((2 * (tokens + frames), 2 * head_dim), bf16)
    pairs = [slice(2 * h * head_dim, 2 * (h + 1) * head_dim) for h in range(heads // 2)]
    await_bytes(kv.at[0, 1 - r], misc_recv.at[0])
    weights = []
    for at in pairs:
        both = jnp.concatenate([
            jnp.where(first_head, queries[:, at], none), jnp.where(first_head, none, queries[:, at]),
        ], axis=0)
        keys = jnp.concatenate([kv[0, 0, :, at], kv[0, 1, :, at], picked_keys[:, at]], axis=0)
        scores = lax.dot_general(both, keys, (((1,), (1,)), ((), ())), preferred_element_type=f32)
        weights.append(jnp.exp(scores - jnp.max(scores, axis=-1, keepdims=True)).astype(bf16))
    await_bytes(kv.at[1, 1 - r], misc_recv.at[3])
    for at, probs in zip(pairs, weights):
        values = jnp.concatenate([kv[1, 0, :, at], kv[1, 1, :, at], picked_values[:, at]], axis=0)
        mixed = jnp.dot(probs, jnp.concatenate([values, ones], axis=1), preferred_element_type=f32)
        mixed = mixed[:, :2 * head_dim] / mixed[:, 2 * head_dim:]
        attended[:, at] = jnp.where(first_head, mixed[:tokens], mixed[tokens:]).astype(bf16)
    result = blended + jnp.dot(attended[...], attn_w[:, 3 * ch:], preferred_element_type=f32)
    out_ref[0] = result.astype(bf16).reshape(rows, columns, ch)

    for k in range(1, QUAD):
        act_copy(k).wait_send()
        sums[k].wait_send()
    for k in range(QUAD):
        edge(k).wait_send()
    await_bytes(conv_w.at[0, 0:4 * conv_quarter], conv_send.at[0])
    await_bytes(cache.at[r, 0:frames - 1], cache_send.at[0])
    cache_mate.wait_send()
    weights_sent(0)
    weights_sent(1)
    swap_keys.wait_send()
    swap_values.wait_send()

    beside.wait_send()
    temporal_swap.wait_send()

    @pl.when(gives)
    def _():
        beyond.wait_send()

    @pl.when(takes)
    def _():
        relay.wait_send()


def by_kernel(
    frame_count, frames_in, norm_gains, conv_weight, time_weight, attention_weight,
    reference_keys, reference_values, reference_pick,
):
    _, rows, columns, ch = frames_in.shape
    tokens = rows * columns
    images = reference_keys.shape[0]
    vmem = pl.BlockSpec(memory_space=pltpu.VMEM)
    hbm = pl.BlockSpec(memory_space=pl.ANY)
    dma = pltpu.SemaphoreType.DMA
    bf16 = jnp.bfloat16
    time_span = round_up(time_weight.shape[0], 64)
    conv_span = max(17 * ch // 8, 7 * ch // 8 + round_up(conv_weight.shape[0], 64))
    return pl.pallas_call(
        functools.partial(kernel, HEADS, images),
        out_shape=pltpu.VMEM(frames_in.shape, bf16),
        in_specs=[hbm, hbm, hbm, hbm, pl.BlockSpec(memory_space=pltpu.SMEM), hbm, hbm, hbm],
        out_specs=vmem,
        scratch_shapes=[
            pltpu.VMEM((rows, columns, ch), bf16),
            pltpu.VMEM(norm_gains.shape, jnp.float32),
            pltpu.VMEM((2, conv_span, ch), bf16),
            pltpu.VMEM((frame_count * time_span, ch), bf16),
            pltpu.VMEM((frame_count * attention_weight.shape[0], 4 * ch), bf16),
            pltpu.VMEM((3, QUAD, tokens + 2 * columns, ch), bf16),
            pltpu.VMEM((QUAD, tokens, ch), jnp.float32),
            pltpu.VMEM((QUAD, tokens, ch), bf16),
            pltpu.VMEM((QUAD, tokens, ch), bf16),
            pltpu.VMEM((LANES + 2, tokens, ch), bf16),
            pltpu.VMEM((2, tokens, ch), bf16),
            pltpu.VMEM((2, 2, tokens, ch), bf16),
            pltpu.VMEM((2, frame_count, 2, images, ch), bf16),
            pltpu.VMEM((tokens, ch), bf16),
            dma((7,)),
            dma((QUAD,)),
            dma((QUAD,)),
            dma((QUAD,)),
            dma((QUAD,)),
            dma((1,)),
            dma((2 * CHUNKS + 1,)),
            dma((2, QUAD)),
            dma((QUAD,)),
            dma((2, frame_count)),
            dma((2,)),
            dma((2,)),
            dma((QUAD,)),
            dma((QUAD,)),
            dma((6,)),
            dma((6,)),
            dma((2,)),
            dma((2,)),
        ],
        compiler_params=pltpu.CompilerParams(
            collective_id=0, has_side_effects=True, vmem_limit_bytes=60 * 2**20
        ),
    )(frames_in, norm_gains, reference_keys[:, 0], reference_values[:, 0], reference_pick, conv_weight, time_weight, attention_weight)


def on_device(sizes, *operands):
    frames_in, _, conv_weight, time_weight, attention_weight, keys, _, _ = operands
    count = sizes["frame"]
    rows, columns, channels = frames_in.shape[1:]
    share = channels // 8
    fits = (
        sizes["groups"] == 2 and sizes["row"] == 2 and count == 2 * QUAD
        and frames_in.shape[0] == 1 and rows == 2 and columns % 16 == 0 and keys.shape[1] == 1
        and channels == 64 * HEADS and HEADS % 2 == 0 and channels % 128 == 0 and conv_weight.shape[0] == 9 * share
        and time_weight.shape[0] == 3 * share and attention_weight.shape[0] == share
    )
    if fits:
        return by_kernel(count, *operands)
    return by_collectives(*operands)


def solution(mesh):
    return jax.shard_map(
        functools.partial(on_device, dict(mesh.shape)),
        mesh=mesh,
        in_specs=(
            P(("groups", "frame"), "row", None, None),
            P(),
            P("frame", None),
            P("frame", None),
            P("frame", None),
            P("groups", ("frame", "row"), None),
            P("groups", ("frame", "row"), None),
            P(("groups", "frame")),
        ),
        out_specs=P(("groups", "frame"), "row", None, None),
        check_vma=False,
    )
```

```python
import functools

import jax
import jax.numpy as jnp
from jax import lax
from jax.experimental import pallas as pl
from jax.experimental.pallas import tpu as pltpu
from jax.sharding import PartitionSpec as P

HEADS = 10
LANES = 2
QUAD = 4
CHUNKS = 3
MESH = pl.DeviceIdType.MESH


def padded_2(x, sides, width):
    for axis, dim in sides:
        devices, length = (lax.axis_size(axis), x.shape[dim])
        up = [(i, (i + 1) % devices) for i in range(devices - 1)]
        down = [(j, i) for i, j in up]
        last = lax.slice_in_dim(x, length - width, length, axis=dim)
        initial = lax.slice_in_dim(x, 0, width, axis=dim)
        before = lax.ppermute(last, axis, up)
        after = lax.ppermute(initial, axis, down)
        x = jnp.concatenate([before, x, after], axis=dim)
    return x


def normalize(values, gain):
    scale = lax.rsqrt(jnp.mean(values * values, axis=-1, keepdims=True) + 1e-05)
    return values * scale * gain


def heads_first(block, head_dim):
    split = block.reshape(block.shape[0], block.shape[1], HEADS, head_dim)
    return jnp.transpose(split, (2, 0, 1, 3))


def by_collectives(
    frames_in,
    norm_gains,
    conv_weight,
    time_weight,
    attention_weight,
    reference_keys,
    reference_values,
    reference_pick,
):
    local_frames, local_rows, columns, channels = frames_in.shape
    head_dim = channels // HEADS
    tokens = local_frames * local_rows * columns
    row_count = lax.axis_size("row")
    row_place = lax.axis_index("row")

    def halve(matrix):
        share = matrix.shape[1] // row_count
        return lax.dynamic_slice_in_dim(matrix, row_place * share, share, 1)

    conv_half, time_half, attention_half = (
        lax.all_gather(halve(conv_weight), "frame", axis=0, tiled=True),
        lax.all_gather(halve(time_weight), "frame", axis=0, tiled=True),
        lax.all_gather(halve(attention_weight), "frame", axis=0, tiled=True),
    )
    conv_full, time_full, attention_full = (
        lax.all_gather(conv_half, "row", axis=1, tiled=True),
        lax.all_gather(time_half, "row", axis=1, tiled=True),
        lax.all_gather(attention_half, "row", axis=1, tiled=True),
    )
    inputs = frames_in.astype(jnp.float32)
    activated = jax.nn.silu(normalize(inputs, norm_gains[0])).astype(jnp.bfloat16)
    padded = padded_2(activated, (("row", 1),), 1)
    padded = jnp.pad(padded, ((0, 0), (0, 0), (1, 1), (0, 0)))
    spatial = jnp.zeros((tokens, channels), jnp.float32)
    for offset_row in range(3):
        for offset_col in range(3):
            window = padded[
                :, offset_row : offset_row + local_rows, offset_col : offset_col + columns, :
            ].reshape(tokens, channels)
            row_start = (3 * offset_row + offset_col) * channels
            spatial = spatial + jnp.dot(
                window,
                conv_full[row_start : row_start + channels],
                preferred_element_type=jnp.float32,
            )
    hidden = (inputs + spatial.reshape(inputs.shape)).astype(jnp.bfloat16)
    hidden_wide = hidden.astype(jnp.float32)
    mixed = jax.nn.silu(normalize(hidden_wide, norm_gains[1])).astype(jnp.bfloat16)
    nearby = padded_2(mixed, (("frame", 0),), 1)
    temporal = jnp.zeros((tokens, channels), jnp.float32)
    for offset_frame in range(3):
        window = nearby[offset_frame : offset_frame + local_frames].reshape(tokens, channels)
        temporal = temporal + jnp.dot(
            window,
            time_full[offset_frame * channels : (offset_frame + 1) * channels],
            preferred_element_type=jnp.float32,
        )
    blended = (hidden_wide + temporal.reshape(inputs.shape)).astype(jnp.bfloat16)
    blended_wide = blended.astype(jnp.float32)
    normed = normalize(blended_wide, norm_gains[2]).astype(jnp.bfloat16).reshape(tokens, channels)
    projected = jnp.dot(
        normed, attention_full[:, : 3 * channels], preferred_element_type=jnp.float32
    ).astype(jnp.bfloat16)
    projected = projected.reshape(local_frames, local_rows * columns, 3 * channels)
    queries = projected[:, :, :channels]
    own_keys = projected[:, :, channels : 2 * channels]
    own_values = projected[:, :, 2 * channels :]
    frame_keys, frame_values = (
        lax.all_gather(own_keys, "row", axis=1, tiled=True),
        lax.all_gather(own_values, "row", axis=1, tiled=True),
    )
    cache_keys, cache_values = (
        lax.all_gather(reference_keys, ("frame", "row"), axis=1, tiled=True),
        lax.all_gather(reference_values, ("frame", "row"), axis=1, tiled=True),
    )
    picked_keys = jnp.take(cache_keys, reference_pick, axis=0)
    picked_values = jnp.take(cache_values, reference_pick, axis=0)
    keys_all = jnp.concatenate([frame_keys, picked_keys], axis=1)
    values_all = jnp.concatenate([frame_values, picked_values], axis=1)

    def one_head(operands):
        query_head, key_head, value_head = operands
        scores = jnp.einsum(
            "fqd,fkd->fqk", query_head, key_head, preferred_element_type=jnp.float32
        ) * head_dim ** (-0.5)
        ceiling = jnp.max(scores, axis=-1, keepdims=True)
        weights = jnp.exp(scores - ceiling)
        probs = (weights / jnp.sum(weights, axis=-1, keepdims=True)).astype(jnp.bfloat16)
        return jnp.einsum(
            "fqk,fkd->fqd", probs, value_head, preferred_element_type=jnp.float32
        ).astype(jnp.bfloat16)

    per_head = lax.map(
        one_head,
        (
            heads_first(queries, head_dim),
            heads_first(keys_all, head_dim),
            heads_first(values_all, head_dim),
        ),
    )
    attended = jnp.transpose(per_head, (1, 2, 0, 3)).reshape(tokens, channels)
    output = jnp.dot(
        attended, attention_full[:, 3 * channels :], preferred_element_type=jnp.float32
    )
    return (blended_wide + output.reshape(inputs.shape)).astype(jnp.bfloat16)


def round_up(value, unit):
    return -(-value // unit) * unit


def flip(frame, k):
    z, x = frame // LANES, frame % LANES
    kz, kx = k // LANES, k % LANES
    high = (z // 2 + kz // 2) % 2
    low = (z % 2 + kz % 2) % 2
    return (2 * high + low) * LANES + (x + kx) % 2


def kernel(
    heads, images,
    x_ref, gains_hbm, keys_ref, values_ref, pick_ref, conv_ref, time_ref, attn_ref,
    out_ref,
    x_own, gains_ref, conv_w, time_w, attn_w, shifted, part, partial_out, partial_in, mix, given, kv, cache, attended,
    local_sem, act_send, act_recv, edge_send, edge_recv, conv_send, conv_recv,
    lane_recv, cross_recv, other_recv, mate_recv, weight_send,
    sum_send, sum_recv, misc_send, misc_recv, cache_send, cache_recv,
):
    y, frame, r = lax.axis_index("groups"), lax.axis_index("frame"), lax.axis_index("row")
    frames = 2 * QUAD
    _, rows, columns, ch = x_ref.shape
    tokens = rows * columns
    head_dim = ch // heads
    share = ch // 8
    conv_rows, time_rows, attn_rows = conv_ref.shape[0], time_ref.shape[0], attn_ref.shape[0]
    conv_quarter = round_up(conv_rows, 64) // 4
    conv_first = conv_quarter // 2 // 16 * 16
    conv_last = max(conv_quarter // 6 // 16 * 16, 16)
    conv_chunks = (
        (0, conv_first), (conv_first, conv_quarter - conv_first - conv_last),
        (conv_quarter - conv_last, conv_last),
    )
    time_quarter = round_up(time_rows, 64) // 4
    time_span = 4 * time_quarter
    f32, bf16 = jnp.float32, jnp.bfloat16
    own = frame % QUAD
    mine, theirs = 2 * y + r, 2 * (1 - y) + r
    mate = {"row": 1 - r}
    opposite = {"groups": 1 - y}

    def rows_at(start, size):
        return pl.ds(pl.multiple_of(start, 16), size)

    def at_frame(k):
        return {"frame": flip(frame, k)}

    def remote(src, dst, send_sem, recv_sem, to):
        return pltpu.make_async_remote_copy(
            src_ref=src, dst_ref=dst, send_sem=send_sem, recv_sem=recv_sem,
            device_id=to, device_id_type=MESH,
        )

    def await_bytes(ref, sem):
        pltpu.make_async_copy(ref, ref, sem).wait()

    def clear(slot, shard, covered, blocks):
        for i in range(blocks):
            start = i * share + jnp.where(i < shard, 0, covered)
            conv_w[slot, rows_at(start, share), :] = jnp.zeros((share, ch), bf16)

    early = [
        pltpu.make_async_copy(x_ref.at[0], x_own, local_sem.at[0]),
        pltpu.make_async_copy(gains_hbm, gains_ref, local_sem.at[6]),
    ]
    for f in early:
        f.start()
    partners = [at_frame(k) for k in range(1, frames)] + [mate, opposite]
    barrier = pltpu.get_barrier_semaphore()
    for to in partners:
        pl.semaphore_signal(barrier, inc=1, device_id=to, device_id_type=MESH)

    opposite_shard = flip(frame, 4)
    clear(0, frame, conv_rows, 8)
    fills = [
        pltpu.make_async_copy(conv_ref, conv_w.at[0, rows_at(frame * share, conv_rows)], local_sem.at[1]),
        pltpu.make_async_copy(time_ref, time_w.at[rows_at(frame * time_span, time_rows)], local_sem.at[2]),
        pltpu.make_async_copy(attn_ref, attn_w.at[rows_at(frame * attn_rows, attn_rows)], local_sem.at[3]),
        pltpu.make_async_copy(keys_ref, cache.at[r, frame, 0], local_sem.at[4]),
        pltpu.make_async_copy(values_ref, cache.at[r, frame, 1], local_sem.at[5]),
    ]
    for f in fills:
        f.start()
    clear(1, opposite_shard, 4 * conv_quarter, 7)
    if time_span > time_rows:
        gap = time_span - time_rows
        time_w[rows_at(frame * time_span + time_rows, gap), :] = jnp.zeros((gap, ch), bf16)
    shifted[1, :, rows_at(r * (rows + 1) * columns, columns), :] = jnp.zeros((QUAD, columns, ch), bf16)

    def act(v, g):
        n = normalize(v, gains_ref[g:g + 1, :])
        return n / (1.0 + jnp.exp(-n))

    for f in early:
        f.wait()
    own_x = x_own[...].reshape(tokens, ch).astype(f32)
    shifted[1, own, columns:columns + tokens, :] = act(own_x, 0).astype(bf16)
    pl.semaphore_wait(barrier, len(partners))

    def act_copy(k):
        ref = shifted.at[1, own if k < 3 else flip(own, 1), columns:columns + tokens]
        return remote(ref, ref, act_send.at[k], act_recv.at[k], at_frame(min(k, 2)))

    def edge(k):
        slot = flip(own, k)
        return remote(
            shifted.at[1, slot, rows_at(rows * columns - r * (rows - 1) * columns, columns)],
            shifted.at[1, slot, rows_at(r * (rows + 1) * columns, columns)],
            edge_send.at[k], edge_recv.at[k], mate,
        )

    def edge_wait(k):
        slot = flip(own, k)
        await_bytes(shifted.at[1, slot, rows_at((1 - r) * (rows + 1) * columns, columns)], edge_recv.at[k])

    def conv_part(slot, shard, q, i):
        first, count = conv_chunks[i]
        return conv_w.at[slot, rows_at(shard * share + q * conv_quarter + first, count)]

    def send_conv(slot, shard, q, i, recv, to):
        remote(
            conv_part(slot, shard, q, i), conv_part(1, shard, q, i),
            conv_send.at[0], conv_recv.at[recv], to,
        ).start()

    def conv_from_lane(i):
        await_bytes(conv_part(1, opposite_shard, mine, i), conv_recv.at[i])
        send_conv(1, opposite_shard, mine, i, CHUNKS + i, opposite)
        send_conv(1, opposite_shard, mine, i, 2 * CHUNKS, mate)

    def conv_from_other(i):
        await_bytes(conv_part(1, opposite_shard, theirs, i), conv_recv.at[CHUNKS + i])
        send_conv(1, opposite_shard, theirs, i, 2 * CHUNKS, mate)

    def conv_from_mate():
        await_bytes(conv_w.at[1, 0:2 * conv_quarter], conv_recv.at[2 * CHUNKS])

    def time_part(d, q, count=1):
        return time_w.at[rows_at(d * time_span + q * time_quarter, count * time_quarter)]

    def attn_part(d, q, count=1):
        return attn_w.at[rows_at(d * attn_rows, attn_rows), pl.ds(pl.multiple_of(q * ch, 128), count * ch)]

    def pieces(w):
        return time_part if w == 0 else attn_part

    def send_weight(w, ref, recv_sem, to):
        remote(ref, ref, weight_send.at[w], recv_sem, to).start()

    def weights_across():
        send_weight(1, attn_part(frame, 2 * r, 2), cross_recv.at[0], at_frame(1))

    def weights_along(w, k):
        send_weight(w, pieces(w)(frame, mine), lane_recv.at[w, k], at_frame(2 * k))

    def from_lane(w, k):
        ref = pieces(w)(flip(frame, 2 * k), mine)
        await_bytes(ref, lane_recv.at[w, k])
        if w == 1 and k != 2:
            send_weight(w, ref, cross_recv.at[k], at_frame(1))
        if w == 0 or k != 2:
            send_weight(w, ref, other_recv.at[w, 2 * k], opposite)
        send_weight(w, ref, mate_recv.at[w], mate)

    def relay_lane(w):
        send_weight(w, pieces(w)(flip(frame, 6), mine), lane_recv.at[w, 2], at_frame(2))

    def from_cross(k):
        ref = attn_part(flip(frame, 1), 2 * r, 2) if k == 0 else attn_part(flip(frame, 2 * k + 1), mine)
        await_bytes(ref, cross_recv.at[k])
        if k == 3:
            send_weight(1, ref, cross_recv.at[2], at_frame(2))
        if k % 2 == 1:
            send_weight(1, ref, other_recv.at[1, 2 * k + 1], opposite)
        send_weight(1, ref, mate_recv.at[1], mate)

    def from_other(w, k):
        ref = pieces(w)(flip(frame, k), theirs)
        await_bytes(ref, other_recv.at[w, k])
        if w == 1 and k >= 6:
            send_weight(w, ref, other_recv.at[w, k - 2], at_frame(2))
        send_weight(w, ref, mate_recv.at[w], mate)

    def weight_bytes(w, quarters):
        if w == 0:
            return time_w.at[0:quarters * time_quarter]
        return attn_w.at[0:quarters * attn_rows // 2, 0:2 * ch]

    def from_mate(w):
        await_bytes(weight_bytes(w, (6, 14)[w]), mate_recv.at[w])

    def weights_sent(w):
        if w == 0:
            await_bytes(time_w.at[0:12 * time_quarter], weight_send.at[w])
        else:
            await_bytes(attn_w.at[0:7 * attn_rows], weight_send.at[w])

    def exchange(src, dst, k, to):
        return remote(src, dst, misc_send.at[k], misc_recv.at[k], to)

    def share_refs(k):
        return remote(cache.at[r, frame], cache.at[r, frame], cache_send.at[0], cache_recv.at[0], at_frame(k))

    act_copy(1).start()
    act_copy(2).start()
    edge(0).start()
    fills[0].wait()
    for i in range(CHUNKS):
        send_conv(0, frame, mine, i, i, at_frame(4))
    for f in fills[1:]:
        f.wait()

    def from_quad(k):
        slot = flip(own, k)
        await_bytes(shifted.at[1, slot, columns:columns + tokens], act_recv.at[k])
        if k == 1:
            act_copy(3).start()
        edge(k).start()

    for k in range(1, frames, 2):
        time_w[rows_at(flip(frame, k) * time_span, time_span), :] = jnp.zeros((time_span, ch), bf16)

    from_quad(1)
    weights_across()
    from_quad(2)
    conv_from_lane(0)
    conv_from_lane(1)
    from_quad(3)
    weights_along(0, 3)
    weights_along(1, 3)
    weights_along(1, 1)
    weights_along(0, 1)
    conv_from_lane(2)
    conv_from_other(0)

    blank = jnp.zeros((1, ch), f32)

    def shift(k):
        slot = flip(own, k)
        edge_wait(k)
        for i in range(rows + 2):
            span = slice(i * columns, (i + 1) * columns)
            row = shifted[1, slot, span, :].astype(f32)
            shifted[0, slot, span, :] = jnp.concatenate([blank, row[:columns - 1]], axis=0).astype(bf16)
            shifted[2, slot, span, :] = jnp.concatenate([row[1:], blank], axis=0).astype(bf16)

    for k in range(QUAD):
        shift(k)

    def windows(shard, j, slot=None):
        tap = shard + j
        dy, dx = tap // 3, tap % 3
        if slot is None:
            return shifted[dx, :, rows_at(dy * columns, tokens), :].reshape(QUAD * tokens, ch)
        return shifted[dx, pl.ds(slot, LANES), rows_at(dy * columns, tokens), :].reshape(LANES * tokens, ch)

    def partial_sum(slot, shard, j, place=None):
        return jnp.dot(windows(shard, j, place), conv_w[slot, j * ch:(j + 1) * ch, :], preferred_element_type=f32)

    part[...] = (partial_sum(0, frame, 0) + partial_sum(0, frame, 1)).reshape(QUAD, tokens, ch)

    for i in range(1, CHUNKS):
        conv_from_other(i)
    conv_from_mate()
    sums = {}
    for near in (1, 0):
        pair = flip(own, 2 * near) // LANES * LANES
        total = part[pl.ds(pair, LANES)] + (
            partial_sum(1, opposite_shard, 0, pair) + partial_sum(1, opposite_shard, 1, pair)
        ).reshape(LANES, tokens, ch)
        partial_out[pl.ds(pair, LANES)] = total.astype(bf16)
        if near == 0:
            part[pl.ds(pair, LANES)] = total
        for k in (2 * near + 1, 2 * near):
            if k:
                slot = flip(own, k)
                sums[k] = remote(partial_out.at[slot], partial_in.at[own], sum_send.at[k], sum_recv.at[k], at_frame(k))
                sums[k].start()

    for k in range(1, frames):
        share_refs(k).start()
    from_lane(0, 3)
    relay_lane(0)
    from_lane(1, 3)
    relay_lane(1)
    from_lane(1, 1)
    from_lane(0, 1)
    from_cross(0)

    total = own_x + part[own]
    for k in range(1, QUAD):
        slot = flip(own, k)
        await_bytes(partial_in.at[slot], sum_recv.at[k])
        total = total + partial_in[slot].astype(f32)
    hidden = total.astype(bf16).astype(f32)
    z, x = frame // LANES, frame % LANES
    depth = frames // LANES
    mix[1 + x] = act(hidden, 1).astype(bf16)

    gives = jnp.where(x == 0, z > 0, z < depth - 1)
    takes = jnp.where(x == 0, z < depth - 1, z > 0)
    far = mix.at[3 * (1 - x)]
    beside = exchange(mix.at[1 + x], mix.at[1 + x], 1, at_frame(1))
    beyond = exchange(mix.at[1 + x], far, 2, {"frame": jnp.clip(frame + 4 * x - 2, 0, frames - 1)})
    relay = exchange(far, far, 4, at_frame(1))

    @pl.when(gives)
    def _():
        beyond.start()

    beside.start()

    @pl.when(z == 0)
    def _():
        mix[0] = jnp.zeros((tokens, ch), bf16)

    @pl.when(z == depth - 1)
    def _():
        mix[3] = jnp.zeros((tokens, ch), bf16)

    from_other(1, 6)
    from_lane(0, 2)
    from_cross(3)
    from_other(0, 6)
    from_other(0, 2)
    from_cross(1)
    from_other(1, 2)
    from_other(0, 4)
    from_lane(1, 2)
    from_other(1, 7)

    @pl.when(takes)
    def _():
        beyond.wait_recv()
        relay.start()

    from_mate(0)

    def time_rows_of(t):
        found = []
        at, left = t * ch, ch
        while left:
            shard, inside = at // time_rows, at % time_rows
            count = min(time_rows - inside, left)
            found.append(time_w[shard * time_span + inside:shard * time_span + inside + count, :])
            at, left = at + count, left - count
        return jnp.concatenate(found, axis=0)

    def temporal(lane):
        total = jnp.dot(mix[lane + 1], time_rows_of(1), preferred_element_type=f32)
        total = total + jnp.dot(mix[lane], time_rows_of(0), preferred_element_type=f32)
        return total + jnp.dot(mix[lane + 2], time_rows_of(2), preferred_element_type=f32)

    await_bytes(mix.at[2 - x], misc_recv.at[1])
    given[0] = temporal(1 - x).astype(bf16)
    temporal_swap = exchange(given.at[0], given.at[1], 5, at_frame(1))
    temporal_swap.start()
    from_other(1, 4)
    from_cross(2)
    from_other(1, 3)
    await_bytes(cache.at[r, 0:frames - 1], cache_recv.at[0])
    cache_mate = remote(cache.at[r], cache.at[r], cache_send.at[1], cache_recv.at[1], mate)
    cache_mate.start()

    @pl.when(gives)
    def _():
        await_bytes(mix.at[3 * x], misc_recv.at[4])

    own_temporal = temporal(x)
    from_other(1, 5)
    await_bytes(cache.at[1 - r], cache_recv.at[1])
    pick = pick_ref[0]
    cached = cache[...].astype(f32).reshape(2 * frames, 2, images, ch)
    picked_keys = jnp.zeros((2 * frames, ch), f32)
    picked_values = jnp.zeros((2 * frames, ch), f32)
    for i in range(images):
        picked_keys = jnp.where(pick == i, cached[:, 0, i, :], picked_keys)
        picked_values = jnp.where(pick == i, cached[:, 1, i, :], picked_values)
    picked_keys, picked_values = picked_keys.astype(bf16), picked_values.astype(bf16)
    temporal_swap.wait_recv()
    total = hidden + own_temporal + given[1].astype(f32)
    blended = total.astype(bf16).astype(f32)
    normed = normalize(blended, gains_ref[2:3, :]).astype(bf16)
    from_mate(1)
    own_keys, own_values = kv.at[0, r], kv.at[1, r]
    own_keys[...] = jnp.dot(normed, attn_w[:, ch:2 * ch], preferred_element_type=f32).astype(bf16)
    swap_keys = exchange(own_keys, own_keys, 0, mate)
    swap_keys.start()
    own_values[...] = jnp.dot(normed, attn_w[:, 2 * ch:3 * ch], preferred_element_type=f32).astype(bf16)
    swap_values = exchange(own_values, own_values, 3, mate)
    swap_values.start()
    queries = jnp.dot(normed, attn_w[:, :ch], preferred_element_type=f32).astype(bf16) * head_dim ** (-0.5)
    first_head = lax.broadcasted_iota(jnp.int32, (tokens, 2 * head_dim), 1) < head_dim
    none = jnp.zeros((tokens, 2 * head_dim), bf16)
    ones = jnp.ones((2 * (tokens + frames), 2 * head_dim), bf16)
    pairs = [slice(2 * h * head_dim, 2 * (h + 1) * head_dim) for h in range(heads // 2)]
    await_bytes(kv.at[0, 1 - r], misc_recv.at[0])
    weights = []
    for at in pairs:
        both = jnp.concatenate([
            jnp.where(first_head, queries[:, at], none), jnp.where(first_head, none, queries[:, at]),
        ], axis=0)
        keys = jnp.concatenate([kv[0, 0, :, at], kv[0, 1, :, at], picked_keys[:, at]], axis=0)
        scores = lax.dot_general(both, keys, (((1,), (1,)), ((), ())), preferred_element_type=f32)
        weights.append(jnp.exp(scores - jnp.max(scores, axis=-1, keepdims=True)).astype(bf16))
    await_bytes(kv.at[1, 1 - r], misc_recv.at[3])
    for at, probs in zip(pairs, weights):
        values = jnp.concatenate([kv[1, 0, :, at], kv[1, 1, :, at], picked_values[:, at]], axis=0)
        mixed = jnp.dot(probs, jnp.concatenate([values, ones], axis=1), preferred_element_type=f32)
        mixed = mixed[:, :2 * head_dim] / mixed[:, 2 * head_dim:]
        attended[:, at] = jnp.where(first_head, mixed[:tokens], mixed[tokens:]).astype(bf16)
    result = blended + jnp.dot(attended[...], attn_w[:, 3 * ch:], preferred_element_type=f32)
    out_ref[0] = result.astype(bf16).reshape(rows, columns, ch)

    for k in range(1, QUAD):
        act_copy(k).wait_send()
        sums[k].wait_send()
    for k in range(QUAD):
        edge(k).wait_send()
    await_bytes(conv_w.at[0, 0:4 * conv_quarter], conv_send.at[0])
    await_bytes(cache.at[r, 0:frames - 1], cache_send.at[0])
    cache_mate.wait_send()
    weights_sent(0)
    weights_sent(1)
    swap_keys.wait_send()
    swap_values.wait_send()

    beside.wait_send()
    temporal_swap.wait_send()

    @pl.when(gives)
    def _():
        beyond.wait_send()

    @pl.when(takes)
    def _():
        relay.wait_send()


def by_kernel(
    frame_count, frames_in, norm_gains, conv_weight, time_weight, attention_weight,
    reference_keys, reference_values, reference_pick,
):
    _, rows, columns, ch = frames_in.shape
    tokens = rows * columns
    images = reference_keys.shape[0]
    vmem = pl.BlockSpec(memory_space=pltpu.VMEM)
    hbm = pl.BlockSpec(memory_space=pl.ANY)
    dma = pltpu.SemaphoreType.DMA
    bf16 = jnp.bfloat16
    time_span = round_up(time_weight.shape[0], 64)
    conv_span = max(17 * ch // 8, 7 * ch // 8 + round_up(conv_weight.shape[0], 64))
    return pl.pallas_call(
        functools.partial(kernel, HEADS, images),
        out_shape=pltpu.VMEM(frames_in.shape, bf16),
        in_specs=[hbm, hbm, hbm, hbm, pl.BlockSpec(memory_space=pltpu.SMEM), hbm, hbm, hbm],
        out_specs=vmem,
        scratch_shapes=[
            pltpu.VMEM((rows, columns, ch), bf16),
            pltpu.VMEM(norm_gains.shape, jnp.float32),
            pltpu.VMEM((2, conv_span, ch), bf16),
            pltpu.VMEM((frame_count * time_span, ch), bf16),
            pltpu.VMEM((frame_count * attention_weight.shape[0], 4 * ch), bf16),
            pltpu.VMEM((3, QUAD, tokens + 2 * columns, ch), bf16),
            pltpu.VMEM((QUAD, tokens, ch), jnp.float32),
            pltpu.VMEM((QUAD, tokens, ch), bf16),
            pltpu.VMEM((QUAD, tokens, ch), bf16),
            pltpu.VMEM((LANES + 2, tokens, ch), bf16),
            pltpu.VMEM((2, tokens, ch), bf16),
            pltpu.VMEM((2, 2, tokens, ch), bf16),
            pltpu.VMEM((2, frame_count, 2, images, ch), bf16),
            pltpu.VMEM((tokens, ch), bf16),
            dma((7,)),
            dma((QUAD,)),
            dma((QUAD,)),
            dma((QUAD,)),
            dma((QUAD,)),
            dma((1,)),
            dma((2 * CHUNKS + 1,)),
            dma((2, QUAD)),
            dma((QUAD,)),
            dma((2, frame_count)),
            dma((2,)),
            dma((2,)),
            dma((QUAD,)),
            dma((QUAD,)),
            dma((6,)),
            dma((6,)),
            dma((2,)),
            dma((2,)),
        ],
        compiler_params=pltpu.CompilerParams(
            collective_id=0, has_side_effects=True, vmem_limit_bytes=60 * 2**20
        ),
    )(frames_in, norm_gains, reference_keys[:, 0], reference_values[:, 0], reference_pick, conv_weight, time_weight, attention_weight)


def on_device(sizes, *operands):
    frames_in, _, conv_weight, time_weight, attention_weight, keys, _, _ = operands
    count = sizes["frame"]
    rows, columns, channels = frames_in.shape[1:]
    share = channels // 8
    fits = (
        sizes["groups"] == 2 and sizes["row"] == 2 and count == 2 * QUAD
        and frames_in.shape[0] == 1 and rows == 2 and columns % 16 == 0 and keys.shape[1] == 1
        and channels == 64 * HEADS and HEADS % 2 == 0 and channels % 128 == 0 and conv_weight.shape[0] == 9 * share
        and time_weight.shape[0] == 3 * share and attention_weight.shape[0] == share
    )
    if fits:
        return by_kernel(count, *operands)
    return by_collectives(*operands)


def solution(mesh):
    return jax.shard_map(
        functools.partial(on_device, dict(mesh.shape)),
        mesh=mesh,
        in_specs=(
            P(("groups", "frame"), "row", None, None),
            P(),
            P("frame", None),
            P("frame", None),
            P("frame", None),
            P("groups", ("frame", "row"), None),
            P("groups", ("frame", "row"), None),
            P(("groups", "frame")),
        ),
        out_specs=P(("groups", "frame"), "row", None, None),
        check_vma=False,
    )
```

```python
import functools

import jax
import jax.numpy as jnp
from jax import lax
from jax.experimental import pallas as pl
from jax.experimental.pallas import tpu as pltpu
from jax.sharding import PartitionSpec as P

HEADS = 10
LANES = 2
QUAD = 4
CHUNKS = 3
MESH = pl.DeviceIdType.MESH


def padded_2(x, sides, width):
    for axis, dim in sides:
        devices, length = (lax.axis_size(axis), x.shape[dim])
        up = [(i, (i + 1) % devices) for i in range(devices - 1)]
        down = [(j, i) for i, j in up]
        last = lax.slice_in_dim(x, length - width, length, axis=dim)
        initial = lax.slice_in_dim(x, 0, width, axis=dim)
        before = lax.ppermute(last, axis, up)
        after = lax.ppermute(initial, axis, down)
        x = jnp.concatenate([before, x, after], axis=dim)
    return x


def normalize(values, gain):
    scale = lax.rsqrt(jnp.mean(values * values, axis=-1, keepdims=True) + 1e-05)
    return values * scale * gain


def heads_first(block, head_dim):
    split = block.reshape(block.shape[0], block.shape[1], HEADS, head_dim)
    return jnp.transpose(split, (2, 0, 1, 3))


def by_collectives(
    frames_in,
    norm_gains,
    conv_weight,
    time_weight,
    attention_weight,
    reference_keys,
    reference_values,
    reference_pick,
):
    local_frames, local_rows, columns, channels = frames_in.shape
    head_dim = channels // HEADS
    tokens = local_frames * local_rows * columns
    row_count = lax.axis_size("row")
    row_place = lax.axis_index("row")

    def halve(matrix):
        share = matrix.shape[1] // row_count
        return lax.dynamic_slice_in_dim(matrix, row_place * share, share, 1)

    conv_half, time_half, attention_half = (
        lax.all_gather(halve(conv_weight), "frame", axis=0, tiled=True),
        lax.all_gather(halve(time_weight), "frame", axis=0, tiled=True),
        lax.all_gather(halve(attention_weight), "frame", axis=0, tiled=True),
    )
    conv_full, time_full, attention_full = (
        lax.all_gather(conv_half, "row", axis=1, tiled=True),
        lax.all_gather(time_half, "row", axis=1, tiled=True),
        lax.all_gather(attention_half, "row", axis=1, tiled=True),
    )
    inputs = frames_in.astype(jnp.float32)
    activated = jax.nn.silu(normalize(inputs, norm_gains[0])).astype(jnp.bfloat16)
    padded = padded_2(activated, (("row", 1),), 1)
    padded = jnp.pad(padded, ((0, 0), (0, 0), (1, 1), (0, 0)))
    spatial = jnp.zeros((tokens, channels), jnp.float32)
    for offset_row in range(3):
        for offset_col in range(3):
            window = padded[
                :, offset_row : offset_row + local_rows, offset_col : offset_col + columns, :
            ].reshape(tokens, channels)
            row_start = (3 * offset_row + offset_col) * channels
            spatial = spatial + jnp.dot(
                window,
                conv_full[row_start : row_start + channels],
                preferred_element_type=jnp.float32,
            )
    hidden = (inputs + spatial.reshape(inputs.shape)).astype(jnp.bfloat16)
    hidden_wide = hidden.astype(jnp.float32)
    mixed = jax.nn.silu(normalize(hidden_wide, norm_gains[1])).astype(jnp.bfloat16)
    nearby = padded_2(mixed, (("frame", 0),), 1)
    temporal = jnp.zeros((tokens, channels), jnp.float32)
    for offset_frame in range(3):
        window = nearby[offset_frame : offset_frame + local_frames].reshape(tokens, channels)
        temporal = temporal + jnp.dot(
            window,
            time_full[offset_frame * channels : (offset_frame + 1) * channels],
            preferred_element_type=jnp.float32,
        )
    blended = (hidden_wide + temporal.reshape(inputs.shape)).astype(jnp.bfloat16)
    blended_wide = blended.astype(jnp.float32)
    normed = normalize(blended_wide, norm_gains[2]).astype(jnp.bfloat16).reshape(tokens, channels)
    projected = jnp.dot(
        normed, attention_full[:, : 3 * channels], preferred_element_type=jnp.float32
    ).astype(jnp.bfloat16)
    projected = projected.reshape(local_frames, local_rows * columns, 3 * channels)
    queries = projected[:, :, :channels]
    own_keys = projected[:, :, channels : 2 * channels]
    own_values = projected[:, :, 2 * channels :]
    frame_keys, frame_values = (
        lax.all_gather(own_keys, "row", axis=1, tiled=True),
        lax.all_gather(own_values, "row", axis=1, tiled=True),
    )
    cache_keys, cache_values = (
        lax.all_gather(reference_keys, ("frame", "row"), axis=1, tiled=True),
        lax.all_gather(reference_values, ("frame", "row"), axis=1, tiled=True),
    )
    picked_keys = jnp.take(cache_keys, reference_pick, axis=0)
    picked_values = jnp.take(cache_values, reference_pick, axis=0)
    keys_all = jnp.concatenate([frame_keys, picked_keys], axis=1)
    values_all = jnp.concatenate([frame_values, picked_values], axis=1)

    def one_head(operands):
        query_head, key_head, value_head = operands
        scores = jnp.einsum(
            "fqd,fkd->fqk", query_head, key_head, preferred_element_type=jnp.float32
        ) * head_dim ** (-0.5)
        ceiling = jnp.max(scores, axis=-1, keepdims=True)
        weights = jnp.exp(scores - ceiling)
        probs = (weights / jnp.sum(weights, axis=-1, keepdims=True)).astype(jnp.bfloat16)
        return jnp.einsum(
            "fqk,fkd->fqd", probs, value_head, preferred_element_type=jnp.float32
        ).astype(jnp.bfloat16)

    per_head = lax.map(
        one_head,
        (
            heads_first(queries, head_dim),
            heads_first(keys_all, head_dim),
            heads_first(values_all, head_dim),
        ),
    )
    attended = jnp.transpose(per_head, (1, 2, 0, 3)).reshape(tokens, channels)
    output = jnp.dot(
        attended, attention_full[:, 3 * channels :], preferred_element_type=jnp.float32
    )
    return (blended_wide + output.reshape(inputs.shape)).astype(jnp.bfloat16)


def round_up(value, unit):
    return -(-value // unit) * unit


def flip(frame, k):
    z, x = frame // LANES, frame % LANES
    kz, kx = k // LANES, k % LANES
    high = (z // 2 + kz // 2) % 2
    low = (z % 2 + kz % 2) % 2
    return (2 * high + low) * LANES + (x + kx) % 2


def kernel(
    heads, images,
    x_ref, gains_hbm, keys_ref, values_ref, pick_ref, conv_ref, time_ref, attn_ref,
    out_ref,
    x_own, gains_ref, conv_w, time_w, attn_w, shifted, part, partial_out, partial_in, mix, given, kv, cache, attended,
    local_sem, act_send, act_recv, edge_send, edge_recv, conv_send, conv_recv,
    lane_recv, cross_recv, other_recv, mate_recv, weight_send,
    sum_send, sum_recv, misc_send, misc_recv, cache_send, cache_recv,
):
    y, frame, r = lax.axis_index("groups"), lax.axis_index("frame"), lax.axis_index("row")
    frames = 2 * QUAD
    _, rows, columns, ch = x_ref.shape
    tokens = rows * columns
    head_dim = ch // heads
    share = ch // 8
    conv_rows, time_rows, attn_rows = conv_ref.shape[0], time_ref.shape[0], attn_ref.shape[0]
    conv_quarter = round_up(conv_rows, 64) // 4
    conv_first = conv_quarter // 2 // 16 * 16
    conv_last = max(conv_quarter // 6 // 16 * 16, 16)
    conv_chunks = (
        (0, conv_first), (conv_first, conv_quarter - conv_first - conv_last),
        (conv_quarter - conv_last, conv_last),
    )
    time_quarter = round_up(time_rows, 64) // 4
    time_span = 4 * time_quarter
    f32, bf16 = jnp.float32, jnp.bfloat16
    z, x = frame // LANES, frame % LANES
    depth = frames // LANES

    def slot_of(k):
        return (x + k % LANES) % LANES * 2 + (z + k // LANES) % 2

    own = slot_of(0)
    mine, theirs = 2 * y + r, 2 * (1 - y) + r
    mate = {"row": 1 - r}
    opposite = {"groups": 1 - y}

    def rows_at(start, size):
        return pl.ds(pl.multiple_of(start, 16), size)

    def at_frame(k):
        return {"frame": flip(frame, k)}

    def remote(src, dst, send_sem, recv_sem, to):
        return pltpu.make_async_remote_copy(
            src_ref=src, dst_ref=dst, send_sem=send_sem, recv_sem=recv_sem,
            device_id=to, device_id_type=MESH,
        )

    def await_bytes(ref, sem):
        pltpu.make_async_copy(ref, ref, sem).wait()

    def clear(slot, shard, covered, blocks):
        for i in range(blocks):
            start = i * share + jnp.where(i < shard, 0, covered)
            conv_w[slot, rows_at(start, share), :] = jnp.zeros((share, ch), bf16)

    early = [
        pltpu.make_async_copy(x_ref.at[0], x_own, local_sem.at[0]),
        pltpu.make_async_copy(gains_hbm, gains_ref, local_sem.at[6]),
    ]
    for f in early:
        f.start()
    partners = [at_frame(k) for k in range(1, frames)] + [mate, opposite]
    barrier = pltpu.get_barrier_semaphore()
    for to in partners:
        pl.semaphore_signal(barrier, inc=1, device_id=to, device_id_type=MESH)

    opposite_shard = flip(frame, 4)
    clear(0, frame, conv_rows, 8)
    fills = [
        pltpu.make_async_copy(conv_ref, conv_w.at[0, rows_at(frame * share, conv_rows)], local_sem.at[1]),
        pltpu.make_async_copy(time_ref, time_w.at[rows_at(frame * time_span, time_rows)], local_sem.at[2]),
        pltpu.make_async_copy(attn_ref, attn_w.at[rows_at(frame * attn_rows, attn_rows)], local_sem.at[3]),
        pltpu.make_async_copy(keys_ref, cache.at[r, frame, 0], local_sem.at[4]),
        pltpu.make_async_copy(values_ref, cache.at[r, frame, 1], local_sem.at[5]),
    ]
    for f in fills:
        f.start()
    clear(1, opposite_shard, 4 * conv_quarter, 7)
    if time_span > time_rows:
        gap = time_span - time_rows
        time_w[rows_at(frame * time_span + time_rows, gap), :] = jnp.zeros((gap, ch), bf16)
    shifted[1, :, rows_at(r * (rows + 1) * columns, columns), :] = jnp.zeros((QUAD, columns, ch), bf16)

    def act(v, g):
        n = normalize(v, gains_ref[g:g + 1, :])
        return n / (1.0 + jnp.exp(-n))

    for f in early:
        f.wait()
    own_x = x_own[...].reshape(tokens, ch).astype(f32)
    shifted[1, own, columns:columns + tokens, :] = act(own_x, 0).astype(bf16)
    pl.semaphore_wait(barrier, len(partners))

    def act_copy(k):
        ref = shifted.at[1, own if k < 3 else slot_of(1), columns:columns + tokens]
        return remote(ref, ref, act_send.at[k], act_recv.at[k], at_frame(min(k, 2)))

    def edge(k):
        slot = slot_of(k)
        return remote(
            shifted.at[1, slot, rows_at(rows * columns - r * (rows - 1) * columns, columns)],
            shifted.at[1, slot, rows_at(r * (rows + 1) * columns, columns)],
            edge_send.at[k], edge_recv.at[k], mate,
        )

    def edge_wait(k):
        slot = slot_of(k)
        await_bytes(shifted.at[1, slot, rows_at((1 - r) * (rows + 1) * columns, columns)], edge_recv.at[k])

    def conv_part(slot, shard, q, i):
        first, count = conv_chunks[i]
        return conv_w.at[slot, rows_at(shard * share + q * conv_quarter + first, count)]

    def send_conv(slot, shard, q, i, recv, to):
        remote(
            conv_part(slot, shard, q, i), conv_part(1, shard, q, i),
            conv_send.at[0], conv_recv.at[recv], to,
        ).start()

    def conv_from_lane(i):
        await_bytes(conv_part(1, opposite_shard, mine, i), conv_recv.at[i])
        send_conv(1, opposite_shard, mine, i, CHUNKS + i, opposite)
        send_conv(1, opposite_shard, mine, i, 2 * CHUNKS, mate)

    def conv_from_other(i):
        await_bytes(conv_part(1, opposite_shard, theirs, i), conv_recv.at[CHUNKS + i])
        send_conv(1, opposite_shard, theirs, i, 2 * CHUNKS, mate)

    def conv_from_mate():
        await_bytes(conv_w.at[1, 0:2 * conv_quarter], conv_recv.at[2 * CHUNKS])

    def time_part(d, q, count=1):
        return time_w.at[rows_at(d * time_span + q * time_quarter, count * time_quarter)]

    def attn_part(d, q, count=1):
        return attn_w.at[rows_at(d * attn_rows, attn_rows), pl.ds(pl.multiple_of(q * ch, 128), count * ch)]

    def pieces(w):
        return time_part if w == 0 else attn_part

    def send_weight(w, ref, recv_sem, to):
        remote(ref, ref, weight_send.at[w], recv_sem, to).start()

    def weights_across():
        send_weight(1, attn_part(frame, 2 * r, 2), cross_recv.at[0], at_frame(1))

    def weights_along(w, k):
        send_weight(w, pieces(w)(frame, mine), lane_recv.at[w, k], at_frame(2 * k))

    def from_lane(w, k):
        ref = pieces(w)(flip(frame, 2 * k), mine)
        await_bytes(ref, lane_recv.at[w, k])
        if w == 1:
            send_weight(w, ref, cross_recv.at[k], at_frame(1))
        if w == 0 or k != 2:
            send_weight(w, ref, other_recv.at[w, 2 * k], opposite)
        send_weight(w, ref, mate_recv.at[w], mate)

    def relay_lane(w):
        send_weight(w, pieces(w)(flip(frame, 6), mine), lane_recv.at[w, 2], at_frame(2))

    def from_cross(k):
        ref = attn_part(flip(frame, 1), 2 * r, 2) if k == 0 else attn_part(flip(frame, 2 * k + 1), mine)
        await_bytes(ref, cross_recv.at[k])
        if k % 2 == 1:
            send_weight(1, ref, other_recv.at[1, 2 * k + 1], opposite)
        send_weight(1, ref, mate_recv.at[1], mate)

    def from_other(w, k):
        ref = pieces(w)(flip(frame, k), theirs)
        await_bytes(ref, other_recv.at[w, k])
        if w == 1 and k >= 6:
            send_weight(w, ref, other_recv.at[w, k - 2], at_frame(2))
        send_weight(w, ref, mate_recv.at[w], mate)

    def weight_bytes(w, quarters):
        if w == 0:
            return time_w.at[0:quarters * time_quarter]
        return attn_w.at[0:quarters * attn_rows // 2, 0:2 * ch]

    def from_mate(w):
        await_bytes(weight_bytes(w, (6, 14)[w]), mate_recv.at[w])

    def weights_sent(w):
        if w == 0:
            await_bytes(time_w.at[0:12 * time_quarter], weight_send.at[w])
        else:
            await_bytes(attn_w.at[0:7 * attn_rows], weight_send.at[w])

    def exchange(src, dst, k, to):
        return remote(src, dst, misc_send.at[k], misc_recv.at[k], to)

    def share_refs(k):
        return remote(cache.at[r, frame], cache.at[r, frame], cache_send.at[0], cache_recv.at[0], at_frame(k))

    act_copy(1).start()
    act_copy(2).start()
    edge(0).start()
    fills[0].wait()
    for i in range(CHUNKS):
        send_conv(0, frame, mine, i, i, at_frame(4))
    for f in fills[1:]:
        f.wait()

    def from_quad(k):
        slot = slot_of(k)
        await_bytes(shifted.at[1, slot, columns:columns + tokens], act_recv.at[k])
        if k == 1:
            act_copy(3).start()
        edge(k).start()

    for k in range(1, frames, 2):
        time_w[rows_at(flip(frame, k) * time_span, time_span), :] = jnp.zeros((time_span, ch), bf16)

    from_quad(1)
    from_quad(2)
    conv_from_lane(0)
    conv_from_lane(1)
    from_quad(3)
    weights_across()
    weights_along(0, 3)
    weights_along(1, 3)
    weights_along(1, 1)
    conv_from_lane(2)
    conv_from_other(0)

    blank = jnp.zeros((1, ch), f32)

    def shift(k):
        slot = slot_of(k)
        edge_wait(k)
        for i in range(rows + 2):
            span = slice(i * columns, (i + 1) * columns)
            row = shifted[1, slot, span, :].astype(f32)
            shifted[0, slot, span, :] = jnp.concatenate([blank, row[:columns - 1]], axis=0).astype(bf16)
            shifted[2, slot, span, :] = jnp.concatenate([row[1:], blank], axis=0).astype(bf16)

    for k in range(QUAD):
        shift(k)

    def windows(shard, j, slot=None):
        tap = shard + j
        dy, dx = tap // 3, tap % 3
        if slot is None:
            return shifted[dx, :, rows_at(dy * columns, tokens), :].reshape(QUAD * tokens, ch)
        return shifted[dx, pl.ds(slot, LANES), rows_at(dy * columns, tokens), :].reshape(LANES * tokens, ch)

    def partial_sum(slot, shard, j, place=None):
        return jnp.dot(windows(shard, j, place), conv_w[slot, j * ch:(j + 1) * ch, :], preferred_element_type=f32)

    part[...] = (partial_sum(0, frame, 0) + partial_sum(0, frame, 1)).reshape(QUAD, tokens, ch)

    for i in range(1, CHUNKS):
        conv_from_other(i)
    conv_from_mate()
    def pair_sum(pair):
        return part[pl.ds(pair, 2)] + (
            partial_sum(1, opposite_shard, 0, pair) + partial_sum(1, opposite_shard, 1, pair)
        ).reshape(2, tokens, ch)

    halves = [slice(0, tokens // 2), slice(tokens // 2, tokens)]
    partial_out[pl.ds(2 * (1 - x), 2)] = pair_sum(2 * (1 - x)).astype(bf16)
    across = [
        remote(partial_out.at[slot_of(3), half], partial_in.at[0, half], sum_send.at[h], sum_recv.at[h], at_frame(1))
        for h, half in enumerate(halves)]
    across.append(remote(partial_out.at[slot_of(1)], partial_in.at[1], sum_send.at[2], sum_recv.at[2], at_frame(1)))
    for c in across:
        c.start()
    part[pl.ds(2 * x, 2)] = pair_sum(2 * x)
    from_lane(0, 3)
    relay_lane(0)
    weights_along(0, 1)
    along = [
        remote(partial_out.at[slot_of(2), half], partial_in.at[2, half], sum_send.at[3 + h], sum_recv.at[3 + h], at_frame(2))
        for h, half in enumerate(halves)]
    for h, half in enumerate(halves):
        await_bytes(partial_in.at[0, half], sum_recv.at[h])
        partial_out[slot_of(2), half] = (part[slot_of(2), half] + partial_in[0, half].astype(f32)).astype(bf16)
        along[h].start()
    from_lane(1, 3)
    relay_lane(1)
    for k in range(1, frames):
        share_refs(k).start()
    from_lane(1, 1)
    from_lane(0, 1)
    from_cross(0)

    await_bytes(partial_in.at[1], sum_recv.at[2])
    total = own_x + part[own] + partial_in[1].astype(f32)
    for h, half in enumerate(halves):
        await_bytes(partial_in.at[2, half], sum_recv.at[3 + h])
    total = total + partial_in[2].astype(f32)
    hidden = total.astype(bf16).astype(f32)
    mix[1 + x] = act(hidden, 1).astype(bf16)

    gives = jnp.where(x == 0, z > 0, z < depth - 1)
    takes = jnp.where(x == 0, z < depth - 1, z > 0)
    far = mix.at[3 * (1 - x)]
    beside = exchange(mix.at[1 + x], mix.at[1 + x], 1, at_frame(1))
    beyond = exchange(mix.at[1 + x], far, 2, {"frame": jnp.clip(frame + 4 * x - 2, 0, frames - 1)})
    passed = exchange(mix.at[2 - x], mix.at[3 * x], 4, {"frame": jnp.clip(frame + 2 - 4 * x, 0, frames - 1)})

    @pl.when(gives)
    def _():
        beyond.start()

    beside.start()

    @pl.when(z == 0)
    def _():
        mix[0] = jnp.zeros((tokens, ch), bf16)

    @pl.when(z == depth - 1)
    def _():
        mix[3] = jnp.zeros((tokens, ch), bf16)

    from_other(1, 6)
    from_lane(0, 2)
    from_cross(3)
    from_other(0, 6)
    from_other(0, 2)
    from_cross(1)
    from_lane(1, 2)
    from_other(0, 4)
    from_other(1, 2)

    await_bytes(mix.at[2 - x], misc_recv.at[1])

    @pl.when(takes)
    def _():
        passed.start()

    from_mate(0)

    def time_rows_of(t):
        found = []
        at, left = t * ch, ch
        while left:
            shard, inside = at // time_rows, at % time_rows
            count = min(time_rows - inside, left)
            found.append(time_w[shard * time_span + inside:shard * time_span + inside + count, :])
            at, left = at + count, left - count
        return jnp.concatenate(found, axis=0)

    def temporal(lane):
        total = jnp.dot(mix[lane + 1], time_rows_of(1), preferred_element_type=f32)
        total = total + jnp.dot(mix[lane], time_rows_of(0), preferred_element_type=f32)
        return total + jnp.dot(mix[lane + 2], time_rows_of(2), preferred_element_type=f32)

    @pl.when(takes)
    def _():
        beyond.wait_recv()

    given[0] = temporal(1 - x).astype(bf16)
    temporal_swap = exchange(given.at[0], given.at[1], 5, at_frame(1))
    temporal_swap.start()
    from_other(1, 7)
    from_cross(2)
    from_other(1, 4)
    from_other(1, 3)
    await_bytes(cache.at[r, 0:frames - 1], cache_recv.at[0])
    cache_mate = remote(cache.at[r], cache.at[r], cache_send.at[1], cache_recv.at[1], mate)
    cache_mate.start()

    @pl.when(gives)
    def _():
        await_bytes(mix.at[3 * x], misc_recv.at[4])

    own_temporal = temporal(x)
    from_other(1, 5)
    await_bytes(cache.at[1 - r], cache_recv.at[1])
    pick = pick_ref[0]
    cached = cache[...].astype(f32).reshape(2 * frames, 2, images, ch)
    picked_keys = jnp.zeros((2 * frames, ch), f32)
    picked_values = jnp.zeros((2 * frames, ch), f32)
    for i in range(images):
        picked_keys = jnp.where(pick == i, cached[:, 0, i, :], picked_keys)
        picked_values = jnp.where(pick == i, cached[:, 1, i, :], picked_values)
    picked_keys, picked_values = picked_keys.astype(bf16), picked_values.astype(bf16)
    temporal_swap.wait_recv()
    total = hidden + own_temporal + given[1].astype(f32)
    blended = total.astype(bf16).astype(f32)
    normed = normalize(blended, gains_ref[2:3, :]).astype(bf16)
    from_mate(1)
    own_keys, own_values = kv.at[0, r], kv.at[1, r]
    own_keys[...] = jnp.dot(normed, attn_w[:, ch:2 * ch], preferred_element_type=f32).astype(bf16)
    swap_keys = exchange(own_keys, own_keys, 0, mate)
    swap_keys.start()
    own_values[...] = jnp.dot(normed, attn_w[:, 2 * ch:3 * ch], preferred_element_type=f32).astype(bf16)
    swap_values = exchange(own_values, own_values, 3, mate)
    swap_values.start()
    queries = jnp.dot(normed, attn_w[:, :ch], preferred_element_type=f32).astype(bf16) * head_dim ** (-0.5)
    first_head = lax.broadcasted_iota(jnp.int32, (tokens, 2 * head_dim), 1) < head_dim
    none = jnp.zeros((tokens, 2 * head_dim), bf16)
    ones = jnp.ones((2 * (tokens + frames), 2 * head_dim), bf16)
    pairs = [slice(2 * h * head_dim, 2 * (h + 1) * head_dim) for h in range(heads // 2)]
    await_bytes(kv.at[0, 1 - r], misc_recv.at[0])
    weights = []
    for at in pairs:
        both = jnp.concatenate([
            jnp.where(first_head, queries[:, at], none), jnp.where(first_head, none, queries[:, at]),
        ], axis=0)
        keys = jnp.concatenate([kv[0, 0, :, at], kv[0, 1, :, at], picked_keys[:, at]], axis=0)
        scores = lax.dot_general(both, keys, (((1,), (1,)), ((), ())), preferred_element_type=f32)
        weights.append(jnp.exp(scores - jnp.max(scores, axis=-1, keepdims=True)).astype(bf16))
    await_bytes(kv.at[1, 1 - r], misc_recv.at[3])
    for at, probs in zip(pairs, weights):
        values = jnp.concatenate([kv[1, 0, :, at], kv[1, 1, :, at], picked_values[:, at]], axis=0)
        mixed = jnp.dot(probs, jnp.concatenate([values, ones], axis=1), preferred_element_type=f32)
        mixed = mixed[:, :2 * head_dim] / mixed[:, 2 * head_dim:]
        attended[:, at] = jnp.where(first_head, mixed[:tokens], mixed[tokens:]).astype(bf16)
    result = blended + jnp.dot(attended[...], attn_w[:, 3 * ch:], preferred_element_type=f32)
    out_ref[0] = result.astype(bf16).reshape(rows, columns, ch)

    for k in range(1, QUAD):
        act_copy(k).wait_send()
    for c in along + across:
        c.wait_send()
    for k in range(QUAD):
        edge(k).wait_send()
    await_bytes(conv_w.at[0, 0:4 * conv_quarter], conv_send.at[0])
    await_bytes(cache.at[r, 0:frames - 1], cache_send.at[0])
    cache_mate.wait_send()
    weights_sent(0)
    weights_sent(1)
    swap_keys.wait_send()
    swap_values.wait_send()

    beside.wait_send()
    temporal_swap.wait_send()

    @pl.when(gives)
    def _():
        beyond.wait_send()

    @pl.when(takes)
    def _():
        passed.wait_send()


def by_kernel(
    frame_count, frames_in, norm_gains, conv_weight, time_weight, attention_weight,
    reference_keys, reference_values, reference_pick,
):
    _, rows, columns, ch = frames_in.shape
    tokens = rows * columns
    images = reference_keys.shape[0]
    vmem = pl.BlockSpec(memory_space=pltpu.VMEM)
    hbm = pl.BlockSpec(memory_space=pl.ANY)
    dma = pltpu.SemaphoreType.DMA
    bf16 = jnp.bfloat16
    time_span = round_up(time_weight.shape[0], 64)
    conv_span = max(17 * ch // 8, 7 * ch // 8 + round_up(conv_weight.shape[0], 64))
    return pl.pallas_call(
        functools.partial(kernel, HEADS, images),
        out_shape=pltpu.VMEM(frames_in.shape, bf16),
        in_specs=[hbm, hbm, hbm, hbm, pl.BlockSpec(memory_space=pltpu.SMEM), hbm, hbm, hbm],
        out_specs=vmem,
        scratch_shapes=[
            pltpu.VMEM((rows, columns, ch), bf16),
            pltpu.VMEM(norm_gains.shape, jnp.float32),
            pltpu.VMEM((2, conv_span, ch), bf16),
            pltpu.VMEM((frame_count * time_span, ch), bf16),
            pltpu.VMEM((frame_count * attention_weight.shape[0], 4 * ch), bf16),
            pltpu.VMEM((3, QUAD, tokens + 2 * columns, ch), bf16),
            pltpu.VMEM((QUAD, tokens, ch), jnp.float32),
            pltpu.VMEM((QUAD, tokens, ch), bf16),
            pltpu.VMEM((QUAD, tokens, ch), bf16),
            pltpu.VMEM((LANES + 2, tokens, ch), bf16),
            pltpu.VMEM((2, tokens, ch), bf16),
            pltpu.VMEM((2, 2, tokens, ch), bf16),
            pltpu.VMEM((2, frame_count, 2, images, ch), bf16),
            pltpu.VMEM((tokens, ch), bf16),
            dma((7,)),
            dma((QUAD,)),
            dma((QUAD,)),
            dma((QUAD,)),
            dma((QUAD,)),
            dma((1,)),
            dma((2 * CHUNKS + 1,)),
            dma((2, QUAD)),
            dma((QUAD,)),
            dma((2, frame_count)),
            dma((2,)),
            dma((2,)),
            dma((5,)),
            dma((5,)),
            dma((6,)),
            dma((6,)),
            dma((2,)),
            dma((2,)),
        ],
        compiler_params=pltpu.CompilerParams(
            collective_id=0, has_side_effects=True, vmem_limit_bytes=60 * 2**20
        ),
    )(frames_in, norm_gains, reference_keys[:, 0], reference_values[:, 0], reference_pick, conv_weight, time_weight, attention_weight)


def on_device(sizes, *operands):
    frames_in, _, conv_weight, time_weight, attention_weight, keys, _, _ = operands
    count = sizes["frame"]
    rows, columns, channels = frames_in.shape[1:]
    share = channels // 8
    fits = (
        sizes["groups"] == 2 and sizes["row"] == 2 and count == 2 * QUAD
        and frames_in.shape[0] == 1 and rows == 2 and columns % 16 == 0 and keys.shape[1] == 1
        and channels == 64 * HEADS and HEADS % 2 == 0 and channels % 128 == 0 and conv_weight.shape[0] == 9 * share
        and time_weight.shape[0] == 3 * share and attention_weight.shape[0] == share
    )
    if fits:
        return by_kernel(count, *operands)
    return by_collectives(*operands)


def solution(mesh):
    return jax.shard_map(
        functools.partial(on_device, dict(mesh.shape)),
        mesh=mesh,
        in_specs=(
            P(("groups", "frame"), "row", None, None),
            P(),
            P("frame", None),
            P("frame", None),
            P("frame", None),
            P("groups", ("frame", "row"), None),
            P("groups", ("frame", "row"), None),
            P(("groups", "frame")),
        ),
        out_specs=P(("groups", "frame"), "row", None, None),
        check_vma=False,
    )
```

```python
import functools

import jax
import jax.numpy as jnp
from jax import lax
from jax.experimental import pallas as pl
from jax.experimental.pallas import tpu as pltpu
from jax.sharding import PartitionSpec as P

HEADS = 10
LANES = 2
QUAD = 4
CHUNKS = 3
MESH = pl.DeviceIdType.MESH


def padded_2(x, sides, width):
    for axis, dim in sides:
        devices, length = (lax.axis_size(axis), x.shape[dim])
        up = [(i, (i + 1) % devices) for i in range(devices - 1)]
        down = [(j, i) for i, j in up]
        last = lax.slice_in_dim(x, length - width, length, axis=dim)
        initial = lax.slice_in_dim(x, 0, width, axis=dim)
        before = lax.ppermute(last, axis, up)
        after = lax.ppermute(initial, axis, down)
        x = jnp.concatenate([before, x, after], axis=dim)
    return x


def normalize(values, gain):
    scale = lax.rsqrt(jnp.mean(values * values, axis=-1, keepdims=True) + 1e-05)
    return values * scale * gain


def heads_first(block, head_dim):
    split = block.reshape(block.shape[0], block.shape[1], HEADS, head_dim)
    return jnp.transpose(split, (2, 0, 1, 3))


def by_collectives(
    frames_in,
    norm_gains,
    conv_weight,
    time_weight,
    attention_weight,
    reference_keys,
    reference_values,
    reference_pick,
):
    local_frames, local_rows, columns, channels = frames_in.shape
    head_dim = channels // HEADS
    tokens = local_frames * local_rows * columns
    row_count = lax.axis_size("row")
    row_place = lax.axis_index("row")

    def halve(matrix):
        share = matrix.shape[1] // row_count
        return lax.dynamic_slice_in_dim(matrix, row_place * share, share, 1)

    conv_half, time_half, attention_half = (
        lax.all_gather(halve(conv_weight), "frame", axis=0, tiled=True),
        lax.all_gather(halve(time_weight), "frame", axis=0, tiled=True),
        lax.all_gather(halve(attention_weight), "frame", axis=0, tiled=True),
    )
    conv_full, time_full, attention_full = (
        lax.all_gather(conv_half, "row", axis=1, tiled=True),
        lax.all_gather(time_half, "row", axis=1, tiled=True),
        lax.all_gather(attention_half, "row", axis=1, tiled=True),
    )
    inputs = frames_in.astype(jnp.float32)
    activated = jax.nn.silu(normalize(inputs, norm_gains[0])).astype(jnp.bfloat16)
    padded = padded_2(activated, (("row", 1),), 1)
    padded = jnp.pad(padded, ((0, 0), (0, 0), (1, 1), (0, 0)))
    spatial = jnp.zeros((tokens, channels), jnp.float32)
    for offset_row in range(3):
        for offset_col in range(3):
            window = padded[
                :, offset_row : offset_row + local_rows, offset_col : offset_col + columns, :
            ].reshape(tokens, channels)
            row_start = (3 * offset_row + offset_col) * channels
            spatial = spatial + jnp.dot(
                window,
                conv_full[row_start : row_start + channels],
                preferred_element_type=jnp.float32,
            )
    hidden = (inputs + spatial.reshape(inputs.shape)).astype(jnp.bfloat16)
    hidden_wide = hidden.astype(jnp.float32)
    mixed = jax.nn.silu(normalize(hidden_wide, norm_gains[1])).astype(jnp.bfloat16)
    nearby = padded_2(mixed, (("frame", 0),), 1)
    temporal = jnp.zeros((tokens, channels), jnp.float32)
    for offset_frame in range(3):
        window = nearby[offset_frame : offset_frame + local_frames].reshape(tokens, channels)
        temporal = temporal + jnp.dot(
            window,
            time_full[offset_frame * channels : (offset_frame + 1) * channels],
            preferred_element_type=jnp.float32,
        )
    blended = (hidden_wide + temporal.reshape(inputs.shape)).astype(jnp.bfloat16)
    blended_wide = blended.astype(jnp.float32)
    normed = normalize(blended_wide, norm_gains[2]).astype(jnp.bfloat16).reshape(tokens, channels)
    projected = jnp.dot(
        normed, attention_full[:, : 3 * channels], preferred_element_type=jnp.float32
    ).astype(jnp.bfloat16)
    projected = projected.reshape(local_frames, local_rows * columns, 3 * channels)
    queries = projected[:, :, :channels]
    own_keys = projected[:, :, channels : 2 * channels]
    own_values = projected[:, :, 2 * channels :]
    frame_keys, frame_values = (
        lax.all_gather(own_keys, "row", axis=1, tiled=True),
        lax.all_gather(own_values, "row", axis=1, tiled=True),
    )
    cache_keys, cache_values = (
        lax.all_gather(reference_keys, ("frame", "row"), axis=1, tiled=True),
        lax.all_gather(reference_values, ("frame", "row"), axis=1, tiled=True),
    )
    picked_keys = jnp.take(cache_keys, reference_pick, axis=0)
    picked_values = jnp.take(cache_values, reference_pick, axis=0)
    keys_all = jnp.concatenate([frame_keys, picked_keys], axis=1)
    values_all = jnp.concatenate([frame_values, picked_values], axis=1)

    def one_head(operands):
        query_head, key_head, value_head = operands
        scores = jnp.einsum(
            "fqd,fkd->fqk", query_head, key_head, preferred_element_type=jnp.float32
        ) * head_dim ** (-0.5)
        ceiling = jnp.max(scores, axis=-1, keepdims=True)
        weights = jnp.exp(scores - ceiling)
        probs = (weights / jnp.sum(weights, axis=-1, keepdims=True)).astype(jnp.bfloat16)
        return jnp.einsum(
            "fqk,fkd->fqd", probs, value_head, preferred_element_type=jnp.float32
        ).astype(jnp.bfloat16)

    per_head = lax.map(
        one_head,
        (
            heads_first(queries, head_dim),
            heads_first(keys_all, head_dim),
            heads_first(values_all, head_dim),
        ),
    )
    attended = jnp.transpose(per_head, (1, 2, 0, 3)).reshape(tokens, channels)
    output = jnp.dot(
        attended, attention_full[:, 3 * channels :], preferred_element_type=jnp.float32
    )
    return (blended_wide + output.reshape(inputs.shape)).astype(jnp.bfloat16)


def round_up(value, unit):
    return -(-value // unit) * unit


def flip(frame, k):
    z, x = frame // LANES, frame % LANES
    kz, kx = k // LANES, k % LANES
    high = (z // 2 + kz // 2) % 2
    low = (z % 2 + kz % 2) % 2
    return (2 * high + low) * LANES + (x + kx) % 2


def kernel(
    heads, images,
    x_ref, gains_hbm, keys_ref, values_ref, pick_ref, conv_ref, time_ref, attn_ref,
    out_ref,
    x_own, gains_ref, conv_w, time_w, attn_w, shifted, part, partial_out, partial_in, mix, given, kv, cache, attended,
    local_sem, act_send, act_recv, edge_send, edge_recv, conv_send, conv_recv,
    lane_recv, cross_recv, other_recv, mate_recv, weight_send,
    sum_send, sum_recv, misc_send, misc_recv, cache_send, cache_recv,
):
    y, frame, r = lax.axis_index("groups"), lax.axis_index("frame"), lax.axis_index("row")
    frames = 2 * QUAD
    _, rows, columns, ch = x_ref.shape
    tokens = rows * columns
    head_dim = ch // heads
    share = ch // 8
    conv_rows, time_rows, attn_rows = conv_ref.shape[0], time_ref.shape[0], attn_ref.shape[0]
    conv_quarter = round_up(conv_rows, 64) // 4
    conv_first = conv_quarter // 2 // 16 * 16
    conv_last = max(conv_quarter // 6 // 16 * 16, 16)
    conv_chunks = (
        (0, conv_first), (conv_first, conv_quarter - conv_first - conv_last),
        (conv_quarter - conv_last, conv_last),
    )
    time_quarter = round_up(time_rows, 64) // 4
    time_span = 4 * time_quarter
    f32, bf16 = jnp.float32, jnp.bfloat16
    z, x = frame // LANES, frame % LANES
    depth = frames // LANES

    def slot_of(k):
        return (x + k % LANES) % LANES * 2 + (z + k // LANES) % 2

    own = slot_of(0)
    mine, theirs = 2 * y + r, 2 * (1 - y) + r
    mate = {"row": 1 - r}
    opposite = {"groups": 1 - y}

    def rows_at(start, size):
        return pl.ds(pl.multiple_of(start, 16), size)

    def at_frame(k):
        return {"frame": flip(frame, k)}

    def remote(src, dst, send_sem, recv_sem, to):
        return pltpu.make_async_remote_copy(
            src_ref=src, dst_ref=dst, send_sem=send_sem, recv_sem=recv_sem,
            device_id=to, device_id_type=MESH,
        )

    def await_bytes(ref, sem):
        pltpu.make_async_copy(ref, ref, sem).wait()

    def clear(slot, shard, covered, blocks):
        for i in range(blocks):
            start = i * share + jnp.where(i < shard, 0, covered)
            conv_w[slot, rows_at(start, share), :] = jnp.zeros((share, ch), bf16)

    early = [
        pltpu.make_async_copy(x_ref.at[0], x_own, local_sem.at[0]),
        pltpu.make_async_copy(gains_hbm, gains_ref, local_sem.at[6]),
    ]
    for f in early:
        f.start()
    partners = [at_frame(k) for k in range(1, frames)] + [mate, opposite]
    barrier = pltpu.get_barrier_semaphore()
    for to in partners:
        pl.semaphore_signal(barrier, inc=1, device_id=to, device_id_type=MESH)

    opposite_shard = flip(frame, 4)
    clear(0, frame, conv_rows, 8)
    fills = [
        pltpu.make_async_copy(conv_ref, conv_w.at[0, rows_at(frame * share, conv_rows)], local_sem.at[1]),
        pltpu.make_async_copy(time_ref, time_w.at[rows_at(frame * time_span, time_rows)], local_sem.at[2]),
        pltpu.make_async_copy(attn_ref, attn_w.at[rows_at(frame * attn_rows, attn_rows)], local_sem.at[3]),
        pltpu.make_async_copy(keys_ref, cache.at[r, frame, 0], local_sem.at[4]),
        pltpu.make_async_copy(values_ref, cache.at[r, frame, 1], local_sem.at[5]),
    ]
    for f in fills:
        f.start()
    clear(1, opposite_shard, 4 * conv_quarter, 7)
    if time_span > time_rows:
        gap = time_span - time_rows
        time_w[rows_at(frame * time_span + time_rows, gap), :] = jnp.zeros((gap, ch), bf16)
    shifted[1, :, rows_at(r * (rows + 1) * columns, columns), :] = jnp.zeros((QUAD, columns, ch), bf16)

    def act(v, g):
        n = normalize(v, gains_ref[g:g + 1, :])
        return n / (1.0 + jnp.exp(-n))

    for f in early:
        f.wait()
    own_x = x_own[...].reshape(tokens, ch).astype(f32)
    shifted[1, own, columns:columns + tokens, :] = act(own_x, 0).astype(bf16)
    pl.semaphore_wait(barrier, len(partners))

    def act_copy(k):
        ref = shifted.at[1, own if k < 3 else slot_of(1), columns:columns + tokens]
        return remote(ref, ref, act_send.at[k], act_recv.at[k], at_frame(min(k, 2)))

    def edge(k):
        slot = slot_of(k)
        return remote(
            shifted.at[1, slot, rows_at(rows * columns - r * (rows - 1) * columns, columns)],
            shifted.at[1, slot, rows_at(r * (rows + 1) * columns, columns)],
            edge_send.at[k], edge_recv.at[k], mate,
        )

    def edge_wait(k):
        slot = slot_of(k)
        await_bytes(shifted.at[1, slot, rows_at((1 - r) * (rows + 1) * columns, columns)], edge_recv.at[k])

    def conv_part(slot, shard, q, i):
        first, count = conv_chunks[i]
        return conv_w.at[slot, rows_at(shard * share + q * conv_quarter + first, count)]

    def send_conv(slot, shard, q, i, recv, to):
        remote(
            conv_part(slot, shard, q, i), conv_part(1, shard, q, i),
            conv_send.at[0], conv_recv.at[recv], to,
        ).start()

    def conv_from_lane(i):
        await_bytes(conv_part(1, opposite_shard, mine, i), conv_recv.at[i])
        send_conv(1, opposite_shard, mine, i, CHUNKS + i, opposite)
        send_conv(1, opposite_shard, mine, i, 2 * CHUNKS, mate)

    def conv_from_other(i):
        await_bytes(conv_part(1, opposite_shard, theirs, i), conv_recv.at[CHUNKS + i])
        send_conv(1, opposite_shard, theirs, i, 2 * CHUNKS, mate)

    def conv_from_mate():
        await_bytes(conv_w.at[1, 0:2 * conv_quarter], conv_recv.at[2 * CHUNKS])

    def time_part(d, q, count=1):
        return time_w.at[rows_at(d * time_span + q * time_quarter, count * time_quarter)]

    def attn_part(d, q, count=1):
        return attn_w.at[rows_at(d * attn_rows, attn_rows), pl.ds(pl.multiple_of(q * ch, 128), count * ch)]

    def pieces(w):
        return time_part if w == 0 else attn_part

    def send_weight(w, ref, recv_sem, to):
        remote(ref, ref, weight_send.at[w], recv_sem, to).start()

    def weights_across():
        send_weight(1, attn_part(frame, 2 * r, 2), cross_recv.at[0], at_frame(1))

    def weights_along(w, k):
        send_weight(w, pieces(w)(frame, mine), lane_recv.at[w, k], at_frame(2 * k))

    def from_lane(w, k):
        ref = pieces(w)(flip(frame, 2 * k), mine)
        await_bytes(ref, lane_recv.at[w, k])
        if w == 1:
            send_weight(w, ref, cross_recv.at[k], at_frame(1))
        if w == 0 or k != 2:
            send_weight(w, ref, other_recv.at[w, 2 * k], opposite)
        send_weight(w, ref, mate_recv.at[w], mate)

    def relay_lane(w):
        send_weight(w, pieces(w)(flip(frame, 6), mine), lane_recv.at[w, 2], at_frame(2))

    def from_cross(k):
        ref = attn_part(flip(frame, 1), 2 * r, 2) if k == 0 else attn_part(flip(frame, 2 * k + 1), mine)
        await_bytes(ref, cross_recv.at[k])
        if k % 2 == 1:
            send_weight(1, ref, other_recv.at[1, 2 * k + 1], opposite)
        send_weight(1, ref, mate_recv.at[1], mate)

    def from_other(w, k):
        ref = pieces(w)(flip(frame, k), theirs)
        await_bytes(ref, other_recv.at[w, k])
        if w == 1 and k >= 6:
            send_weight(w, ref, other_recv.at[w, k - 2], at_frame(2))
        send_weight(w, ref, mate_recv.at[w], mate)

    def weight_bytes(w, quarters):
        if w == 0:
            return time_w.at[0:quarters * time_quarter]
        return attn_w.at[0:quarters * attn_rows // 2, 0:2 * ch]

    def from_mate(w):
        await_bytes(weight_bytes(w, (6, 14)[w]), mate_recv.at[w])

    def weights_sent(w):
        if w == 0:
            await_bytes(time_w.at[0:12 * time_quarter], weight_send.at[w])
        else:
            await_bytes(attn_w.at[0:7 * attn_rows], weight_send.at[w])

    def exchange(src, dst, k, to):
        return remote(src, dst, misc_send.at[k], misc_recv.at[k], to)

    def share_refs(k):
        return remote(cache.at[r, frame], cache.at[r, frame], cache_send.at[0], cache_recv.at[0], at_frame(k))

    act_copy(1).start()
    act_copy(2).start()
    edge(0).start()
    fills[0].wait()
    for i in range(CHUNKS):
        send_conv(0, frame, mine, i, i, at_frame(4))
    for f in fills[1:]:
        f.wait()

    def from_quad(k):
        slot = slot_of(k)
        await_bytes(shifted.at[1, slot, columns:columns + tokens], act_recv.at[k])
        if k == 1:
            act_copy(3).start()
        edge(k).start()

    for k in range(1, frames, 2):
        time_w[rows_at(flip(frame, k) * time_span, time_span), :] = jnp.zeros((time_span, ch), bf16)

    from_quad(1)
    from_quad(2)
    conv_from_lane(0)
    conv_from_lane(1)
    from_quad(3)
    weights_across()
    weights_along(0, 3)
    weights_along(0, 1)
    weights_along(1, 3)
    conv_from_lane(2)
    conv_from_other(0)

    blank = jnp.zeros((1, ch), f32)

    def shift(k):
        slot = slot_of(k)
        edge_wait(k)
        for i in range(rows + 2):
            span = slice(i * columns, (i + 1) * columns)
            row = shifted[1, slot, span, :].astype(f32)
            shifted[0, slot, span, :] = jnp.concatenate([blank, row[:columns - 1]], axis=0).astype(bf16)
            shifted[2, slot, span, :] = jnp.concatenate([row[1:], blank], axis=0).astype(bf16)

    for k in range(QUAD):
        shift(k)

    def windows(shard, j, slot=None):
        tap = shard + j
        dy, dx = tap // 3, tap % 3
        if slot is None:
            return shifted[dx, :, rows_at(dy * columns, tokens), :].reshape(QUAD * tokens, ch)
        return shifted[dx, pl.ds(slot, LANES), rows_at(dy * columns, tokens), :].reshape(LANES * tokens, ch)

    def partial_sum(slot, shard, j, place=None):
        return jnp.dot(windows(shard, j, place), conv_w[slot, j * ch:(j + 1) * ch, :], preferred_element_type=f32)

    part[...] = (partial_sum(0, frame, 0) + partial_sum(0, frame, 1)).reshape(QUAD, tokens, ch)

    for i in range(1, CHUNKS):
        conv_from_other(i)
    conv_from_mate()
    def pair_sum(pair):
        return part[pl.ds(pair, 2)] + (
            partial_sum(1, opposite_shard, 0, pair) + partial_sum(1, opposite_shard, 1, pair)
        ).reshape(2, tokens, ch)

    halves = [slice(0, tokens // 2), slice(tokens // 2, tokens)]
    partial_out[pl.ds(2 * (1 - x), 2)] = pair_sum(2 * (1 - x)).astype(bf16)
    across = [
        remote(partial_out.at[slot_of(3), half], partial_in.at[0, half], sum_send.at[h], sum_recv.at[h], at_frame(1))
        for h, half in enumerate(halves)]
    across.append(remote(partial_out.at[slot_of(1)], partial_in.at[1], sum_send.at[2], sum_recv.at[2], at_frame(1)))
    for c in across:
        c.start()
    part[pl.ds(2 * x, 2)] = pair_sum(2 * x)
    from_lane(0, 3)
    relay_lane(0)
    weights_along(1, 1)
    from_lane(0, 1)
    along = [
        remote(partial_out.at[slot_of(2), half], partial_in.at[2, half], sum_send.at[3 + h], sum_recv.at[3 + h], at_frame(2))
        for h, half in enumerate(halves)]
    for h, half in enumerate(halves):
        await_bytes(partial_in.at[0, half], sum_recv.at[h])
        partial_out[slot_of(2), half] = (part[slot_of(2), half] + partial_in[0, half].astype(f32)).astype(bf16)
        along[h].start()
    from_lane(1, 3)
    relay_lane(1)
    for k in range(1, frames):
        share_refs(k).start()
    from_lane(0, 2)
    from_lane(1, 1)
    from_cross(0)

    await_bytes(partial_in.at[1], sum_recv.at[2])
    total = own_x + part[own] + partial_in[1].astype(f32)
    for h, half in enumerate(halves):
        await_bytes(partial_in.at[2, half], sum_recv.at[3 + h])
    total = total + partial_in[2].astype(f32)
    hidden = total.astype(bf16).astype(f32)
    mix[1 + x] = act(hidden, 1).astype(bf16)

    gives = jnp.where(x == 0, z > 0, z < depth - 1)
    takes = jnp.where(x == 0, z < depth - 1, z > 0)
    far = mix.at[3 * (1 - x)]
    beside = [exchange(mix.at[1 + x, half], mix.at[1 + x, half], 1 + 5 * h, at_frame(1)) for h, half in enumerate(halves)]
    beyond = exchange(mix.at[1 + x], far, 2, {"frame": jnp.clip(frame + 4 * x - 2, 0, frames - 1)})
    past = {"frame": jnp.clip(frame + 2 - 4 * x, 0, frames - 1)}
    passed = [exchange(mix.at[2 - x, half], mix.at[3 * x, half], 4 + 3 * h, past) for h, half in enumerate(halves)]

    @pl.when(gives)
    def _():
        beyond.start()

    for c in beside:
        c.start()

    @pl.when(z == 0)
    def _():
        mix[0] = jnp.zeros((tokens, ch), bf16)

    @pl.when(z == depth - 1)
    def _():
        mix[3] = jnp.zeros((tokens, ch), bf16)

    from_other(1, 6)
    from_cross(3)
    from_other(0, 6)
    from_other(0, 2)
    from_cross(1)
    from_lane(1, 2)
    from_other(0, 4)
    from_other(1, 2)
    await_bytes(mix.at[2 - x, halves[0]], misc_recv.at[1])

    @pl.when(takes)
    def _():
        passed[0].start()

    await_bytes(mix.at[2 - x, halves[1]], misc_recv.at[6])

    @pl.when(takes)
    def _():
        passed[1].start()

    from_other(1, 7)
    from_mate(0)

    def time_rows_of(t):
        found = []
        at, left = t * ch, ch
        while left:
            shard, inside = at // time_rows, at % time_rows
            count = min(time_rows - inside, left)
            found.append(time_w[shard * time_span + inside:shard * time_span + inside + count, :])
            at, left = at + count, left - count
        return jnp.concatenate(found, axis=0)

    def temporal(lane):
        total = jnp.dot(mix[lane + 1], time_rows_of(1), preferred_element_type=f32)
        total = total + jnp.dot(mix[lane], time_rows_of(0), preferred_element_type=f32)
        return total + jnp.dot(mix[lane + 2], time_rows_of(2), preferred_element_type=f32)

    @pl.when(takes)
    def _():
        beyond.wait_recv()

    given[0] = temporal(1 - x).astype(bf16)
    temporal_swap = exchange(given.at[0], given.at[1], 5, at_frame(1))
    temporal_swap.start()
    from_cross(2)
    from_other(1, 4)
    from_other(1, 3)
    await_bytes(cache.at[r, 0:frames - 1], cache_recv.at[0])
    cache_mate = remote(cache.at[r], cache.at[r], cache_send.at[1], cache_recv.at[1], mate)
    cache_mate.start()

    from_other(1, 5)

    @pl.when(gives)
    def _():
        for h, half in enumerate(halves):
            await_bytes(mix.at[3 * x, half], misc_recv.at[4 + 3 * h])

    own_temporal = temporal(x)
    await_bytes(cache.at[1 - r], cache_recv.at[1])
    pick = pick_ref[0]
    cached = cache[...].astype(f32).reshape(2 * frames, 2, images, ch)
    picked_keys = jnp.zeros((2 * frames, ch), f32)
    picked_values = jnp.zeros((2 * frames, ch), f32)
    for i in range(images):
        picked_keys = jnp.where(pick == i, cached[:, 0, i, :], picked_keys)
        picked_values = jnp.where(pick == i, cached[:, 1, i, :], picked_values)
    picked_keys, picked_values = picked_keys.astype(bf16), picked_values.astype(bf16)
    temporal_swap.wait_recv()
    total = hidden + own_temporal + given[1].astype(f32)
    blended = total.astype(bf16).astype(f32)
    normed = normalize(blended, gains_ref[2:3, :]).astype(bf16)
    from_mate(1)
    own_keys, own_values = kv.at[0, r], kv.at[1, r]
    own_keys[...] = jnp.dot(normed, attn_w[:, ch:2 * ch], preferred_element_type=f32).astype(bf16)
    swap_keys = exchange(own_keys, own_keys, 0, mate)
    swap_keys.start()
    own_values[...] = jnp.dot(normed, attn_w[:, 2 * ch:3 * ch], preferred_element_type=f32).astype(bf16)
    swap_values = exchange(own_values, own_values, 3, mate)
    swap_values.start()
    queries = jnp.dot(normed, attn_w[:, :ch], preferred_element_type=f32).astype(bf16) * head_dim ** (-0.5)
    first_head = lax.broadcasted_iota(jnp.int32, (tokens, 2 * head_dim), 1) < head_dim
    none = jnp.zeros((tokens, 2 * head_dim), bf16)
    ones = jnp.ones((2 * (tokens + frames), 2 * head_dim), bf16)
    pairs = [slice(2 * h * head_dim, 2 * (h + 1) * head_dim) for h in range(heads // 2)]
    await_bytes(kv.at[0, 1 - r], misc_recv.at[0])
    weights = []
    for at in pairs:
        both = jnp.concatenate([
            jnp.where(first_head, queries[:, at], none), jnp.where(first_head, none, queries[:, at]),
        ], axis=0)
        keys = jnp.concatenate([kv[0, 0, :, at], kv[0, 1, :, at], picked_keys[:, at]], axis=0)
        scores = lax.dot_general(both, keys, (((1,), (1,)), ((), ())), preferred_element_type=f32)
        weights.append(jnp.exp(scores - jnp.max(scores, axis=-1, keepdims=True)).astype(bf16))
    await_bytes(kv.at[1, 1 - r], misc_recv.at[3])
    for at, probs in zip(pairs, weights):
        values = jnp.concatenate([kv[1, 0, :, at], kv[1, 1, :, at], picked_values[:, at]], axis=0)
        mixed = jnp.dot(probs, jnp.concatenate([values, ones], axis=1), preferred_element_type=f32)
        mixed = mixed[:, :2 * head_dim] / mixed[:, 2 * head_dim:]
        attended[:, at] = jnp.where(first_head, mixed[:tokens], mixed[tokens:]).astype(bf16)
    result = blended + jnp.dot(attended[...], attn_w[:, 3 * ch:], preferred_element_type=f32)
    out_ref[0] = result.astype(bf16).reshape(rows, columns, ch)

    for k in range(1, QUAD):
        act_copy(k).wait_send()
    for c in along + across:
        c.wait_send()
    for k in range(QUAD):
        edge(k).wait_send()
    await_bytes(conv_w.at[0, 0:4 * conv_quarter], conv_send.at[0])
    await_bytes(cache.at[r, 0:frames - 1], cache_send.at[0])
    cache_mate.wait_send()
    weights_sent(0)
    weights_sent(1)
    swap_keys.wait_send()
    swap_values.wait_send()

    for c in beside:
        c.wait_send()
    temporal_swap.wait_send()

    @pl.when(gives)
    def _():
        beyond.wait_send()

    @pl.when(takes)
    def _():
        for c in passed:
            c.wait_send()


def by_kernel(
    frame_count, frames_in, norm_gains, conv_weight, time_weight, attention_weight,
    reference_keys, reference_values, reference_pick,
):
    _, rows, columns, ch = frames_in.shape
    tokens = rows * columns
    images = reference_keys.shape[0]
    vmem = pl.BlockSpec(memory_space=pltpu.VMEM)
    hbm = pl.BlockSpec(memory_space=pl.ANY)
    dma = pltpu.SemaphoreType.DMA
    bf16 = jnp.bfloat16
    time_span = round_up(time_weight.shape[0], 64)
    conv_span = max(17 * ch // 8, 7 * ch // 8 + round_up(conv_weight.shape[0], 64))
    return pl.pallas_call(
        functools.partial(kernel, HEADS, images),
        out_shape=pltpu.VMEM(frames_in.shape, bf16),
        in_specs=[hbm, hbm, hbm, hbm, pl.BlockSpec(memory_space=pltpu.SMEM), hbm, hbm, hbm],
        out_specs=vmem,
        scratch_shapes=[
            pltpu.VMEM((rows, columns, ch), bf16),
            pltpu.VMEM(norm_gains.shape, jnp.float32),
            pltpu.VMEM((2, conv_span, ch), bf16),
            pltpu.VMEM((frame_count * time_span, ch), bf16),
            pltpu.VMEM((frame_count * attention_weight.shape[0], 4 * ch), bf16),
            pltpu.VMEM((3, QUAD, tokens + 2 * columns, ch), bf16),
            pltpu.VMEM((QUAD, tokens, ch), jnp.float32),
            pltpu.VMEM((QUAD, tokens, ch), bf16),
            pltpu.VMEM((QUAD, tokens, ch), bf16),
            pltpu.VMEM((LANES + 2, tokens, ch), bf16),
            pltpu.VMEM((2, tokens, ch), bf16),
            pltpu.VMEM((2, 2, tokens, ch), bf16),
            pltpu.VMEM((2, frame_count, 2, images, ch), bf16),
            pltpu.VMEM((tokens, ch), bf16),
            dma((7,)),
            dma((QUAD,)),
            dma((QUAD,)),
            dma((QUAD,)),
            dma((QUAD,)),
            dma((1,)),
            dma((2 * CHUNKS + 1,)),
            dma((2, QUAD)),
            dma((QUAD,)),
            dma((2, frame_count)),
            dma((2,)),
            dma((2,)),
            dma((5,)),
            dma((5,)),
            dma((8,)),
            dma((8,)),
            dma((2,)),
            dma((2,)),
        ],
        compiler_params=pltpu.CompilerParams(
            collective_id=0, has_side_effects=True, vmem_limit_bytes=60 * 2**20
        ),
    )(frames_in, norm_gains, reference_keys[:, 0], reference_values[:, 0], reference_pick, conv_weight, time_weight, attention_weight)


def on_device(sizes, *operands):
    frames_in, _, conv_weight, time_weight, attention_weight, keys, _, _ = operands
    count = sizes["frame"]
    rows, columns, channels = frames_in.shape[1:]
    share = channels // 8
    fits = (
        sizes["groups"] == 2 and sizes["row"] == 2 and count == 2 * QUAD
        and frames_in.shape[0] == 1 and rows == 2 and columns % 16 == 0 and keys.shape[1] == 1
        and channels == 64 * HEADS and HEADS % 2 == 0 and channels % 128 == 0 and conv_weight.shape[0] == 9 * share
        and time_weight.shape[0] == 3 * share and attention_weight.shape[0] == share
    )
    if fits:
        return by_kernel(count, *operands)
    return by_collectives(*operands)


def solution(mesh):
    return jax.shard_map(
        functools.partial(on_device, dict(mesh.shape)),
        mesh=mesh,
        in_specs=(
            P(("groups", "frame"), "row", None, None),
            P(),
            P("frame", None),
            P("frame", None),
            P("frame", None),
            P("groups", ("frame", "row"), None),
            P("groups", ("frame", "row"), None),
            P(("groups", "frame")),
        ),
        out_specs=P(("groups", "frame"), "row", None, None),
        check_vma=False,
    )
```

```python
import functools

import jax
import jax.numpy as jnp
from jax import lax
from jax.experimental import pallas as pl
from jax.experimental.pallas import tpu as pltpu
from jax.sharding import PartitionSpec as P

HEADS = 10
LANES = 2
QUAD = 4
CHUNKS = 3
MESH = pl.DeviceIdType.MESH


def padded_2(x, sides, width):
    for axis, dim in sides:
        devices, length = (lax.axis_size(axis), x.shape[dim])
        up = [(i, (i + 1) % devices) for i in range(devices - 1)]
        down = [(j, i) for i, j in up]
        last = lax.slice_in_dim(x, length - width, length, axis=dim)
        initial = lax.slice_in_dim(x, 0, width, axis=dim)
        before = lax.ppermute(last, axis, up)
        after = lax.ppermute(initial, axis, down)
        x = jnp.concatenate([before, x, after], axis=dim)
    return x


def normalize(values, gain):
    scale = lax.rsqrt(jnp.mean(values * values, axis=-1, keepdims=True) + 1e-05)
    return values * scale * gain


def heads_first(block, head_dim):
    split = block.reshape(block.shape[0], block.shape[1], HEADS, head_dim)
    return jnp.transpose(split, (2, 0, 1, 3))


def by_collectives(
    frames_in,
    norm_gains,
    conv_weight,
    time_weight,
    attention_weight,
    reference_keys,
    reference_values,
    reference_pick,
):
    local_frames, local_rows, columns, channels = frames_in.shape
    head_dim = channels // HEADS
    tokens = local_frames * local_rows * columns
    row_count = lax.axis_size("row")
    row_place = lax.axis_index("row")

    def halve(matrix):
        share = matrix.shape[1] // row_count
        return lax.dynamic_slice_in_dim(matrix, row_place * share, share, 1)

    conv_half, time_half, attention_half = (
        lax.all_gather(halve(conv_weight), "frame", axis=0, tiled=True),
        lax.all_gather(halve(time_weight), "frame", axis=0, tiled=True),
        lax.all_gather(halve(attention_weight), "frame", axis=0, tiled=True),
    )
    conv_full, time_full, attention_full = (
        lax.all_gather(conv_half, "row", axis=1, tiled=True),
        lax.all_gather(time_half, "row", axis=1, tiled=True),
        lax.all_gather(attention_half, "row", axis=1, tiled=True),
    )
    inputs = frames_in.astype(jnp.float32)
    activated = jax.nn.silu(normalize(inputs, norm_gains[0])).astype(jnp.bfloat16)
    padded = padded_2(activated, (("row", 1),), 1)
    padded = jnp.pad(padded, ((0, 0), (0, 0), (1, 1), (0, 0)))
    spatial = jnp.zeros((tokens, channels), jnp.float32)
    for offset_row in range(3):
        for offset_col in range(3):
            window = padded[
                :, offset_row : offset_row + local_rows, offset_col : offset_col + columns, :
            ].reshape(tokens, channels)
            row_start = (3 * offset_row + offset_col) * channels
            spatial = spatial + jnp.dot(
                window,
                conv_full[row_start : row_start + channels],
                preferred_element_type=jnp.float32,
            )
    hidden = (inputs + spatial.reshape(inputs.shape)).astype(jnp.bfloat16)
    hidden_wide = hidden.astype(jnp.float32)
    mixed = jax.nn.silu(normalize(hidden_wide, norm_gains[1])).astype(jnp.bfloat16)
    nearby = padded_2(mixed, (("frame", 0),), 1)
    temporal = jnp.zeros((tokens, channels), jnp.float32)
    for offset_frame in range(3):
        window = nearby[offset_frame : offset_frame + local_frames].reshape(tokens, channels)
        temporal = temporal + jnp.dot(
            window,
            time_full[offset_frame * channels : (offset_frame + 1) * channels],
            preferred_element_type=jnp.float32,
        )
    blended = (hidden_wide + temporal.reshape(inputs.shape)).astype(jnp.bfloat16)
    blended_wide = blended.astype(jnp.float32)
    normed = normalize(blended_wide, norm_gains[2]).astype(jnp.bfloat16).reshape(tokens, channels)
    projected = jnp.dot(
        normed, attention_full[:, : 3 * channels], preferred_element_type=jnp.float32
    ).astype(jnp.bfloat16)
    projected = projected.reshape(local_frames, local_rows * columns, 3 * channels)
    queries = projected[:, :, :channels]
    own_keys = projected[:, :, channels : 2 * channels]
    own_values = projected[:, :, 2 * channels :]
    frame_keys, frame_values = (
        lax.all_gather(own_keys, "row", axis=1, tiled=True),
        lax.all_gather(own_values, "row", axis=1, tiled=True),
    )
    cache_keys, cache_values = (
        lax.all_gather(reference_keys, ("frame", "row"), axis=1, tiled=True),
        lax.all_gather(reference_values, ("frame", "row"), axis=1, tiled=True),
    )
    picked_keys = jnp.take(cache_keys, reference_pick, axis=0)
    picked_values = jnp.take(cache_values, reference_pick, axis=0)
    keys_all = jnp.concatenate([frame_keys, picked_keys], axis=1)
    values_all = jnp.concatenate([frame_values, picked_values], axis=1)

    def one_head(operands):
        query_head, key_head, value_head = operands
        scores = jnp.einsum(
            "fqd,fkd->fqk", query_head, key_head, preferred_element_type=jnp.float32
        ) * head_dim ** (-0.5)
        ceiling = jnp.max(scores, axis=-1, keepdims=True)
        weights = jnp.exp(scores - ceiling)
        probs = (weights / jnp.sum(weights, axis=-1, keepdims=True)).astype(jnp.bfloat16)
        return jnp.einsum(
            "fqk,fkd->fqd", probs, value_head, preferred_element_type=jnp.float32
        ).astype(jnp.bfloat16)

    per_head = lax.map(
        one_head,
        (
            heads_first(queries, head_dim),
            heads_first(keys_all, head_dim),
            heads_first(values_all, head_dim),
        ),
    )
    attended = jnp.transpose(per_head, (1, 2, 0, 3)).reshape(tokens, channels)
    output = jnp.dot(
        attended, attention_full[:, 3 * channels :], preferred_element_type=jnp.float32
    )
    return (blended_wide + output.reshape(inputs.shape)).astype(jnp.bfloat16)


def round_up(value, unit):
    return -(-value // unit) * unit


def flip(frame, k):
    z, x = frame // LANES, frame % LANES
    kz, kx = k // LANES, k % LANES
    high = (z // 2 + kz // 2) % 2
    low = (z % 2 + kz % 2) % 2
    return (2 * high + low) * LANES + (x + kx) % 2


def kernel(
    heads, images,
    x_ref, gains_hbm, keys_ref, values_ref, pick_ref, conv_ref, time_ref, attn_ref,
    out_ref,
    x_own, gains_ref, conv_w, time_w, attn_w, shifted, part, partial_out, partial_in, mix, given, kv, cache, attended,
    local_sem, rows_send, act_recv, edge_recv, conv_send, conv_recv,
    lane_recv, cross_recv, other_recv, mate_recv, weight_send,
    sum_recv, misc_recv, cache_send, cache_recv,
):
    y, frame, r = lax.axis_index("groups"), lax.axis_index("frame"), lax.axis_index("row")
    frames = 2 * QUAD
    _, rows, columns, ch = x_ref.shape
    tokens = rows * columns
    head_dim = ch // heads
    share = ch // 8
    conv_rows, time_rows, attn_rows = conv_ref.shape[0], time_ref.shape[0], attn_ref.shape[0]
    conv_quarter = round_up(conv_rows, 64) // 4
    conv_first = conv_quarter // 2 // 16 * 16
    conv_last = max(conv_quarter // 6 // 16 * 16, 16)
    conv_chunks = (
        (0, conv_first), (conv_first, conv_quarter - conv_first - conv_last),
        (conv_quarter - conv_last, conv_last),
    )
    time_quarter = round_up(time_rows, 64) // 4
    time_span = 4 * time_quarter
    f32, bf16 = jnp.float32, jnp.bfloat16
    z, x = frame // LANES, frame % LANES
    depth = frames // LANES

    def slot_of(k):
        return (x + k % LANES) % LANES * 2 + (z + k // LANES) % 2

    own = slot_of(0)
    mine, theirs = 2 * y + r, 2 * (1 - y) + r
    mate = {"row": 1 - r}
    opposite = {"groups": 1 - y}

    def rows_at(start, size):
        return pl.ds(pl.multiple_of(start, 16), size)

    def at_frame(k):
        return {"frame": flip(frame, k)}

    def remote(src, dst, send_sem, recv_sem, to):
        return pltpu.make_async_remote_copy(
            src_ref=src, dst_ref=dst, send_sem=send_sem, recv_sem=recv_sem,
            device_id=to, device_id_type=MESH,
        )

    def await_bytes(ref, sem):
        pltpu.make_async_copy(ref, ref, sem).wait()

    def clear(slot, shard, covered, blocks):
        for i in range(blocks):
            start = i * share + jnp.where(i < shard, 0, covered)
            conv_w[slot, rows_at(start, share), :] = jnp.zeros((share, ch), bf16)

    early = [
        pltpu.make_async_copy(x_ref.at[0], x_own, local_sem.at[0]),
        pltpu.make_async_copy(gains_hbm, gains_ref, local_sem.at[6]),
    ]
    for f in early:
        f.start()
    partners = [at_frame(k) for k in range(1, frames)] + [mate, opposite]
    barrier = pltpu.get_barrier_semaphore()
    for to in partners:
        pl.semaphore_signal(barrier, inc=1, device_id=to, device_id_type=MESH)

    opposite_shard = flip(frame, 4)
    clear(0, frame, conv_rows, 8)
    fills = [
        pltpu.make_async_copy(conv_ref, conv_w.at[0, rows_at(frame * share, conv_rows)], local_sem.at[1]),
        pltpu.make_async_copy(time_ref, time_w.at[rows_at(frame * time_span, time_rows)], local_sem.at[2]),
        pltpu.make_async_copy(attn_ref, attn_w.at[rows_at(frame * attn_rows, attn_rows)], local_sem.at[3]),
        pltpu.make_async_copy(keys_ref, cache.at[r, frame, 0], local_sem.at[4]),
        pltpu.make_async_copy(values_ref, cache.at[r, frame, 1], local_sem.at[5]),
    ]
    for f in fills:
        f.start()
    clear(1, opposite_shard, 4 * conv_quarter, 7)
    if time_span > time_rows:
        gap = time_span - time_rows
        time_w[rows_at(frame * time_span + time_rows, gap), :] = jnp.zeros((gap, ch), bf16)
    shifted[1, :, rows_at(r * (rows + 1) * columns, columns), :] = jnp.zeros((QUAD, columns, ch), bf16)

    def act(v, g):
        n = normalize(v, gains_ref[g:g + 1, :])
        return n / (1.0 + jnp.exp(-n))

    for f in early:
        f.wait()
    own_x = x_own[...].reshape(tokens, ch).astype(f32)
    shifted[1, own, columns:columns + tokens, :] = act(own_x, 0).astype(bf16)
    pl.semaphore_wait(barrier, len(partners))

    def act_copy(k):
        ref = shifted.at[1, own if k < 3 else slot_of(1), columns:columns + tokens]
        return remote(ref, ref, rows_send.at[0], act_recv.at[k - 1], at_frame(min(k, 2)))

    def edge(k):
        slot = slot_of(k)
        return remote(
            shifted.at[1, slot, rows_at(rows * columns - r * (rows - 1) * columns, columns)],
            shifted.at[1, slot, rows_at(r * (rows + 1) * columns, columns)],
            rows_send.at[0], edge_recv.at[k], mate,
        )

    def edge_wait(k):
        slot = slot_of(k)
        await_bytes(shifted.at[1, slot, rows_at((1 - r) * (rows + 1) * columns, columns)], edge_recv.at[k])

    def conv_part(slot, shard, q, i):
        first, count = conv_chunks[i]
        return conv_w.at[slot, rows_at(shard * share + q * conv_quarter + first, count)]

    def send_conv(slot, shard, q, i, recv, to):
        remote(
            conv_part(slot, shard, q, i), conv_part(1, shard, q, i),
            conv_send.at[0], conv_recv.at[recv], to,
        ).start()

    def conv_from_lane(i):
        await_bytes(conv_part(1, opposite_shard, mine, i), conv_recv.at[i])
        send_conv(1, opposite_shard, mine, i, CHUNKS + i, opposite)
        send_conv(1, opposite_shard, mine, i, 2 * CHUNKS, mate)

    def conv_from_other(i):
        await_bytes(conv_part(1, opposite_shard, theirs, i), conv_recv.at[CHUNKS + i])
        send_conv(1, opposite_shard, theirs, i, 2 * CHUNKS, mate)

    def conv_from_mate():
        await_bytes(conv_w.at[1, 0:2 * conv_quarter], conv_recv.at[2 * CHUNKS])

    def time_part(d, q, count=1):
        return time_w.at[rows_at(d * time_span + q * time_quarter, count * time_quarter)]

    def attn_part(d, q, count=1):
        return attn_w.at[rows_at(d * attn_rows, attn_rows), pl.ds(pl.multiple_of(q * ch, 128), count * ch)]

    def pieces(w):
        return time_part if w == 0 else attn_part

    def send_weight(w, ref, recv_sem, to):
        remote(ref, ref, weight_send.at[w], recv_sem, to).start()

    def weights_across():
        send_weight(1, attn_part(frame, 2 * r, 2), cross_recv.at[0], at_frame(1))

    def weights_along(w, k):
        send_weight(w, pieces(w)(frame, mine), lane_recv.at[3 * w + k - 1], at_frame(2 * k))

    def other_place(w, k):
        return k // 2 - 1 if w == 0 else k + 1

    def from_lane(w, k):
        ref = pieces(w)(flip(frame, 2 * k), mine)
        await_bytes(ref, lane_recv.at[3 * w + k - 1])
        if w == 1:
            send_weight(w, ref, cross_recv.at[k], at_frame(1))
        if w == 0 or k != 2:
            send_weight(w, ref, other_recv.at[other_place(w, 2 * k)], opposite)
        send_weight(w, ref, mate_recv.at[w], mate)

    def relay_lane(w):
        send_weight(w, pieces(w)(flip(frame, 6), mine), lane_recv.at[3 * w + 1], at_frame(2))

    def from_cross(k):
        ref = attn_part(flip(frame, 1), 2 * r, 2) if k == 0 else attn_part(flip(frame, 2 * k + 1), mine)
        await_bytes(ref, cross_recv.at[k])
        if k % 2 == 1:
            send_weight(1, ref, other_recv.at[other_place(1, 2 * k + 1)], opposite)
        send_weight(1, ref, mate_recv.at[1], mate)

    def from_other(w, k):
        ref = pieces(w)(flip(frame, k), theirs)
        await_bytes(ref, other_recv.at[other_place(w, k)])
        if w == 1 and k >= 6:
            send_weight(w, ref, other_recv.at[other_place(w, k - 2)], at_frame(2))
        send_weight(w, ref, mate_recv.at[w], mate)

    def weight_bytes(w, quarters):
        if w == 0:
            return time_w.at[0:quarters * time_quarter]
        return attn_w.at[0:quarters * attn_rows // 2, 0:2 * ch]

    def from_mate(w):
        await_bytes(weight_bytes(w, (6, 14)[w]), mate_recv.at[w])

    def weights_sent(w):
        if w == 0:
            await_bytes(time_w.at[0:12 * time_quarter], weight_send.at[w])
        else:
            await_bytes(attn_w.at[0:7 * attn_rows], weight_send.at[w])

    def exchange(src, dst, k, to, sender=0):
        return remote(src, dst, rows_send.at[sender], misc_recv.at[k], to)

    def share_refs(k):
        return remote(cache.at[r, frame], cache.at[r, frame], cache_send.at[0], cache_recv.at[0], at_frame(k))

    act_copy(1).start()
    act_copy(2).start()
    edge(0).start()
    fills[0].wait()
    for i in range(CHUNKS):
        send_conv(0, frame, mine, i, i, at_frame(4))
    for f in fills[1:]:
        f.wait()

    def from_quad(k):
        slot = slot_of(k)
        await_bytes(shifted.at[1, slot, columns:columns + tokens], act_recv.at[k - 1])
        if k == 1:
            act_copy(3).start()
        edge(k).start()

    for k in range(1, frames, 2):
        time_w[rows_at(flip(frame, k) * time_span, time_span), :] = jnp.zeros((time_span, ch), bf16)

    from_quad(1)
    from_quad(2)
    conv_from_lane(0)
    conv_from_lane(1)
    from_quad(3)
    weights_across()
    weights_along(0, 3)
    weights_along(0, 1)
    weights_along(1, 3)
    conv_from_lane(2)

    blank = jnp.zeros((1, ch), f32)

    def shift(k):
        slot = slot_of(k)
        edge_wait(k)
        for i in range(rows + 2):
            span = slice(i * columns, (i + 1) * columns)
            row = shifted[1, slot, span, :].astype(f32)
            shifted[0, slot, span, :] = jnp.concatenate([blank, row[:columns - 1]], axis=0).astype(bf16)
            shifted[2, slot, span, :] = jnp.concatenate([row[1:], blank], axis=0).astype(bf16)

    for k in range(QUAD):
        shift(k)

    def windows(shard, j, slot=None):
        tap = shard + j
        dy, dx = tap // 3, tap % 3
        if slot is None:
            return shifted[dx, :, rows_at(dy * columns, tokens), :].reshape(QUAD * tokens, ch)
        return shifted[dx, pl.ds(slot, LANES), rows_at(dy * columns, tokens), :].reshape(LANES * tokens, ch)

    def partial_sum(slot, shard, j, place=None):
        return jnp.dot(windows(shard, j, place), conv_w[slot, j * ch:(j + 1) * ch, :], preferred_element_type=f32)

    part[...] = (partial_sum(0, frame, 0) + partial_sum(0, frame, 1)).reshape(QUAD, tokens, ch)

    for i in range(CHUNKS):
        conv_from_other(i)
    conv_from_mate()
    def pair_sum(pair):
        return part[pl.ds(pair, 2)] + (
            partial_sum(1, opposite_shard, 0, pair) + partial_sum(1, opposite_shard, 1, pair)
        ).reshape(2, tokens, ch)

    halves = [slice(0, tokens // 2), slice(tokens // 2, tokens)]
    partial_out[pl.ds(2 * (1 - x), 2)] = pair_sum(2 * (1 - x)).astype(bf16)
    across = [
        remote(partial_out.at[slot_of(3), half], partial_in.at[0, half], rows_send.at[0], sum_recv.at[h], at_frame(1))
        for h, half in enumerate(halves)]
    across.append(remote(partial_out.at[slot_of(1)], partial_in.at[1], rows_send.at[0], sum_recv.at[2], at_frame(1)))
    for c in across:
        c.start()
    part[pl.ds(2 * x, 2)] = pair_sum(2 * x)
    from_lane(0, 3)
    relay_lane(0)
    weights_along(1, 1)
    from_lane(0, 1)
    along = [
        remote(partial_out.at[slot_of(2), half], partial_in.at[2, half], rows_send.at[0], sum_recv.at[3 + h], at_frame(2))
        for h, half in enumerate(halves)]
    for h, half in enumerate(halves):
        await_bytes(partial_in.at[0, half], sum_recv.at[h])
        partial_out[slot_of(2), half] = (part[slot_of(2), half] + partial_in[0, half].astype(f32)).astype(bf16)
        along[h].start()
    from_lane(1, 3)
    relay_lane(1)
    for k in range(1, frames):
        share_refs(k).start()
    from_lane(0, 2)
    from_lane(1, 1)
    from_cross(0)

    await_bytes(partial_in.at[1], sum_recv.at[2])
    total = own_x + part[own] + partial_in[1].astype(f32)
    for h, half in enumerate(halves):
        await_bytes(partial_in.at[2, half], sum_recv.at[3 + h])
    total = total + partial_in[2].astype(f32)
    hidden = total.astype(bf16).astype(f32)
    mix[1 + x] = act(hidden, 1).astype(bf16)

    gives = jnp.where(x == 0, z > 0, z < depth - 1)
    takes = jnp.where(x == 0, z < depth - 1, z > 0)
    far = mix.at[3 * (1 - x)]
    beside = [exchange(mix.at[1 + x, half], mix.at[1 + x, half], 1 + 5 * h, at_frame(1)) for h, half in enumerate(halves)]
    beyond = exchange(mix.at[1 + x], far, 2, {"frame": jnp.clip(frame + 4 * x - 2, 0, frames - 1)}, 1)
    past = {"frame": jnp.clip(frame + 2 - 4 * x, 0, frames - 1)}
    passed = [exchange(mix.at[2 - x, half], mix.at[3 * x, half], 4 + 3 * h, past, 2) for h, half in enumerate(halves)]

    @pl.when(gives)
    def _():
        beyond.start()

    for c in beside:
        c.start()

    @pl.when(z == 0)
    def _():
        mix[0] = jnp.zeros((tokens, ch), bf16)

    @pl.when(z == depth - 1)
    def _():
        mix[3] = jnp.zeros((tokens, ch), bf16)

    from_other(1, 6)
    from_cross(3)
    from_other(0, 6)
    from_other(0, 2)
    from_cross(1)
    from_lane(1, 2)
    from_other(0, 4)
    from_other(1, 2)
    await_bytes(mix.at[2 - x, halves[0]], misc_recv.at[1])

    @pl.when(takes)
    def _():
        passed[0].start()

    await_bytes(mix.at[2 - x, halves[1]], misc_recv.at[6])

    @pl.when(takes)
    def _():
        passed[1].start()

    from_other(1, 7)
    from_mate(0)

    def time_rows_of(t):
        found = []
        at, left = t * ch, ch
        while left:
            shard, inside = at // time_rows, at % time_rows
            count = min(time_rows - inside, left)
            found.append(time_w[shard * time_span + inside:shard * time_span + inside + count, :])
            at, left = at + count, left - count
        return jnp.concatenate(found, axis=0)

    def temporal(lane):
        total = jnp.dot(mix[lane + 1], time_rows_of(1), preferred_element_type=f32)
        total = total + jnp.dot(mix[lane], time_rows_of(0), preferred_element_type=f32)
        return total + jnp.dot(mix[lane + 2], time_rows_of(2), preferred_element_type=f32)

    @pl.when(takes)
    def _():
        beyond.wait_recv()

    given[0] = temporal(1 - x).astype(bf16)
    temporal_swap = exchange(given.at[0], given.at[1], 5, at_frame(1))
    temporal_swap.start()
    from_cross(2)
    from_other(1, 4)
    from_other(1, 3)
    await_bytes(cache.at[r, 0:frames - 1], cache_recv.at[0])
    cache_mate = remote(cache.at[r], cache.at[r], cache_send.at[1], cache_recv.at[1], mate)
    cache_mate.start()

    @pl.when(gives)
    def _():
        for h, half in enumerate(halves):
            await_bytes(mix.at[3 * x, half], misc_recv.at[4 + 3 * h])

    own_temporal = temporal(x)
    from_other(1, 5)
    await_bytes(cache.at[1 - r], cache_recv.at[1])
    pick = pick_ref[0]
    cached = cache[...].astype(f32).reshape(2 * frames, 2, images, ch)
    picked_keys = jnp.zeros((2 * frames, ch), f32)
    picked_values = jnp.zeros((2 * frames, ch), f32)
    for i in range(images):
        picked_keys = jnp.where(pick == i, cached[:, 0, i, :], picked_keys)
        picked_values = jnp.where(pick == i, cached[:, 1, i, :], picked_values)
    picked_keys, picked_values = picked_keys.astype(bf16), picked_values.astype(bf16)
    temporal_swap.wait_recv()
    total = hidden + own_temporal + given[1].astype(f32)
    blended = total.astype(bf16).astype(f32)
    normed = normalize(blended, gains_ref[2:3, :]).astype(bf16)
    from_mate(1)
    own_keys, own_values = kv.at[0, r], kv.at[1, r]
    own_keys[...] = jnp.dot(normed, attn_w[:, ch:2 * ch], preferred_element_type=f32).astype(bf16)
    swap_keys = exchange(own_keys, own_keys, 0, mate)
    swap_keys.start()
    own_values[...] = jnp.dot(normed, attn_w[:, 2 * ch:3 * ch], preferred_element_type=f32).astype(bf16)
    swap_values = exchange(own_values, own_values, 3, mate)
    swap_values.start()
    queries = jnp.dot(normed, attn_w[:, :ch], preferred_element_type=f32).astype(bf16) * head_dim ** (-0.5)
    first_head = lax.broadcasted_iota(jnp.int32, (tokens, 2 * head_dim), 1) < head_dim
    none = jnp.zeros((tokens, 2 * head_dim), bf16)
    ones = jnp.ones((2 * (tokens + frames), 2 * head_dim), bf16)
    pairs = [slice(2 * h * head_dim, 2 * (h + 1) * head_dim) for h in range(heads // 2)]
    await_bytes(kv.at[0, 1 - r], misc_recv.at[0])
    weights = []
    for at in pairs:
        both = jnp.concatenate([
            jnp.where(first_head, queries[:, at], none), jnp.where(first_head, none, queries[:, at]),
        ], axis=0)
        keys = jnp.concatenate([kv[0, 0, :, at], kv[0, 1, :, at], picked_keys[:, at]], axis=0)
        scores = lax.dot_general(both, keys, (((1,), (1,)), ((), ())), preferred_element_type=f32)
        weights.append(jnp.exp(scores - jnp.max(scores, axis=-1, keepdims=True)).astype(bf16))
    await_bytes(kv.at[1, 1 - r], misc_recv.at[3])
    for at, probs in zip(pairs, weights):
        values = jnp.concatenate([kv[1, 0, :, at], kv[1, 1, :, at], picked_values[:, at]], axis=0)
        mixed = jnp.dot(probs, jnp.concatenate([values, ones], axis=1), preferred_element_type=f32)
        mixed = mixed[:, :2 * head_dim] / mixed[:, 2 * head_dim:]
        attended[:, at] = jnp.where(first_head, mixed[:tokens], mixed[tokens:]).astype(bf16)
    result = blended + jnp.dot(attended[...], attn_w[:, 3 * ch:], preferred_element_type=f32)
    out_ref[0] = result.astype(bf16).reshape(rows, columns, ch)

    await_bytes(conv_w.at[0:2, 0:6 * tokens], rows_send.at[0])
    await_bytes(conv_w.at[0, 0:4 * conv_quarter], conv_send.at[0])
    await_bytes(cache.at[r, 0:frames - 1], cache_send.at[0])
    cache_mate.wait_send()
    weights_sent(0)
    weights_sent(1)

    @pl.when(gives)
    def _():
        beyond.wait_send()

    @pl.when(takes)
    def _():
        await_bytes(mix.at[0], rows_send.at[2])


def by_kernel(
    frame_count, frames_in, norm_gains, conv_weight, time_weight, attention_weight,
    reference_keys, reference_values, reference_pick,
):
    _, rows, columns, ch = frames_in.shape
    tokens = rows * columns
    images = reference_keys.shape[0]
    vmem = pl.BlockSpec(memory_space=pltpu.VMEM)
    hbm = pl.BlockSpec(memory_space=pl.ANY)
    dma = pltpu.SemaphoreType.DMA
    bf16 = jnp.bfloat16
    time_span = round_up(time_weight.shape[0], 64)
    conv_span = max(17 * ch // 8, 7 * ch // 8 + round_up(conv_weight.shape[0], 64))
    return pl.pallas_call(
        functools.partial(kernel, HEADS, images),
        out_shape=pltpu.VMEM(frames_in.shape, bf16),
        in_specs=[hbm, hbm, hbm, hbm, pl.BlockSpec(memory_space=pltpu.SMEM), hbm, hbm, hbm],
        out_specs=vmem,
        scratch_shapes=[
            pltpu.VMEM((rows, columns, ch), bf16),
            pltpu.VMEM(norm_gains.shape, jnp.float32),
            pltpu.VMEM((2, conv_span, ch), bf16),
            pltpu.VMEM((frame_count * time_span, ch), bf16),
            pltpu.VMEM((frame_count * attention_weight.shape[0], 4 * ch), bf16),
            pltpu.VMEM((3, QUAD, tokens + 2 * columns, ch), bf16),
            pltpu.VMEM((QUAD, tokens, ch), jnp.float32),
            pltpu.VMEM((QUAD, tokens, ch), bf16),
            pltpu.VMEM((QUAD, tokens, ch), bf16),
            pltpu.VMEM((LANES + 2, tokens, ch), bf16),
            pltpu.VMEM((2, tokens, ch), bf16),
            pltpu.VMEM((2, 2, tokens, ch), bf16),
            pltpu.VMEM((2, frame_count, 2, images, ch), bf16),
            pltpu.VMEM((tokens, ch), bf16),
            dma((7,)),
            dma((3,)),
            dma((QUAD - 1,)),
            dma((QUAD,)),
            dma((1,)),
            dma((2 * CHUNKS + 1,)),
            dma((6,)),
            dma((QUAD,)),
            dma((9,)),
            dma((2,)),
            dma((2,)),
            dma((5,)),
            dma((8,)),
            dma((2,)),
            dma((2,)),
        ],
        compiler_params=pltpu.CompilerParams(
            collective_id=0, has_side_effects=True, vmem_limit_bytes=60 * 2**20
        ),
    )(frames_in, norm_gains, reference_keys[:, 0], reference_values[:, 0], reference_pick, conv_weight, time_weight, attention_weight)


def on_device(sizes, *operands):
    frames_in, _, conv_weight, time_weight, attention_weight, keys, _, _ = operands
    count = sizes["frame"]
    rows, columns, channels = frames_in.shape[1:]
    share = channels // 8
    fits = (
        sizes["groups"] == 2 and sizes["row"] == 2 and count == 2 * QUAD
        and frames_in.shape[0] == 1 and rows == 2 and columns % 16 == 0 and keys.shape[1] == 1
        and channels == 64 * HEADS and HEADS % 2 == 0 and channels % 128 == 0 and conv_weight.shape[0] == 9 * share
        and time_weight.shape[0] == 3 * share and attention_weight.shape[0] == share
    )
    if fits:
        return by_kernel(count, *operands)
    return by_collectives(*operands)


def solution(mesh):
    return jax.shard_map(
        functools.partial(on_device, dict(mesh.shape)),
        mesh=mesh,
        in_specs=(
            P(("groups", "frame"), "row", None, None),
            P(),
            P("frame", None),
            P("frame", None),
            P("frame", None),
            P("groups", ("frame", "row"), None),
            P("groups", ("frame", "row"), None),
            P(("groups", "frame")),
        ),
        out_specs=P(("groups", "frame"), "row", None, None),
        check_vma=False,
    )
```

```python
import functools

import jax
import jax.numpy as jnp
from jax import lax
from jax.experimental import pallas as pl
from jax.experimental.pallas import tpu as pltpu
from jax.sharding import PartitionSpec as P

HEADS = 10
LANES = 2
QUAD = 4
CHUNKS = 3
MESH = pl.DeviceIdType.MESH


def padded_2(x, sides, width):
    for axis, dim in sides:
        devices, length = (lax.axis_size(axis), x.shape[dim])
        up = [(i, (i + 1) % devices) for i in range(devices - 1)]
        down = [(j, i) for i, j in up]
        last = lax.slice_in_dim(x, length - width, length, axis=dim)
        initial = lax.slice_in_dim(x, 0, width, axis=dim)
        before = lax.ppermute(last, axis, up)
        after = lax.ppermute(initial, axis, down)
        x = jnp.concatenate([before, x, after], axis=dim)
    return x


def normalize(values, gain):
    scale = lax.rsqrt(jnp.mean(values * values, axis=-1, keepdims=True) + 1e-05)
    return values * scale * gain


def heads_first(block, head_dim):
    split = block.reshape(block.shape[0], block.shape[1], HEADS, head_dim)
    return jnp.transpose(split, (2, 0, 1, 3))


def by_collectives(
    frames_in,
    norm_gains,
    conv_weight,
    time_weight,
    attention_weight,
    reference_keys,
    reference_values,
    reference_pick,
):
    local_frames, local_rows, columns, channels = frames_in.shape
    head_dim = channels // HEADS
    tokens = local_frames * local_rows * columns
    row_count = lax.axis_size("row")
    row_place = lax.axis_index("row")

    def halve(matrix):
        share = matrix.shape[1] // row_count
        return lax.dynamic_slice_in_dim(matrix, row_place * share, share, 1)

    conv_half, time_half, attention_half = (
        lax.all_gather(halve(conv_weight), "frame", axis=0, tiled=True),
        lax.all_gather(halve(time_weight), "frame", axis=0, tiled=True),
        lax.all_gather(halve(attention_weight), "frame", axis=0, tiled=True),
    )
    conv_full, time_full, attention_full = (
        lax.all_gather(conv_half, "row", axis=1, tiled=True),
        lax.all_gather(time_half, "row", axis=1, tiled=True),
        lax.all_gather(attention_half, "row", axis=1, tiled=True),
    )
    inputs = frames_in.astype(jnp.float32)
    activated = jax.nn.silu(normalize(inputs, norm_gains[0])).astype(jnp.bfloat16)
    padded = padded_2(activated, (("row", 1),), 1)
    padded = jnp.pad(padded, ((0, 0), (0, 0), (1, 1), (0, 0)))
    spatial = jnp.zeros((tokens, channels), jnp.float32)
    for offset_row in range(3):
        for offset_col in range(3):
            window = padded[
                :, offset_row : offset_row + local_rows, offset_col : offset_col + columns, :
            ].reshape(tokens, channels)
            row_start = (3 * offset_row + offset_col) * channels
            spatial = spatial + jnp.dot(
                window,
                conv_full[row_start : row_start + channels],
                preferred_element_type=jnp.float32,
            )
    hidden = (inputs + spatial.reshape(inputs.shape)).astype(jnp.bfloat16)
    hidden_wide = hidden.astype(jnp.float32)
    mixed = jax.nn.silu(normalize(hidden_wide, norm_gains[1])).astype(jnp.bfloat16)
    nearby = padded_2(mixed, (("frame", 0),), 1)
    temporal = jnp.zeros((tokens, channels), jnp.float32)
    for offset_frame in range(3):
        window = nearby[offset_frame : offset_frame + local_frames].reshape(tokens, channels)
        temporal = temporal + jnp.dot(
            window,
            time_full[offset_frame * channels : (offset_frame + 1) * channels],
            preferred_element_type=jnp.float32,
        )
    blended = (hidden_wide + temporal.reshape(inputs.shape)).astype(jnp.bfloat16)
    blended_wide = blended.astype(jnp.float32)
    normed = normalize(blended_wide, norm_gains[2]).astype(jnp.bfloat16).reshape(tokens, channels)
    projected = jnp.dot(
        normed, attention_full[:, : 3 * channels], preferred_element_type=jnp.float32
    ).astype(jnp.bfloat16)
    projected = projected.reshape(local_frames, local_rows * columns, 3 * channels)
    queries = projected[:, :, :channels]
    own_keys = projected[:, :, channels : 2 * channels]
    own_values = projected[:, :, 2 * channels :]
    frame_keys, frame_values = (
        lax.all_gather(own_keys, "row", axis=1, tiled=True),
        lax.all_gather(own_values, "row", axis=1, tiled=True),
    )
    cache_keys, cache_values = (
        lax.all_gather(reference_keys, ("frame", "row"), axis=1, tiled=True),
        lax.all_gather(reference_values, ("frame", "row"), axis=1, tiled=True),
    )
    picked_keys = jnp.take(cache_keys, reference_pick, axis=0)
    picked_values = jnp.take(cache_values, reference_pick, axis=0)
    keys_all = jnp.concatenate([frame_keys, picked_keys], axis=1)
    values_all = jnp.concatenate([frame_values, picked_values], axis=1)

    def one_head(operands):
        query_head, key_head, value_head = operands
        scores = jnp.einsum(
            "fqd,fkd->fqk", query_head, key_head, preferred_element_type=jnp.float32
        ) * head_dim ** (-0.5)
        ceiling = jnp.max(scores, axis=-1, keepdims=True)
        weights = jnp.exp(scores - ceiling)
        probs = (weights / jnp.sum(weights, axis=-1, keepdims=True)).astype(jnp.bfloat16)
        return jnp.einsum(
            "fqk,fkd->fqd", probs, value_head, preferred_element_type=jnp.float32
        ).astype(jnp.bfloat16)

    per_head = lax.map(
        one_head,
        (
            heads_first(queries, head_dim),
            heads_first(keys_all, head_dim),
            heads_first(values_all, head_dim),
        ),
    )
    attended = jnp.transpose(per_head, (1, 2, 0, 3)).reshape(tokens, channels)
    output = jnp.dot(
        attended, attention_full[:, 3 * channels :], preferred_element_type=jnp.float32
    )
    return (blended_wide + output.reshape(inputs.shape)).astype(jnp.bfloat16)


def round_up(value, unit):
    return -(-value // unit) * unit


def flip(frame, k):
    z, x = frame // LANES, frame % LANES
    kz, kx = k // LANES, k % LANES
    high = (z // 2 + kz // 2) % 2
    low = (z % 2 + kz % 2) % 2
    return (2 * high + low) * LANES + (x + kx) % 2


def kernel(
    heads, images,
    x_ref, gains_hbm, keys_ref, values_ref, pick_ref, conv_ref, time_ref, attn_ref,
    out_ref,
    x_own, gains_ref, conv_w, time_w, attn_w, shifted, part, partial_out, partial_in, mix, given, kv, cache, attended,
    local_sem, rows_send, act_recv, edge_recv, conv_send, conv_recv,
    lane_recv, cross_recv, other_recv, mate_recv, weight_send,
    sum_recv, misc_recv, cache_send, cache_recv,
):
    y, frame, r = lax.axis_index("groups"), lax.axis_index("frame"), lax.axis_index("row")
    frames = 2 * QUAD
    _, rows, columns, ch = x_ref.shape
    tokens = rows * columns
    head_dim = ch // heads
    share = ch // 8
    conv_rows, time_rows, attn_rows = conv_ref.shape[0], time_ref.shape[0], attn_ref.shape[0]
    conv_quarter = round_up(conv_rows, 64) // 4
    conv_first = conv_quarter // 2 // 16 * 16
    conv_last = max(conv_quarter // 6 // 16 * 16, 16)
    conv_chunks = (
        (0, conv_first), (conv_first, conv_quarter - conv_first - conv_last),
        (conv_quarter - conv_last, conv_last),
    )
    time_quarter = round_up(time_rows, 64) // 4
    time_span = 4 * time_quarter
    f32, bf16 = jnp.float32, jnp.bfloat16
    z, x = frame // LANES, frame % LANES
    depth = frames // LANES

    def slot_of(k):
        return (x + k % LANES) % LANES * 2 + (z + k // LANES) % 2

    own = slot_of(0)
    mine, theirs = 2 * y + r, 2 * (1 - y) + r
    mate = {"row": 1 - r}
    opposite = {"groups": 1 - y}

    def rows_at(start, size):
        return pl.ds(pl.multiple_of(start, 16), size)

    def at_frame(k):
        return {"frame": flip(frame, k)}

    def remote(src, dst, send_sem, recv_sem, to):
        return pltpu.make_async_remote_copy(
            src_ref=src, dst_ref=dst, send_sem=send_sem, recv_sem=recv_sem,
            device_id=to, device_id_type=MESH,
        )

    def await_bytes(ref, sem):
        pltpu.make_async_copy(ref, ref, sem).wait()

    def clear(slot, shard, covered, blocks):
        for i in range(blocks):
            start = i * share + jnp.where(i < shard, 0, covered)
            conv_w[slot, rows_at(start, share), :] = jnp.zeros((share, ch), bf16)

    early = [
        pltpu.make_async_copy(x_ref.at[0], x_own, local_sem.at[0]),
        pltpu.make_async_copy(gains_hbm, gains_ref, local_sem.at[6]),
    ]
    for f in early:
        f.start()
    partners = [at_frame(k) for k in range(1, frames)] + [mate, opposite]
    barrier = pltpu.get_barrier_semaphore()
    for to in partners:
        pl.semaphore_signal(barrier, inc=1, device_id=to, device_id_type=MESH)

    opposite_shard = flip(frame, 4)
    clear(0, frame, conv_rows, 8)
    fills = [
        pltpu.make_async_copy(conv_ref, conv_w.at[0, rows_at(frame * share, conv_rows)], local_sem.at[1]),
        pltpu.make_async_copy(time_ref, time_w.at[rows_at(frame * time_span, time_rows)], local_sem.at[2]),
        pltpu.make_async_copy(attn_ref, attn_w.at[rows_at(frame * attn_rows, attn_rows)], local_sem.at[3]),
        pltpu.make_async_copy(keys_ref, cache.at[r, frame, 0], local_sem.at[4]),
        pltpu.make_async_copy(values_ref, cache.at[r, frame, 1], local_sem.at[5]),
    ]
    for f in fills:
        f.start()
    clear(1, opposite_shard, 4 * conv_quarter, 7)
    if time_span > time_rows:
        gap = time_span - time_rows
        time_w[rows_at(frame * time_span + time_rows, gap), :] = jnp.zeros((gap, ch), bf16)
    shifted[1, :, rows_at(r * (rows + 1) * columns, columns), :] = jnp.zeros((QUAD, columns, ch), bf16)

    def act(v, g):
        n = normalize(v, gains_ref[g:g + 1, :])
        return n / (1.0 + jnp.exp(-n))

    for f in early:
        f.wait()
    own_x = x_own[...].reshape(tokens, ch).astype(f32)
    shifted[1, own, columns:columns + tokens, :] = act(own_x, 0).astype(bf16)
    pl.semaphore_wait(barrier, len(partners))

    def act_copy(k):
        ref = shifted.at[1, own if k < 3 else slot_of(1), columns:columns + tokens]
        return remote(ref, ref, rows_send.at[0], act_recv.at[k - 1], at_frame(min(k, 2)))

    def edge(k):
        slot = slot_of(k)
        return remote(
            shifted.at[1, slot, rows_at(rows * columns - r * (rows - 1) * columns, columns)],
            shifted.at[1, slot, rows_at(r * (rows + 1) * columns, columns)],
            rows_send.at[0], edge_recv.at[k], mate,
        )

    def edge_wait(k):
        slot = slot_of(k)
        await_bytes(shifted.at[1, slot, rows_at((1 - r) * (rows + 1) * columns, columns)], edge_recv.at[k])

    def conv_part(slot, shard, q, i):
        first, count = conv_chunks[i]
        return conv_w.at[slot, rows_at(shard * share + q * conv_quarter + first, count)]

    def send_conv(slot, shard, q, i, recv, to):
        remote(
            conv_part(slot, shard, q, i), conv_part(1, shard, q, i),
            conv_send.at[0], conv_recv.at[recv], to,
        ).start()

    def conv_from_lane(i):
        await_bytes(conv_part(1, opposite_shard, mine, i), conv_recv.at[i])
        send_conv(1, opposite_shard, mine, i, CHUNKS + i, opposite)
        send_conv(1, opposite_shard, mine, i, 2 * CHUNKS, mate)

    def conv_from_other(i):
        await_bytes(conv_part(1, opposite_shard, theirs, i), conv_recv.at[CHUNKS + i])
        send_conv(1, opposite_shard, theirs, i, 2 * CHUNKS, mate)

    def conv_from_mate():
        await_bytes(conv_w.at[1, 0:2 * conv_quarter], conv_recv.at[2 * CHUNKS])

    def time_part(d, q, count=1):
        return time_w.at[rows_at(d * time_span + q * time_quarter, count * time_quarter)]

    def attn_part(d, q, count=1):
        return attn_w.at[rows_at(d * attn_rows, attn_rows), pl.ds(pl.multiple_of(q * ch, 128), count * ch)]

    def pieces(w):
        return time_part if w == 0 else attn_part

    def send_weight(w, ref, recv_sem, to):
        remote(ref, ref, weight_send.at[w], recv_sem, to).start()

    def weights_across():
        send_weight(1, attn_part(frame, 2 * r, 2), cross_recv.at[0], at_frame(1))

    def weights_along(w, k):
        send_weight(w, pieces(w)(frame, mine), lane_recv.at[3 * w + k - 1], at_frame(2 * k))

    def other_place(w, k):
        return k // 2 - 1 if w == 0 else k + 1

    def from_lane(w, k):
        ref = pieces(w)(flip(frame, 2 * k), mine)
        await_bytes(ref, lane_recv.at[3 * w + k - 1])
        if w == 1:
            send_weight(w, ref, cross_recv.at[k], at_frame(1))
        if w == 0 or k != 2:
            send_weight(w, ref, other_recv.at[other_place(w, 2 * k)], opposite)
        send_weight(w, ref, mate_recv.at[w], mate)

    def relay_lane(w):
        send_weight(w, pieces(w)(flip(frame, 6), mine), lane_recv.at[3 * w + 1], at_frame(2))

    def from_cross(k):
        ref = attn_part(flip(frame, 1), 2 * r, 2) if k == 0 else attn_part(flip(frame, 2 * k + 1), mine)
        await_bytes(ref, cross_recv.at[k])
        if k % 2 == 1:
            send_weight(1, ref, other_recv.at[other_place(1, 2 * k + 1)], opposite)
        send_weight(1, ref, mate_recv.at[1], mate)

    def from_other(w, k):
        ref = pieces(w)(flip(frame, k), theirs)
        await_bytes(ref, other_recv.at[other_place(w, k)])
        if w == 1 and k >= 6:
            send_weight(w, ref, other_recv.at[other_place(w, k - 2)], at_frame(2))
        send_weight(w, ref, mate_recv.at[w], mate)

    def weight_bytes(w, quarters):
        if w == 0:
            return time_w.at[0:quarters * time_quarter]
        return attn_w.at[0:quarters * attn_rows // 2, 0:2 * ch]

    def from_mate(w):
        await_bytes(weight_bytes(w, (6, 14)[w]), mate_recv.at[w])

    def weights_sent(w):
        if w == 0:
            await_bytes(time_w.at[0:12 * time_quarter], weight_send.at[w])
        else:
            await_bytes(attn_w.at[0:7 * attn_rows], weight_send.at[w])

    def exchange(src, dst, k, to, sender=0):
        return remote(src, dst, rows_send.at[sender], misc_recv.at[k], to)

    def share_refs(k):
        return remote(cache.at[r, frame], cache.at[r, frame], cache_send.at[0], cache_recv.at[0], at_frame(k))

    act_copy(1).start()
    act_copy(2).start()
    edge(0).start()
    fills[0].wait()
    for i in range(CHUNKS):
        send_conv(0, frame, mine, i, i, at_frame(4))
    for f in fills[1:]:
        f.wait()

    def from_quad(k):
        slot = slot_of(k)
        await_bytes(shifted.at[1, slot, columns:columns + tokens], act_recv.at[k - 1])
        if k == 1:
            act_copy(3).start()
        edge(k).start()

    for k in range(1, frames, 2):
        time_w[rows_at(flip(frame, k) * time_span, time_span), :] = jnp.zeros((time_span, ch), bf16)

    from_quad(1)
    from_quad(2)
    conv_from_lane(0)
    conv_from_lane(1)
    from_quad(3)
    weights_across()
    weights_along(0, 3)
    weights_along(0, 1)
    weights_along(1, 3)
    conv_from_lane(2)

    blank = jnp.zeros((1, ch), f32)

    def shift(k):
        slot = slot_of(k)
        edge_wait(k)
        for i in range(rows + 2):
            span = slice(i * columns, (i + 1) * columns)
            row = shifted[1, slot, span, :].astype(f32)
            shifted[0, slot, span, :] = jnp.concatenate([blank, row[:columns - 1]], axis=0).astype(bf16)
            shifted[2, slot, span, :] = jnp.concatenate([row[1:], blank], axis=0).astype(bf16)

    for k in range(QUAD):
        shift(k)

    def windows(shard, j, slot=None):
        tap = shard + j
        dy, dx = tap // 3, tap % 3
        if slot is None:
            return shifted[dx, :, rows_at(dy * columns, tokens), :].reshape(QUAD * tokens, ch)
        return shifted[dx, pl.ds(slot, LANES), rows_at(dy * columns, tokens), :].reshape(LANES * tokens, ch)

    def partial_sum(slot, shard, j, place=None):
        return jnp.dot(windows(shard, j, place), conv_w[slot, j * ch:(j + 1) * ch, :], preferred_element_type=f32)

    part[...] = (partial_sum(0, frame, 0) + partial_sum(0, frame, 1)).reshape(QUAD, tokens, ch)

    for i in range(CHUNKS):
        conv_from_other(i)
    conv_from_mate()
    def pair_sum(pair):
        return part[pl.ds(pair, 2)] + (
            partial_sum(1, opposite_shard, 0, pair) + partial_sum(1, opposite_shard, 1, pair)
        ).reshape(2, tokens, ch)

    halves = [slice(0, tokens // 2), slice(tokens // 2, tokens)]
    partial_out[pl.ds(2 * (1 - x), 2)] = pair_sum(2 * (1 - x)).astype(bf16)
    across = [
        remote(partial_out.at[slot_of(3), half], partial_in.at[0, half], rows_send.at[0], sum_recv.at[h], at_frame(1))
        for h, half in enumerate(halves)]
    across.append(remote(partial_out.at[slot_of(1)], partial_in.at[1], rows_send.at[0], sum_recv.at[2], at_frame(1)))
    for c in across:
        c.start()
    part[pl.ds(2 * x, 2)] = pair_sum(2 * x)
    from_lane(0, 3)
    relay_lane(0)
    weights_along(1, 1)
    from_lane(0, 1)
    along = [
        remote(partial_out.at[slot_of(2), half], partial_in.at[2, half], rows_send.at[0], sum_recv.at[3 + h], at_frame(2))
        for h, half in enumerate(halves)]
    for h, half in enumerate(halves):
        await_bytes(partial_in.at[0, half], sum_recv.at[h])
        partial_out[slot_of(2), half] = (part[slot_of(2), half] + partial_in[0, half].astype(f32)).astype(bf16)
        along[h].start()
    from_lane(1, 3)
    relay_lane(1)
    for k in range(1, frames):
        share_refs(k).start()
    from_lane(0, 2)
    from_lane(1, 1)
    from_cross(0)
    from_cross(3)

    await_bytes(partial_in.at[1], sum_recv.at[2])
    total = own_x + part[own] + partial_in[1].astype(f32)
    for h, half in enumerate(halves):
        await_bytes(partial_in.at[2, half], sum_recv.at[3 + h])
    total = total + partial_in[2].astype(f32)
    hidden = total.astype(bf16).astype(f32)
    mix[1 + x] = act(hidden, 1).astype(bf16)

    gives = jnp.where(x == 0, z > 0, z < depth - 1)
    takes = jnp.where(x == 0, z < depth - 1, z > 0)
    far = mix.at[3 * (1 - x)]
    beside = [exchange(mix.at[1 + x, half], mix.at[1 + x, half], 1 + 5 * h, at_frame(1)) for h, half in enumerate(halves)]
    beyond = exchange(mix.at[1 + x], far, 2, {"frame": jnp.clip(frame + 4 * x - 2, 0, frames - 1)}, 1)
    past = {"frame": jnp.clip(frame + 2 - 4 * x, 0, frames - 1)}
    passed = [exchange(mix.at[2 - x, half], mix.at[3 * x, half], 4 + 3 * h, past, 2) for h, half in enumerate(halves)]

    @pl.when(gives)
    def _():
        beyond.start()

    for c in beside:
        c.start()

    @pl.when(z == 0)
    def _():
        mix[0] = jnp.zeros((tokens, ch), bf16)

    @pl.when(z == depth - 1)
    def _():
        mix[3] = jnp.zeros((tokens, ch), bf16)

    from_other(1, 6)
    from_other(0, 6)
    from_other(0, 2)
    from_cross(1)
    from_lane(1, 2)
    from_other(0, 4)
    from_other(1, 2)
    await_bytes(mix.at[2 - x, halves[0]], misc_recv.at[1])

    @pl.when(takes)
    def _():
        passed[0].start()

    await_bytes(mix.at[2 - x, halves[1]], misc_recv.at[6])

    @pl.when(takes)
    def _():
        passed[1].start()

    from_other(1, 7)
    from_mate(0)

    def time_rows_of(t):
        found = []
        at, left = t * ch, ch
        while left:
            shard, inside = at // time_rows, at % time_rows
            count = min(time_rows - inside, left)
            found.append(time_w[shard * time_span + inside:shard * time_span + inside + count, :])
            at, left = at + count, left - count
        return jnp.concatenate(found, axis=0)

    def temporal(lane):
        total = jnp.dot(mix[lane + 1], time_rows_of(1), preferred_element_type=f32)
        total = total + jnp.dot(mix[lane], time_rows_of(0), preferred_element_type=f32)
        return total + jnp.dot(mix[lane + 2], time_rows_of(2), preferred_element_type=f32)

    @pl.when(takes)
    def _():
        beyond.wait_recv()

    given[0] = temporal(1 - x).astype(bf16)
    temporal_swap = exchange(given.at[0], given.at[1], 5, at_frame(1))
    temporal_swap.start()
    from_cross(2)
    from_other(1, 4)
    from_other(1, 3)
    await_bytes(cache.at[r, 0:frames - 1], cache_recv.at[0])
    cache_mate = remote(cache.at[r], cache.at[r], cache_send.at[1], cache_recv.at[1], mate)
    cache_mate.start()

    @pl.when(gives)
    def _():
        for h, half in enumerate(halves):
            await_bytes(mix.at[3 * x, half], misc_recv.at[4 + 3 * h])

    own_temporal = temporal(x)
    from_other(1, 5)
    await_bytes(cache.at[1 - r], cache_recv.at[1])
    pick = pick_ref[0]
    cached = cache[...].astype(f32).reshape(2 * frames, 2, images, ch)
    picked_keys = jnp.zeros((2 * frames, ch), f32)
    picked_values = jnp.zeros((2 * frames, ch), f32)
    for i in range(images):
        picked_keys = jnp.where(pick == i, cached[:, 0, i, :], picked_keys)
        picked_values = jnp.where(pick == i, cached[:, 1, i, :], picked_values)
    picked_keys, picked_values = picked_keys.astype(bf16), picked_values.astype(bf16)
    temporal_swap.wait_recv()
    total = hidden + own_temporal + given[1].astype(f32)
    blended = total.astype(bf16).astype(f32)
    normed = normalize(blended, gains_ref[2:3, :]).astype(bf16)
    from_mate(1)
    own_keys, own_values = kv.at[0, r], kv.at[1, r]
    own_keys[...] = jnp.dot(normed, attn_w[:, ch:2 * ch], preferred_element_type=f32).astype(bf16)
    swap_keys = exchange(own_keys, own_keys, 0, mate)
    swap_keys.start()
    own_values[...] = jnp.dot(normed, attn_w[:, 2 * ch:3 * ch], preferred_element_type=f32).astype(bf16)
    swap_values = exchange(own_values, own_values, 3, mate)
    swap_values.start()
    queries = jnp.dot(normed, attn_w[:, :ch], preferred_element_type=f32).astype(bf16) * head_dim ** (-0.5)
    first_head = lax.broadcasted_iota(jnp.int32, (tokens, 2 * head_dim), 1) < head_dim
    none = jnp.zeros((tokens, 2 * head_dim), bf16)
    ones = jnp.ones((2 * (tokens + frames), 2 * head_dim), bf16)
    pairs = [slice(2 * h * head_dim, 2 * (h + 1) * head_dim) for h in range(heads // 2)]
    await_bytes(kv.at[0, 1 - r], misc_recv.at[0])
    weights = []
    for at in pairs:
        both = jnp.concatenate([
            jnp.where(first_head, queries[:, at], none), jnp.where(first_head, none, queries[:, at]),
        ], axis=0)
        keys = jnp.concatenate([kv[0, 0, :, at], kv[0, 1, :, at], picked_keys[:, at]], axis=0)
        scores = lax.dot_general(both, keys, (((1,), (1,)), ((), ())), preferred_element_type=f32)
        weights.append(jnp.exp(scores - jnp.max(scores, axis=-1, keepdims=True)).astype(bf16))
    await_bytes(kv.at[1, 1 - r], misc_recv.at[3])
    for at, probs in zip(pairs, weights):
        values = jnp.concatenate([kv[1, 0, :, at], kv[1, 1, :, at], picked_values[:, at]], axis=0)
        mixed = jnp.dot(probs, jnp.concatenate([values, ones], axis=1), preferred_element_type=f32)
        mixed = mixed[:, :2 * head_dim] / mixed[:, 2 * head_dim:]
        attended[:, at] = jnp.where(first_head, mixed[:tokens], mixed[tokens:]).astype(bf16)
    result = blended + jnp.dot(attended[...], attn_w[:, 3 * ch:], preferred_element_type=f32)
    out_ref[0] = result.astype(bf16).reshape(rows, columns, ch)

    await_bytes(conv_w.at[0:2, 0:6 * tokens], rows_send.at[0])
    await_bytes(conv_w.at[0, 0:4 * conv_quarter], conv_send.at[0])
    await_bytes(cache.at[r, 0:frames - 1], cache_send.at[0])
    cache_mate.wait_send()
    weights_sent(0)
    weights_sent(1)

    @pl.when(gives)
    def _():
        beyond.wait_send()

    @pl.when(takes)
    def _():
        await_bytes(mix.at[0], rows_send.at[2])


def by_kernel(
    frame_count, frames_in, norm_gains, conv_weight, time_weight, attention_weight,
    reference_keys, reference_values, reference_pick,
):
    _, rows, columns, ch = frames_in.shape
    tokens = rows * columns
    images = reference_keys.shape[0]
    vmem = pl.BlockSpec(memory_space=pltpu.VMEM)
    hbm = pl.BlockSpec(memory_space=pl.ANY)
    dma = pltpu.SemaphoreType.DMA
    bf16 = jnp.bfloat16
    time_span = round_up(time_weight.shape[0], 64)
    conv_span = max(17 * ch // 8, 7 * ch // 8 + round_up(conv_weight.shape[0], 64))
    return pl.pallas_call(
        functools.partial(kernel, HEADS, images),
        out_shape=pltpu.VMEM(frames_in.shape, bf16),
        in_specs=[hbm, hbm, hbm, hbm, pl.BlockSpec(memory_space=pltpu.SMEM), hbm, hbm, hbm],
        out_specs=vmem,
        scratch_shapes=[
            pltpu.VMEM((rows, columns, ch), bf16),
            pltpu.VMEM(norm_gains.shape, jnp.float32),
            pltpu.VMEM((2, conv_span, ch), bf16),
            pltpu.VMEM((frame_count * time_span, ch), bf16),
            pltpu.VMEM((frame_count * attention_weight.shape[0], 4 * ch), bf16),
            pltpu.VMEM((3, QUAD, tokens + 2 * columns, ch), bf16),
            pltpu.VMEM((QUAD, tokens, ch), jnp.float32),
            pltpu.VMEM((QUAD, tokens, ch), bf16),
            pltpu.VMEM((QUAD, tokens, ch), bf16),
            pltpu.VMEM((LANES + 2, tokens, ch), bf16),
            pltpu.VMEM((2, tokens, ch), bf16),
            pltpu.VMEM((2, 2, tokens, ch), bf16),
            pltpu.VMEM((2, frame_count, 2, images, ch), bf16),
            pltpu.VMEM((tokens, ch), bf16),
            dma((7,)),
            dma((3,)),
            dma((QUAD - 1,)),
            dma((QUAD,)),
            dma((1,)),
            dma((2 * CHUNKS + 1,)),
            dma((6,)),
            dma((QUAD,)),
            dma((9,)),
            dma((2,)),
            dma((2,)),
            dma((5,)),
            dma((8,)),
            dma((2,)),
            dma((2,)),
        ],
        compiler_params=pltpu.CompilerParams(
            collective_id=0, has_side_effects=True, vmem_limit_bytes=60 * 2**20
        ),
    )(frames_in, norm_gains, reference_keys[:, 0], reference_values[:, 0], reference_pick, conv_weight, time_weight, attention_weight)


def on_device(sizes, *operands):
    frames_in, _, conv_weight, time_weight, attention_weight, keys, _, _ = operands
    count = sizes["frame"]
    rows, columns, channels = frames_in.shape[1:]
    share = channels // 8
    fits = (
        sizes["groups"] == 2 and sizes["row"] == 2 and count == 2 * QUAD
        and frames_in.shape[0] == 1 and rows == 2 and columns % 16 == 0 and keys.shape[1] == 1
        and channels == 64 * HEADS and HEADS % 2 == 0 and channels % 128 == 0 and conv_weight.shape[0] == 9 * share
        and time_weight.shape[0] == 3 * share and attention_weight.shape[0] == share
    )
    if fits:
        return by_kernel(count, *operands)
    return by_collectives(*operands)


def solution(mesh):
    return jax.shard_map(
        functools.partial(on_device, dict(mesh.shape)),
        mesh=mesh,
        in_specs=(
            P(("groups", "frame"), "row", None, None),
            P(),
            P("frame", None),
            P("frame", None),
            P("frame", None),
            P("groups", ("frame", "row"), None),
            P("groups", ("frame", "row"), None),
            P(("groups", "frame")),
        ),
        out_specs=P(("groups", "frame"), "row", None, None),
        check_vma=False,
    )
```

```python
import functools

import jax
import jax.numpy as jnp
from jax import lax
from jax.experimental import pallas as pl
from jax.experimental.pallas import tpu as pltpu
from jax.sharding import PartitionSpec as P

HEADS = 10
LANES = 2
QUAD = 4
CHUNKS = 3
MESH = pl.DeviceIdType.MESH


def padded_2(x, sides, width):
    for axis, dim in sides:
        devices, length = (lax.axis_size(axis), x.shape[dim])
        up = [(i, (i + 1) % devices) for i in range(devices - 1)]
        down = [(j, i) for i, j in up]
        last = lax.slice_in_dim(x, length - width, length, axis=dim)
        initial = lax.slice_in_dim(x, 0, width, axis=dim)
        before = lax.ppermute(last, axis, up)
        after = lax.ppermute(initial, axis, down)
        x = jnp.concatenate([before, x, after], axis=dim)
    return x


def normalize(values, gain):
    scale = lax.rsqrt(jnp.mean(values * values, axis=-1, keepdims=True) + 1e-05)
    return values * scale * gain


def heads_first(block, head_dim):
    split = block.reshape(block.shape[0], block.shape[1], HEADS, head_dim)
    return jnp.transpose(split, (2, 0, 1, 3))


def by_collectives(
    frames_in,
    norm_gains,
    conv_weight,
    time_weight,
    attention_weight,
    reference_keys,
    reference_values,
    reference_pick,
):
    local_frames, local_rows, columns, channels = frames_in.shape
    head_dim = channels // HEADS
    tokens = local_frames * local_rows * columns
    row_count = lax.axis_size("row")
    row_place = lax.axis_index("row")

    def halve(matrix):
        share = matrix.shape[1] // row_count
        return lax.dynamic_slice_in_dim(matrix, row_place * share, share, 1)

    conv_half, time_half, attention_half = (
        lax.all_gather(halve(conv_weight), "frame", axis=0, tiled=True),
        lax.all_gather(halve(time_weight), "frame", axis=0, tiled=True),
        lax.all_gather(halve(attention_weight), "frame", axis=0, tiled=True),
    )
    conv_full, time_full, attention_full = (
        lax.all_gather(conv_half, "row", axis=1, tiled=True),
        lax.all_gather(time_half, "row", axis=1, tiled=True),
        lax.all_gather(attention_half, "row", axis=1, tiled=True),
    )
    inputs = frames_in.astype(jnp.float32)
    activated = jax.nn.silu(normalize(inputs, norm_gains[0])).astype(jnp.bfloat16)
    padded = padded_2(activated, (("row", 1),), 1)
    padded = jnp.pad(padded, ((0, 0), (0, 0), (1, 1), (0, 0)))
    spatial = jnp.zeros((tokens, channels), jnp.float32)
    for offset_row in range(3):
        for offset_col in range(3):
            window = padded[
                :, offset_row : offset_row + local_rows, offset_col : offset_col + columns, :
            ].reshape(tokens, channels)
            row_start = (3 * offset_row + offset_col) * channels
            spatial = spatial + jnp.dot(
                window,
                conv_full[row_start : row_start + channels],
                preferred_element_type=jnp.float32,
            )
    hidden = (inputs + spatial.reshape(inputs.shape)).astype(jnp.bfloat16)
    hidden_wide = hidden.astype(jnp.float32)
    mixed = jax.nn.silu(normalize(hidden_wide, norm_gains[1])).astype(jnp.bfloat16)
    nearby = padded_2(mixed, (("frame", 0),), 1)
    temporal = jnp.zeros((tokens, channels), jnp.float32)
    for offset_frame in range(3):
        window = nearby[offset_frame : offset_frame + local_frames].reshape(tokens, channels)
        temporal = temporal + jnp.dot(
            window,
            time_full[offset_frame * channels : (offset_frame + 1) * channels],
            preferred_element_type=jnp.float32,
        )
    blended = (hidden_wide + temporal.reshape(inputs.shape)).astype(jnp.bfloat16)
    blended_wide = blended.astype(jnp.float32)
    normed = normalize(blended_wide, norm_gains[2]).astype(jnp.bfloat16).reshape(tokens, channels)
    projected = jnp.dot(
        normed, attention_full[:, : 3 * channels], preferred_element_type=jnp.float32
    ).astype(jnp.bfloat16)
    projected = projected.reshape(local_frames, local_rows * columns, 3 * channels)
    queries = projected[:, :, :channels]
    own_keys = projected[:, :, channels : 2 * channels]
    own_values = projected[:, :, 2 * channels :]
    frame_keys, frame_values = (
        lax.all_gather(own_keys, "row", axis=1, tiled=True),
        lax.all_gather(own_values, "row", axis=1, tiled=True),
    )
    cache_keys, cache_values = (
        lax.all_gather(reference_keys, ("frame", "row"), axis=1, tiled=True),
        lax.all_gather(reference_values, ("frame", "row"), axis=1, tiled=True),
    )
    picked_keys = jnp.take(cache_keys, reference_pick, axis=0)
    picked_values = jnp.take(cache_values, reference_pick, axis=0)
    keys_all = jnp.concatenate([frame_keys, picked_keys], axis=1)
    values_all = jnp.concatenate([frame_values, picked_values], axis=1)

    def one_head(operands):
        query_head, key_head, value_head = operands
        scores = jnp.einsum(
            "fqd,fkd->fqk", query_head, key_head, preferred_element_type=jnp.float32
        ) * head_dim ** (-0.5)
        ceiling = jnp.max(scores, axis=-1, keepdims=True)
        weights = jnp.exp(scores - ceiling)
        probs = (weights / jnp.sum(weights, axis=-1, keepdims=True)).astype(jnp.bfloat16)
        return jnp.einsum(
            "fqk,fkd->fqd", probs, value_head, preferred_element_type=jnp.float32
        ).astype(jnp.bfloat16)

    per_head = lax.map(
        one_head,
        (
            heads_first(queries, head_dim),
            heads_first(keys_all, head_dim),
            heads_first(values_all, head_dim),
        ),
    )
    attended = jnp.transpose(per_head, (1, 2, 0, 3)).reshape(tokens, channels)
    output = jnp.dot(
        attended, attention_full[:, 3 * channels :], preferred_element_type=jnp.float32
    )
    return (blended_wide + output.reshape(inputs.shape)).astype(jnp.bfloat16)


def round_up(value, unit):
    return -(-value // unit) * unit


def flip(frame, k):
    z, x = frame // LANES, frame % LANES
    kz, kx = k // LANES, k % LANES
    high = (z // 2 + kz // 2) % 2
    low = (z % 2 + kz % 2) % 2
    return (2 * high + low) * LANES + (x + kx) % 2


def kernel(
    heads, images,
    x_ref, gains_hbm, keys_ref, values_ref, pick_ref, conv_ref, time_ref, attn_ref,
    out_ref,
    x_own, gains_ref, conv_w, time_w, attn_w, shifted, part, partial_out, partial_in, mix, given, kv, cache, attended,
    local_sem, rows_send, act_recv, edge_recv, conv_send, conv_recv,
    lane_recv, cross_recv, other_recv, mate_recv, weight_send,
    sum_recv, misc_recv, cache_send, cache_recv,
):
    y, frame, r = lax.axis_index("groups"), lax.axis_index("frame"), lax.axis_index("row")
    frames = 2 * QUAD
    _, rows, columns, ch = x_ref.shape
    tokens = rows * columns
    head_dim = ch // heads
    share = ch // 8
    conv_rows, time_rows, attn_rows = conv_ref.shape[0], time_ref.shape[0], attn_ref.shape[0]
    conv_quarter = round_up(conv_rows, 64) // 4
    conv_first = conv_quarter // 2 // 16 * 16
    conv_last = max(conv_quarter // 6 // 16 * 16, 16)
    conv_chunks = (
        (0, conv_first), (conv_first, conv_quarter - conv_first - conv_last),
        (conv_quarter - conv_last, conv_last),
    )
    time_quarter = round_up(time_rows, 64) // 4
    time_span = 4 * time_quarter
    f32, bf16 = jnp.float32, jnp.bfloat16
    z, x = frame // LANES, frame % LANES
    depth = frames // LANES

    def slot_of(k):
        return (x + k % LANES) % LANES * 2 + (z + k // LANES) % 2

    own = slot_of(0)
    mine, theirs = 2 * y + r, 2 * (1 - y) + r
    mate = {"row": 1 - r}
    opposite = {"groups": 1 - y}

    def rows_at(start, size):
        return pl.ds(pl.multiple_of(start, 16), size)

    def at_frame(k):
        return {"frame": flip(frame, k)}

    def remote(src, dst, send_sem, recv_sem, to):
        return pltpu.make_async_remote_copy(
            src_ref=src, dst_ref=dst, send_sem=send_sem, recv_sem=recv_sem,
            device_id=to, device_id_type=MESH,
        )

    def await_bytes(ref, sem):
        pltpu.make_async_copy(ref, ref, sem).wait()

    def clear(slot, shard, covered, blocks):
        for i in range(blocks):
            start = i * share + jnp.where(i < shard, 0, covered)
            conv_w[slot, rows_at(start, share), :] = jnp.zeros((share, ch), bf16)

    early = [
        pltpu.make_async_copy(x_ref.at[0], x_own, local_sem.at[0]),
        pltpu.make_async_copy(gains_hbm, gains_ref, local_sem.at[6]),
    ]
    for f in early:
        f.start()
    partners = [at_frame(k) for k in range(1, frames)] + [mate, opposite]
    barrier = pltpu.get_barrier_semaphore()
    for to in partners:
        pl.semaphore_signal(barrier, inc=1, device_id=to, device_id_type=MESH)

    opposite_shard = flip(frame, 4)
    clear(0, frame, conv_rows, 8)
    fills = [
        pltpu.make_async_copy(conv_ref, conv_w.at[0, rows_at(frame * share, conv_rows)], local_sem.at[1]),
        pltpu.make_async_copy(time_ref, time_w.at[rows_at(frame * time_span, time_rows)], local_sem.at[2]),
        pltpu.make_async_copy(attn_ref, attn_w.at[rows_at(frame * attn_rows, attn_rows)], local_sem.at[3]),
        pltpu.make_async_copy(keys_ref, cache.at[r, frame, 0], local_sem.at[4]),
        pltpu.make_async_copy(values_ref, cache.at[r, frame, 1], local_sem.at[5]),
    ]
    for f in fills:
        f.start()
    clear(1, opposite_shard, 4 * conv_quarter, 7)
    if time_span > time_rows:
        gap = time_span - time_rows
        time_w[rows_at(frame * time_span + time_rows, gap), :] = jnp.zeros((gap, ch), bf16)
    shifted[1, :, rows_at(r * (rows + 1) * columns, columns), :] = jnp.zeros((QUAD, columns, ch), bf16)

    def act(v, g):
        n = normalize(v, gains_ref[g:g + 1, :])
        return n / (1.0 + jnp.exp(-n))

    for f in early:
        f.wait()
    own_x = x_own[...].reshape(tokens, ch).astype(f32)
    shifted[1, own, columns:columns + tokens, :] = act(own_x, 0).astype(bf16)
    pl.semaphore_wait(barrier, len(partners))

    def act_copy(k):
        ref = shifted.at[1, own if k < 3 else slot_of(1), columns:columns + tokens]
        return remote(ref, ref, rows_send.at[0], act_recv.at[k - 1], at_frame(min(k, 2)))

    def edge(k):
        slot = slot_of(k)
        return remote(
            shifted.at[1, slot, rows_at(rows * columns - r * (rows - 1) * columns, columns)],
            shifted.at[1, slot, rows_at(r * (rows + 1) * columns, columns)],
            rows_send.at[0], edge_recv.at[k], mate,
        )

    def edge_wait(k):
        slot = slot_of(k)
        await_bytes(shifted.at[1, slot, rows_at((1 - r) * (rows + 1) * columns, columns)], edge_recv.at[k])

    def conv_part(slot, shard, q, i):
        first, count = conv_chunks[i]
        return conv_w.at[slot, rows_at(shard * share + q * conv_quarter + first, count)]

    def send_conv(slot, shard, q, i, recv, to):
        remote(
            conv_part(slot, shard, q, i), conv_part(1, shard, q, i),
            conv_send.at[0], conv_recv.at[recv], to,
        ).start()

    def conv_from_lane(i):
        await_bytes(conv_part(1, opposite_shard, mine, i), conv_recv.at[i])
        send_conv(1, opposite_shard, mine, i, CHUNKS + i, opposite)
        send_conv(1, opposite_shard, mine, i, 2 * CHUNKS, mate)

    def conv_from_other(i):
        await_bytes(conv_part(1, opposite_shard, theirs, i), conv_recv.at[CHUNKS + i])
        send_conv(1, opposite_shard, theirs, i, 2 * CHUNKS, mate)

    def conv_from_mate():
        await_bytes(conv_w.at[1, 0:2 * conv_quarter], conv_recv.at[2 * CHUNKS])

    def time_part(d, q, count=1):
        return time_w.at[rows_at(d * time_span + q * time_quarter, count * time_quarter)]

    def attn_part(d, q, count=1):
        return attn_w.at[rows_at(d * attn_rows, attn_rows), pl.ds(pl.multiple_of(q * ch, 128), count * ch)]

    def pieces(w):
        return time_part if w == 0 else attn_part

    def send_weight(w, ref, recv_sem, to):
        remote(ref, ref, weight_send.at[w], recv_sem, to).start()

    def weights_across():
        send_weight(1, attn_part(frame, 2 * r, 2), cross_recv.at[0], at_frame(1))

    def weights_along(w, k):
        send_weight(w, pieces(w)(frame, mine), lane_recv.at[3 * w + k - 1], at_frame(2 * k))

    def other_place(w, k):
        return k // 2 - 1 if w == 0 else k + 1

    def from_lane(w, k):
        ref = pieces(w)(flip(frame, 2 * k), mine)
        await_bytes(ref, lane_recv.at[3 * w + k - 1])
        if w == 1:
            send_weight(w, ref, cross_recv.at[k], at_frame(1))
        if w == 0 or k != 2:
            send_weight(w, ref, other_recv.at[other_place(w, 2 * k)], opposite)
        send_weight(w, ref, mate_recv.at[w], mate)

    def relay_lane(w):
        send_weight(w, pieces(w)(flip(frame, 6), mine), lane_recv.at[3 * w + 1], at_frame(2))

    def from_cross(k):
        ref = attn_part(flip(frame, 1), 2 * r, 2) if k == 0 else attn_part(flip(frame, 2 * k + 1), mine)
        await_bytes(ref, cross_recv.at[k])
        if k % 2 == 1:
            send_weight(1, ref, other_recv.at[other_place(1, 2 * k + 1)], opposite)
        send_weight(1, ref, mate_recv.at[1], mate)

    def from_other(w, k):
        ref = pieces(w)(flip(frame, k), theirs)
        await_bytes(ref, other_recv.at[other_place(w, k)])
        if w == 1 and k >= 6:
            send_weight(w, ref, other_recv.at[other_place(w, k - 2)], at_frame(2))
        send_weight(w, ref, mate_recv.at[w], mate)

    def weight_bytes(w, quarters):
        if w == 0:
            return time_w.at[0:quarters * time_quarter]
        return attn_w.at[0:quarters * attn_rows // 2, 0:2 * ch]

    def from_mate(w):
        await_bytes(weight_bytes(w, (6, 14)[w]), mate_recv.at[w])

    def weights_sent(w):
        if w == 0:
            await_bytes(time_w.at[0:12 * time_quarter], weight_send.at[w])
        else:
            await_bytes(attn_w.at[0:7 * attn_rows], weight_send.at[w])

    def exchange(src, dst, k, to, sender=0):
        return remote(src, dst, rows_send.at[sender], misc_recv.at[k], to)

    def share_refs(k):
        return remote(cache.at[r, frame], cache.at[r, frame], cache_send.at[0], cache_recv.at[0], at_frame(k))

    act_copy(1).start()
    act_copy(2).start()
    edge(0).start()
    fills[0].wait()
    for i in range(CHUNKS):
        send_conv(0, frame, mine, i, i, at_frame(4))
    for f in fills[1:]:
        f.wait()

    def from_quad(k):
        slot = slot_of(k)
        await_bytes(shifted.at[1, slot, columns:columns + tokens], act_recv.at[k - 1])
        if k == 1:
            act_copy(3).start()
        edge(k).start()

    for k in range(1, frames, 2):
        time_w[rows_at(flip(frame, k) * time_span, time_span), :] = jnp.zeros((time_span, ch), bf16)

    from_quad(1)
    from_quad(2)
    conv_from_lane(0)
    conv_from_lane(1)
    from_quad(3)
    weights_across()
    weights_along(0, 3)
    weights_along(0, 1)
    weights_along(1, 3)
    conv_from_lane(2)

    blank = jnp.zeros((1, ch), f32)

    def shift(k):
        slot = slot_of(k)
        edge_wait(k)
        for i in range(rows + 2):
            span = slice(i * columns, (i + 1) * columns)
            row = shifted[1, slot, span, :].astype(f32)
            shifted[0, slot, span, :] = jnp.concatenate([blank, row[:columns - 1]], axis=0).astype(bf16)
            shifted[2, slot, span, :] = jnp.concatenate([row[1:], blank], axis=0).astype(bf16)

    for k in range(QUAD):
        shift(k)

    def windows(shard, j, slot=None):
        tap = shard + j
        dy, dx = tap // 3, tap % 3
        if slot is None:
            return shifted[dx, :, rows_at(dy * columns, tokens), :].reshape(QUAD * tokens, ch)
        return shifted[dx, pl.ds(slot, LANES), rows_at(dy * columns, tokens), :].reshape(LANES * tokens, ch)

    def partial_sum(slot, shard, j, place=None):
        return jnp.dot(windows(shard, j, place), conv_w[slot, j * ch:(j + 1) * ch, :], preferred_element_type=f32)

    part[...] = (partial_sum(0, frame, 0) + partial_sum(0, frame, 1)).reshape(QUAD, tokens, ch)

    for i in range(CHUNKS):
        conv_from_other(i)
    conv_from_mate()
    def pair_sum(pair):
        return part[pl.ds(pair, 2)] + (
            partial_sum(1, opposite_shard, 0, pair) + partial_sum(1, opposite_shard, 1, pair)
        ).reshape(2, tokens, ch)

    halves = [slice(0, tokens // 2), slice(tokens // 2, tokens)]
    partial_out[pl.ds(2 * (1 - x), 2)] = pair_sum(2 * (1 - x)).astype(bf16)
    across = [
        remote(partial_out.at[slot_of(3), half], partial_in.at[0, half], rows_send.at[0], sum_recv.at[h], at_frame(1))
        for h, half in enumerate(halves)]
    across.append(remote(partial_out.at[slot_of(1)], partial_in.at[1], rows_send.at[0], sum_recv.at[2], at_frame(1)))
    for c in across:
        c.start()
    part[pl.ds(2 * x, 2)] = pair_sum(2 * x)
    from_lane(0, 3)
    relay_lane(0)
    weights_along(1, 1)
    from_lane(0, 1)
    along = [
        remote(partial_out.at[slot_of(2), half], partial_in.at[2, half], rows_send.at[0], sum_recv.at[3 + h], at_frame(2))
        for h, half in enumerate(halves)]
    for h, half in enumerate(halves):
        await_bytes(partial_in.at[0, half], sum_recv.at[h])
        partial_out[slot_of(2), half] = (part[slot_of(2), half] + partial_in[0, half].astype(f32)).astype(bf16)
        along[h].start()
    from_lane(1, 3)
    relay_lane(1)
    from_lane(0, 2)
    from_lane(1, 1)
    from_cross(0)
    from_cross(3)

    await_bytes(partial_in.at[1], sum_recv.at[2])
    total = own_x + part[own] + partial_in[1].astype(f32)
    for h, half in enumerate(halves):
        await_bytes(partial_in.at[2, half], sum_recv.at[3 + h])
    total = total + partial_in[2].astype(f32)
    hidden = total.astype(bf16).astype(f32)
    mix[1 + x] = act(hidden, 1).astype(bf16)

    gives = jnp.where(x == 0, z > 0, z < depth - 1)
    takes = jnp.where(x == 0, z < depth - 1, z > 0)
    far = mix.at[3 * (1 - x)]
    beside = [exchange(mix.at[1 + x, half], mix.at[1 + x, half], 1 + 5 * h, at_frame(1)) for h, half in enumerate(halves)]
    beyond = exchange(mix.at[1 + x], far, 2, {"frame": jnp.clip(frame + 4 * x - 2, 0, frames - 1)}, 1)
    past = {"frame": jnp.clip(frame + 2 - 4 * x, 0, frames - 1)}
    passed = [exchange(mix.at[2 - x, half], mix.at[3 * x, half], 4 + 3 * h, past, 2) for h, half in enumerate(halves)]

    @pl.when(gives)
    def _():
        beyond.start()

    for c in beside:
        c.start()
    for k in range(1, frames):
        share_refs(k).start()

    @pl.when(z == 0)
    def _():
        mix[0] = jnp.zeros((tokens, ch), bf16)

    @pl.when(z == depth - 1)
    def _():
        mix[3] = jnp.zeros((tokens, ch), bf16)

    from_other(1, 6)
    from_other(0, 6)
    from_other(0, 2)
    from_cross(1)
    from_lane(1, 2)
    from_other(0, 4)
    from_other(1, 2)
    await_bytes(mix.at[2 - x, halves[0]], misc_recv.at[1])

    @pl.when(takes)
    def _():
        passed[0].start()

    await_bytes(mix.at[2 - x, halves[1]], misc_recv.at[6])

    @pl.when(takes)
    def _():
        passed[1].start()

    from_other(1, 7)
    from_mate(0)

    def time_rows_of(t):
        found = []
        at, left = t * ch, ch
        while left:
            shard, inside = at // time_rows, at % time_rows
            count = min(time_rows - inside, left)
            found.append(time_w[shard * time_span + inside:shard * time_span + inside + count, :])
            at, left = at + count, left - count
        return jnp.concatenate(found, axis=0)

    def temporal(lane):
        total = jnp.dot(mix[lane + 1], time_rows_of(1), preferred_element_type=f32)
        total = total + jnp.dot(mix[lane], time_rows_of(0), preferred_element_type=f32)
        return total + jnp.dot(mix[lane + 2], time_rows_of(2), preferred_element_type=f32)

    @pl.when(takes)
    def _():
        beyond.wait_recv()

    given[0] = temporal(1 - x).astype(bf16)
    temporal_swap = exchange(given.at[0], given.at[1], 5, at_frame(1))
    temporal_swap.start()
    from_cross(2)
    from_other(1, 4)
    from_other(1, 3)
    await_bytes(cache.at[r, 0:frames - 1], cache_recv.at[0])
    cache_mate = remote(cache.at[r], cache.at[r], cache_send.at[1], cache_recv.at[1], mate)
    cache_mate.start()

    @pl.when(gives)
    def _():
        for h, half in enumerate(halves):
            await_bytes(mix.at[3 * x, half], misc_recv.at[4 + 3 * h])

    own_temporal = temporal(x)
    from_other(1, 5)
    await_bytes(cache.at[1 - r], cache_recv.at[1])
    pick = pick_ref[0]
    cached = cache[...].astype(f32).reshape(2 * frames, 2, images, ch)
    picked_keys = jnp.zeros((2 * frames, ch), f32)
    picked_values = jnp.zeros((2 * frames, ch), f32)
    for i in range(images):
        picked_keys = jnp.where(pick == i, cached[:, 0, i, :], picked_keys)
        picked_values = jnp.where(pick == i, cached[:, 1, i, :], picked_values)
    picked_keys, picked_values = picked_keys.astype(bf16), picked_values.astype(bf16)
    temporal_swap.wait_recv()
    total = hidden + own_temporal + given[1].astype(f32)
    blended = total.astype(bf16).astype(f32)
    normed = normalize(blended, gains_ref[2:3, :]).astype(bf16)
    from_mate(1)
    own_keys, own_values = kv.at[0, r], kv.at[1, r]
    own_keys[...] = jnp.dot(normed, attn_w[:, ch:2 * ch], preferred_element_type=f32).astype(bf16)
    swap_keys = exchange(own_keys, own_keys, 0, mate)
    swap_keys.start()
    own_values[...] = jnp.dot(normed, attn_w[:, 2 * ch:3 * ch], preferred_element_type=f32).astype(bf16)
    swap_values = exchange(own_values, own_values, 3, mate)
    swap_values.start()
    queries = jnp.dot(normed, attn_w[:, :ch], preferred_element_type=f32).astype(bf16) * head_dim ** (-0.5)
    first_head = lax.broadcasted_iota(jnp.int32, (tokens, 2 * head_dim), 1) < head_dim
    none = jnp.zeros((tokens, 2 * head_dim), bf16)
    ones = jnp.ones((2 * (tokens + frames), 2 * head_dim), bf16)
    pairs = [slice(2 * h * head_dim, 2 * (h + 1) * head_dim) for h in range(heads // 2)]
    await_bytes(kv.at[0, 1 - r], misc_recv.at[0])
    weights = []
    for at in pairs:
        both = jnp.concatenate([
            jnp.where(first_head, queries[:, at], none), jnp.where(first_head, none, queries[:, at]),
        ], axis=0)
        keys = jnp.concatenate([kv[0, 0, :, at], kv[0, 1, :, at], picked_keys[:, at]], axis=0)
        scores = lax.dot_general(both, keys, (((1,), (1,)), ((), ())), preferred_element_type=f32)
        weights.append(jnp.exp(scores - jnp.max(scores, axis=-1, keepdims=True)).astype(bf16))
    await_bytes(kv.at[1, 1 - r], misc_recv.at[3])
    for at, probs in zip(pairs, weights):
        values = jnp.concatenate([kv[1, 0, :, at], kv[1, 1, :, at], picked_values[:, at]], axis=0)
        mixed = jnp.dot(probs, jnp.concatenate([values, ones], axis=1), preferred_element_type=f32)
        mixed = mixed[:, :2 * head_dim] / mixed[:, 2 * head_dim:]
        attended[:, at] = jnp.where(first_head, mixed[:tokens], mixed[tokens:]).astype(bf16)
    result = blended + jnp.dot(attended[...], attn_w[:, 3 * ch:], preferred_element_type=f32)
    out_ref[0] = result.astype(bf16).reshape(rows, columns, ch)

    await_bytes(conv_w.at[0:2, 0:6 * tokens], rows_send.at[0])
    await_bytes(conv_w.at[0, 0:4 * conv_quarter], conv_send.at[0])
    await_bytes(cache.at[r, 0:frames - 1], cache_send.at[0])
    cache_mate.wait_send()
    weights_sent(0)
    weights_sent(1)

    @pl.when(gives)
    def _():
        beyond.wait_send()

    @pl.when(takes)
    def _():
        await_bytes(mix.at[0], rows_send.at[2])


def by_kernel(
    frame_count, frames_in, norm_gains, conv_weight, time_weight, attention_weight,
    reference_keys, reference_values, reference_pick,
):
    _, rows, columns, ch = frames_in.shape
    tokens = rows * columns
    images = reference_keys.shape[0]
    vmem = pl.BlockSpec(memory_space=pltpu.VMEM)
    hbm = pl.BlockSpec(memory_space=pl.ANY)
    dma = pltpu.SemaphoreType.DMA
    bf16 = jnp.bfloat16
    time_span = round_up(time_weight.shape[0], 64)
    conv_span = max(17 * ch // 8, 7 * ch // 8 + round_up(conv_weight.shape[0], 64))
    return pl.pallas_call(
        functools.partial(kernel, HEADS, images),
        out_shape=pltpu.VMEM(frames_in.shape, bf16),
        in_specs=[hbm, hbm, hbm, hbm, pl.BlockSpec(memory_space=pltpu.SMEM), hbm, hbm, hbm],
        out_specs=vmem,
        scratch_shapes=[
            pltpu.VMEM((rows, columns, ch), bf16),
            pltpu.VMEM(norm_gains.shape, jnp.float32),
            pltpu.VMEM((2, conv_span, ch), bf16),
            pltpu.VMEM((frame_count * time_span, ch), bf16),
            pltpu.VMEM((frame_count * attention_weight.shape[0], 4 * ch), bf16),
            pltpu.VMEM((3, QUAD, tokens + 2 * columns, ch), bf16),
            pltpu.VMEM((QUAD, tokens, ch), jnp.float32),
            pltpu.VMEM((QUAD, tokens, ch), bf16),
            pltpu.VMEM((QUAD, tokens, ch), bf16),
            pltpu.VMEM((LANES + 2, tokens, ch), bf16),
            pltpu.VMEM((2, tokens, ch), bf16),
            pltpu.VMEM((2, 2, tokens, ch), bf16),
            pltpu.VMEM((2, frame_count, 2, images, ch), bf16),
            pltpu.VMEM((tokens, ch), bf16),
            dma((7,)),
            dma((3,)),
            dma((QUAD - 1,)),
            dma((QUAD,)),
            dma((1,)),
            dma((2 * CHUNKS + 1,)),
            dma((6,)),
            dma((QUAD,)),
            dma((9,)),
            dma((2,)),
            dma((2,)),
            dma((5,)),
            dma((8,)),
            dma((2,)),
            dma((2,)),
        ],
        compiler_params=pltpu.CompilerParams(
            collective_id=0, has_side_effects=True, vmem_limit_bytes=60 * 2**20
        ),
    )(frames_in, norm_gains, reference_keys[:, 0], reference_values[:, 0], reference_pick, conv_weight, time_weight, attention_weight)


def on_device(sizes, *operands):
    frames_in, _, conv_weight, time_weight, attention_weight, keys, _, _ = operands
    count = sizes["frame"]
    rows, columns, channels = frames_in.shape[1:]
    share = channels // 8
    fits = (
        sizes["groups"] == 2 and sizes["row"] == 2 and count == 2 * QUAD
        and frames_in.shape[0] == 1 and rows == 2 and columns % 16 == 0 and keys.shape[1] == 1
        and channels == 64 * HEADS and HEADS % 2 == 0 and channels % 128 == 0 and conv_weight.shape[0] == 9 * share
        and time_weight.shape[0] == 3 * share and attention_weight.shape[0] == share
    )
    if fits:
        return by_kernel(count, *operands)
    return by_collectives(*operands)


def solution(mesh):
    return jax.shard_map(
        functools.partial(on_device, dict(mesh.shape)),
        mesh=mesh,
        in_specs=(
            P(("groups", "frame"), "row", None, None),
            P(),
            P("frame", None),
            P("frame", None),
            P("frame", None),
            P("groups", ("frame", "row"), None),
            P("groups", ("frame", "row"), None),
            P(("groups", "frame")),
        ),
        out_specs=P(("groups", "frame"), "row", None, None),
        check_vma=False,
    )
```
